512 devices in a mesh: gx: 32 (over z_lo, y, core), gy: 16 (over z_hi, x).
Axes of the slice: x: 4, y: 8, z: 8 (z_hi: 4, z_lo: 2; z = z_hi * 2 + z_lo), core: 2. Of those that a mesh axis runs over, the one named last changes fastest.
Arguments:
- traces: bfloat16 [3, 48, 128, 64, 128], P(None, None, 'gx', 'gy'), may hold values from -6 to 6
- dirichlet: int32 [3, 128, 64, 128], P(None, 'gx', 'gy'), may hold values 0 or 1
- visc_class: int32 [128, 64, 128], P('gx', 'gy'), may hold values from 0 to 3
- viscosity: float32 [4], replicated, may hold values from 0.25 to 4
- coarse_diag: float32 [128, 64, 128], P('gx', 'gy'), may hold values from 2 to 16
- solve_map: bfloat16 [256, 288], replicated, may hold values from -0.375 to 0.375
- flux_map: bfloat16 [288, 256], replicated, may hold values from -0.375 to 0.375
Outputs:
- corrected: bfloat16 [3, 48, 128, 64, 128], P(None, None, 'gx', 'gy')
The draws below stay inside these ranges and needn't reach their ends.
All inputs are finite; a program needn't handle non-finite values. No bound on the sum of `dirichlet` on one device may be relied on, other than what follows from the above.
Results may differ from the reference program's by a relative error of at most 0.005.
Values may be sent and summed in bfloat16 or wider, within the bound.
A program may use at most 64 MiB of HBM per device.

```python
import math
import jax
import jax.numpy as jnp
from jax import lax

FU = 48
NI = 256
NCLS = 4
NX = 128
NY = 64
NZ = 128


def with_ends(entries, key, low, high):
    longest = entries.shape.index(max(entries.shape))
    spots = []
    for shift in (0, 1):
        where = [jax.random.randint(jax.random.fold_in(key, axis), (), 0, length) for axis, length in enumerate(entries.shape)]
        where[longest] = (where[longest] + shift) % entries.shape[longest]
        spots.append(tuple(where))
    return entries.at[spots[0]].set(low).at[spots[1]].set(high)


def block_scale(key, shape, shards, smallest, high):
    def one(position, blocks):
        heights = jax.random.uniform(jax.random.fold_in(jax.random.fold_in(key, 6), position), (blocks,), jnp.float32, smallest / len(shards), high / len(shards))
        return jnp.repeat(jnp.exp(heights), shape[position] // blocks).reshape((-1,) + (1,) * (len(shape) - position - 1))

    level = one(*shards[0])
    for cut in shards[1:]:
        level = level * one(*cut)
    return level


def centred(rng, dims, width, reach, pieces=(), kind=jnp.bfloat16):
    level = block_scale(rng, dims, pieces, -0.22, 0.18) if pieces else 1.0
    values = jax.random.normal(rng, dims, jnp.float32) * width * level
    return jnp.minimum(jnp.maximum(values, -reach), reach).astype(kind)


def setup_inputs(seed: int = 0) -> dict:
    arg_keys = jax.random.split(jax.random.key(seed), 8)
    return {
        "traces": centred(arg_keys[0], (3, FU, NX, NY, NZ), 1.0, 6.0, ((2, 32), (3, 16))),
        "dirichlet": with_ends((jax.random.randint(arg_keys[1], (3, NX, NY, NZ), 0, 8) < 1).astype(jnp.int32), jax.random.fold_in(arg_keys[1], 1), 0, 1),
        "visc_class": with_ends(jax.random.randint(arg_keys[2], (NX, NY, NZ), 0, NCLS), jax.random.fold_in(arg_keys[2], 1), 0, NCLS - 1).astype(jnp.int32),
        "viscosity": jnp.clip(jnp.exp(jax.random.uniform(arg_keys[3], (NCLS,), jnp.float32, math.log(0.25), math.log(4.0))), 0.25, 4.0),
        "coarse_diag": jnp.clip(jnp.exp(math.log(16.0) - 2.0794415 * jax.random.uniform(arg_keys[4], (NX, NY, NZ), jnp.float32) ** block_scale(arg_keys[4], (NX, NY, NZ), ((0, 32), (1, 16)), -0.2, 0.2)), 2.0, 16.0),
        "solve_map": centred(arg_keys[5], (NI, 6 * FU), (6 * FU) ** -0.5, 0.375),
        "flux_map": centred(arg_keys[6], (6 * FU, NI), NI ** -0.5, 0.375),
    }


penalty = 0.5

def corner_table():
    gll_points = [-1.0, -math.sqrt(0.2), math.sqrt(0.2), 1.0]
    table_rows = []
    for node_s in range(4):
        for node_t in range(4):
            table_row = []
            for high_s in range(2):
                for high_t in range(2):
                    table_row.append((1.0 + (2 * high_s - 1) * gll_points[node_s]) * (1.0 + (2 * high_t - 1) * gll_points[node_t]) / 4.0)
            table_rows.append(table_row)
    return jnp.asarray(table_rows, dtype=jnp.float32)

def landing(face_slot, high_s, high_t):
    direction = face_slot // 2
    outward = face_slot % 2
    if direction == 0:
        return (outward, high_s, high_t)
    if direction == 1:
        return (high_s, outward, high_t)
    return (high_s, high_t, outward)

def cell_viscosity(visc_class, viscosity):
    result = jnp.zeros(visc_class.shape, jnp.float32)
    for level in range(viscosity.shape[0]):
        result = result + jnp.where(visc_class == level, viscosity[level], jnp.float32(0.0))
    return result

def forward_last(piece, axis):
    zero_part = jnp.zeros_like(lax.slice_in_dim(piece, 0, 1, axis=axis))
    return jnp.concatenate([zero_part, lax.slice_in_dim(piece, 0, piece.shape[axis] - 1, axis=axis)], axis=axis)

def backward_last(piece, axis):
    zero_part = jnp.zeros_like(lax.slice_in_dim(piece, 0, 1, axis=axis))
    return jnp.concatenate([lax.slice_in_dim(piece, 1, piece.shape[axis], axis=axis), zero_part], axis=axis)

def reference(traces, dirichlet, visc_class, viscosity, coarse_diag, solve_map, flux_map):
    weights = corner_table()
    faces = traces.shape[1]
    keep_mask = (1 - dirichlet).astype(jnp.bfloat16)
    lifted = traces * keep_mask[:, None]
    visc_all = cell_viscosity(visc_class, viscosity)

    def plane_contrib(index):
        has_next = index + 1 < NX
        next_index = jnp.minimum(index + 1, NX - 1).astype(jnp.int32)
        here = lax.dynamic_index_in_dim(lifted, index, 2, keepdims=False)
        keep_here = lax.dynamic_index_in_dim(keep_mask, index, 1, keepdims=False)
        x_next = jnp.where(has_next, lax.dynamic_index_in_dim(lifted, next_index, 2, keepdims=False)[0], jnp.zeros((), jnp.bfloat16))
        keep_xnext = jnp.where(has_next, lax.dynamic_index_in_dim(keep_mask, next_index, 1, keepdims=False)[0], jnp.zeros((), jnp.bfloat16))
        y_high = backward_last(here[1], 1)
        z_high = backward_last(here[2], 2)
        keep_yhigh = backward_last(keep_here[1], 0)
        keep_zhigh = backward_last(keep_here[2], 1)
        element_traces = jnp.concatenate([here[0], x_next, here[1], y_high, here[2], z_high], axis=0)
        flat_traces = element_traces.reshape(6 * faces, NY * NZ)
        interior = jnp.dot(solve_map, flat_traces, preferred_element_type=jnp.float32).astype(jnp.bfloat16)
        flux_term = jnp.dot(flux_map, interior, preferred_element_type=jnp.float32) + penalty * flat_traces.astype(jnp.float32)
        face_keep = jnp.stack([keep_here[0], keep_xnext, keep_here[1], keep_yhigh, keep_here[2], keep_zhigh]).astype(jnp.float32)
        visc_here = lax.dynamic_index_in_dim(visc_all, index, 0, keepdims=False)
        scaled = (visc_here[None] * face_keep).reshape(6, 1, NY * NZ)
        return (flux_term.reshape(6, faces, NY * NZ) * scaled).reshape(6, faces, NY, NZ)

    def plane_terms(index):
        contrib = plane_contrib(index)
        res_y = contrib[2] + forward_last(contrib[3], 1)
        res_z = contrib[4] + forward_last(contrib[5], 2)
        split_parts = contrib.reshape(6, 3, faces // 3, NY, NZ)
        corners = jnp.einsum('fmnyz,nc->fcmyz', split_parts, weights, precision=lax.Precision.HIGHEST)
        here_sum = jnp.zeros((3, NY, NZ), jnp.float32)
        next_sum = jnp.zeros((3, NY, NZ), jnp.float32)
        for face_slot in range(6):
            for high_s in range(2):
                for high_t in range(2):
                    step_x, step_y, step_z = landing(face_slot, high_s, high_t)
                    corner_part = corners[face_slot, 2 * high_s + high_t]
                    if step_y:
                        corner_part = forward_last(corner_part, 1)
                    if step_z:
                        corner_part = forward_last(corner_part, 2)
                    if step_x:
                        next_sum = next_sum + corner_part
                    else:
                        here_sum = here_sum + corner_part
        return (jnp.stack([contrib[0], res_y, res_z]), contrib[1], here_sum, next_sum)
    own_planes, high_planes, here_sums, next_sums = lax.map(plane_terms, jnp.arange(NX, dtype=jnp.int32))
    residual_x = own_planes[:, 0] + forward_last(high_planes, 0)
    residual_planes = jnp.concatenate([residual_x[:, None], own_planes[:, 1:]], axis=1)
    vertex_planes = forward_last(next_sums, 0) + here_sums
    coarse_fix = jnp.moveaxis(vertex_planes, 0, 1) / coarse_diag[None]

    def plane_output(index):
        has_next = index + 1 < NX
        next_index = jnp.minimum(index + 1, NX - 1).astype(jnp.int32)
        fix_here = lax.dynamic_index_in_dim(coarse_fix, index, 1, keepdims=False)
        fix_next = jnp.where(has_next, lax.dynamic_index_in_dim(coarse_fix, next_index, 1, keepdims=False), jnp.float32(0.0))
        paired = jnp.pad(jnp.stack([fix_here, fix_next]), ((0, 0), (0, 0), (0, 1), (0, 1)))
        residual_here = lax.dynamic_index_in_dim(residual_planes, index, 0, keepdims=False)
        keep_here = lax.dynamic_index_in_dim(keep_mask, index, 1, keepdims=False)
        results = []
        for direction in range(3):
            picks = []
            for high_s in range(2):
                for high_t in range(2):
                    step_x, step_y, step_z = landing(2 * direction, high_s, high_t)
                    picks.append(paired[step_x][:, step_y:step_y + NY, step_z:step_z + NZ])
            lifted_fix = jnp.einsum('nc,cmyz->mnyz', weights, jnp.stack(picks), precision=lax.Precision.HIGHEST).reshape(faces, NY, NZ)
            results.append(residual_here[direction] + keep_here[direction].astype(jnp.float32) * lifted_fix)
        return jnp.stack(results).astype(jnp.bfloat16)
    planes_out = lax.map(plane_output, jnp.arange(NX, dtype=jnp.int32))
    return jnp.transpose(planes_out, (1, 2, 0, 3, 4))
```

```python
import functools
import itertools
import math

import jax
import jax.numpy as jnp
import ml_dtypes
import numpy as np
from jax import lax
from jax.experimental import pallas as pl
from jax.experimental.pallas import tpu as pltpu
from jax.sharding import PartitionSpec as P

MESH = pl.DeviceIdType.MESH
penalty = 0.5
CORNER = 4


def corner_table():
    points = [-1.0, -math.sqrt(0.2), math.sqrt(0.2), 1.0]
    table = np.zeros((16, 4), np.float64)
    for a, b, p, q in itertools.product(range(4), range(4), range(2), range(2)):
        table[4 * a + b, 2 * p + q] = (1 + (2 * p - 1) * points[a]) * (1 + (2 * q - 1) * points[b]) / 4
    return table.astype(np.float32)


def in_two(table):
    high = table.astype(ml_dtypes.bfloat16)
    low = (table - high.astype(np.float32)).astype(ml_dtypes.bfloat16)
    return high, low


def gather_table():
    weights = corner_table()
    table = np.zeros((32, 6, 3, 16), np.float32)
    for dx, dy, dz, m in itertools.product(range(2), range(2), range(2), range(3)):
        row = 16 * dx + 8 * dy + CORNER * dz + m
        table[row, dx, m] = weights[:, 2 * dy + dz]
        table[row, 2 + dy, m] = weights[:, 2 * dx + dz]
        table[row, 4 + dz, m] = weights[:, 2 * dx + dy]
    return np.concatenate(in_two(table.reshape(32, 288)), axis=0)


def spread_table():
    weights = corner_table()
    table = np.zeros((3, 3, 16, 32), np.float32)
    for dx, dy, dz, m in itertools.product(range(2), range(2), range(2), range(3)):
        column = 16 * dx + 8 * dy + CORNER * dz + m
        if dx == 0:
            table[0, m, :, column] = weights[:, 2 * dy + dz]
        if dy == 0:
            table[1, m, :, column] = weights[:, 2 * dx + dz]
        if dz == 0:
            table[2, m, :, column] = weights[:, 2 * dx + dy]
    high, low = in_two(table.reshape(144, 32))
    return np.concatenate([high, high, low], axis=1)


def kernel(
    count_x, count_y,
    lifted, keep, visc, diag, solve_t, flux_map, gather, spread,
    out,
    halo_x, halo_y, keep_x, keep_y, residual, high, send_x, send_y, recv_x, recv_y, vertex, rim_x, rim_y, rim_c,
    send_sem, recv_sem,
):
    wx, wy = lifted.shape[1], lifted.shape[2]
    faces, depth = lifted.shape[3], lifted.shape[4]
    me_x, me_y = lax.axis_index("gx"), lax.axis_index("gy")
    there = {-1: (me_x > 0, me_y > 0), 0: (None, None), 1: (me_x < count_x - 1, me_y < count_y - 1)}

    def present(dx, dy):
        a, b = there[dx][0], there[dy][1]
        if a is None:
            return b
        return a if b is None else jnp.logical_and(a, b)

    def device(dx, dy):
        return {"gx": me_x + dx, "gy": me_y + dy}

    around = [(dx, dy) for dx in (-1, 0, 1) for dy in (-1, 0, 1) if (dx, dy) != (0, 0)]
    barrier = pltpu.get_barrier_semaphore()
    total = 0
    for dx, dy in around:
        here = present(dx, dy)
        total = total + here.astype(jnp.int32)

        @pl.when(here)
        def _():
            pl.semaphore_signal(barrier, inc=1, device_id=device(dx, dy), device_id_type=MESH)

    pl.semaphore_wait(barrier, total)

    class Exchange:
        def __init__(self, slot, dx, dy, source, target):
            self.to, self.origin, self.target = present(dx, dy), present(-dx, -dy), target
            self.copy = pltpu.make_async_remote_copy(
                src_ref=source, dst_ref=target, send_sem=send_sem.at[slot], recv_sem=recv_sem.at[slot],
                device_id=device(dx, dy), device_id_type=MESH,
            )

        def start(self):
            pl.when(self.to)(self.copy.start)

            @pl.when(jnp.logical_not(self.origin))
            def _():
                self.target[...] = jnp.zeros(self.target.shape, self.target.dtype)

        def arrive(self):
            pl.when(self.origin)(self.copy.wait_recv)

        def drain(self):
            pl.when(self.to)(self.copy.wait_send)

    traces_x = Exchange(0, -1, 0, lifted.at[0, 0], halo_x)
    flags_x = Exchange(1, -1, 0, keep.at[0, 0], keep_x)
    traces_y = Exchange(2, 0, -1, lifted.at[1, :, 0], halo_y)
    flags_y = Exchange(3, 0, -1, keep.at[1, :, 0], keep_y)
    first = [traces_x, flags_x, traces_y, flags_y]
    for exchange in first:
        exchange.start()

    terms_x = Exchange(4, 1, 0, send_x, recv_x)
    terms_y = Exchange(5, 0, 1, send_y, recv_y)
    rims = {}
    for slot, (dx, dy) in enumerate(around):
        edge_x = {-1: 0, 1: wx}.get(dx)
        edge_y = {-1: 0, 1: wy}.get(dy)
        if dy == 0:
            source, target = vertex.at[edge_x], rim_x.at[(dx + 1) // 2]
        elif dx == 0:
            source, target = vertex.at[:, edge_y], rim_y.at[(dy + 1) // 2]
        else:
            source, target = vertex.at[edge_x, edge_y], rim_c.at[(dx + 1) // 2, (dy + 1) // 2]
        rims[dx, dy] = Exchange(6 + slot, dx, dy, source, target)

    lane = lax.broadcasted_iota(jnp.int32, (8, depth), 1)
    row = lax.broadcasted_iota(jnp.int32, (8, depth), 0)
    lane_faces = lax.broadcasted_iota(jnp.int32, (faces, depth), 1)

    def next_flag(x, y, d):
        if d == 0:
            return keep[0, x + 1, y] if x + 1 < wx else keep_x[y]
        if d == 1:
            return keep[1, x, y + 1] if y + 1 < wy else keep_y[x]
        flag = jnp.broadcast_to(keep[2, x, y], (8, depth))
        return jnp.where(lane == depth - 1, 0.0, pltpu.roll(flag, depth - 1, 1))[:1]

    corners = {}

    def process(columns):
        pieces = []
        for x, y in columns:
            low_z = lifted[2, x, y].astype(jnp.float32)
            high_z = jnp.where(lane_faces == depth - 1, 0.0, pltpu.roll(low_z, depth - 1, 1)).astype(jnp.bfloat16)
            pieces.append(
                jnp.concatenate(
                    [
                        lifted[0, x, y],
                        lifted[0, x + 1, y] if x + 1 < wx else halo_x[y],
                        lifted[1, x, y],
                        lifted[1, x, y + 1] if y + 1 < wy else halo_y[x],
                        lifted[2, x, y],
                        high_z,
                    ],
                    axis=0,
                )
            )
        element = jnp.concatenate(pieces, axis=1)
        interior = lax.dot_general(
            solve_t[...], element, (((0,), (0,)), ((), ())), preferred_element_type=jnp.float32
        ).astype(jnp.bfloat16)
        flux = jnp.dot(flux_map[...], interior, preferred_element_type=jnp.float32)
        rounded = []
        for index, (x, y) in enumerate(columns):
            lanes = slice(index * depth, (index + 1) * depth)
            parts = []
            for face_slot in range(6):
                rows = slice(face_slot * faces, (face_slot + 1) * faces)
                d, outward = face_slot // 2, face_slot % 2
                flag = next_flag(x, y, d) if outward else keep[d, x, y]
                scale = visc[x, y] * flag
                parts.append((flux[rows, lanes] + penalty * pieces[index][rows].astype(jnp.float32)) * scale)
            residual[0, x, y] = parts[0]
            residual[1, x, y] = parts[2]
            residual[2, x, y] = parts[4] + pltpu.roll(parts[5], 1, 1)
            cut = jnp.concatenate(parts, axis=0).astype(jnp.bfloat16)
            if x + 1 < wx:
                high[0, x, y] = parts[1]
            else:
                send_x[y] = cut[faces : 2 * faces]
            if y + 1 < wy:
                high[1, x, y] = parts[3]
            else:
                send_y[x] = cut[3 * faces : 4 * faces]
            rounded.append(cut)
        both = jnp.dot(gather[...], jnp.concatenate(rounded, axis=1), preferred_element_type=jnp.float32)
        sums = both[:32] + both[32:]
        for index, (x, y) in enumerate(columns):
            for dx, dy in itertools.product(range(2), range(2)):
                part = sums[16 * dx + 8 * dy : 16 * dx + 8 * dy + 8, index * depth : (index + 1) * depth]
                key = (x + dx, y + dy)
                corners[key] = part if key not in corners else corners[key] + part

    everything = list(itertools.product(range(wx), range(wy)))
    inner = [(x, y) for x, y in everything if x + 1 < wx and y + 1 < wy]
    need_x = [(x, y) for x, y in everything if x + 1 == wx and y + 1 < wy]
    need_y = [(x, y) for x, y in everything if y + 1 == wy]
    early = len(inner) // 4 * 4
    for start in range(0, early, 4):
        process(inner[start : start + 4])
    traces_x.arrive()
    flags_x.arrive()
    process(inner[early:] + need_x)
    traces_y.arrive()
    flags_y.arrive()
    process(need_y)

    for x, y in itertools.product(range(wx + 1), range(wy + 1)):
        value = corners[x, y]
        above = pltpu.roll(jnp.where(lane == depth - 1, 0.0, value), 1, 1)
        value = value + pltpu.roll(above, 4, 0)
        if x < wx and y < wy:
            vertex[x, y] = jnp.where(row == CORNER - 1, diag[x, y], value)
        else:
            vertex[x, y] = jnp.where(row == CORNER - 1, 0.0, value)
    for exchange in rims.values():
        exchange.start()
    terms_x.start()
    terms_y.start()

    for x, y in everything:
        if x:
            residual[0, x, y] += high[0, x - 1, y]
        if y:
            residual[1, x, y] += high[1, x, y - 1]

    for exchange in rims.values():
        exchange.arrive()
    fixes = {}
    for x, y in itertools.product(range(wx + 1), range(wy + 1)):
        value = vertex[x, y]
        side_x = {0: 1, wx: 0}.get(x)
        side_y = {0: 1, wy: 0}.get(y)
        if side_x is not None:
            value = value + rim_x[side_x, y]
        if side_y is not None:
            value = value + rim_y[side_y, x]
        if side_x is not None and side_y is not None:
            value = value + rim_c[side_x, side_y]
        inside = present(int(x == wx), int(y == wy))
        below = jnp.broadcast_to(value[CORNER - 1 : CORNER], value.shape)
        if inside is not None:
            value = jnp.where(inside, value, 0.0)
            below = jnp.where(inside, below, 1.0)
        fix = value / below
        above = jnp.where(lane == depth - 1, 0.0, pltpu.roll(fix, depth - 1, 1))
        fixes[x, y] = jnp.where(row < CORNER, fix, pltpu.roll(above, 4, 0))

    terms_x.arrive()
    terms_y.arrive()
    for x in range(wx):
        stacks = []
        for y in range(wy):
            value = jnp.concatenate([fixes[x, y], fixes[x, y + 1], fixes[x + 1, y], fixes[x + 1, y + 1]], axis=0)
            upper = value.astype(jnp.bfloat16)
            lower = (value - upper.astype(jnp.float32)).astype(jnp.bfloat16)
            stacks.append(jnp.concatenate([upper, lower, upper], axis=0))
        lift = jnp.dot(spread[...], jnp.concatenate(stacks, axis=1), preferred_element_type=jnp.float32)
        for y in range(wy):
            for d in range(3):
                value = residual[d, x, y]
                if d == 0 and x == 0:
                    value = value + recv_x[y].astype(jnp.float32)
                if d == 1 and y == 0:
                    value = value + recv_y[x].astype(jnp.float32)
                piece = lift[d * faces : (d + 1) * faces, y * depth : (y + 1) * depth]
                out[d, x, y] = (value + keep[d, x, y] * piece).astype(jnp.bfloat16)

    for exchange in first + list(rims.values()) + [terms_x, terms_y]:
        exchange.drain()


def cell_viscosity(visc_class, viscosity):
    result = jnp.zeros(visc_class.shape, jnp.float32)
    for level in range(viscosity.shape[0]):
        result = result + jnp.where(visc_class == level, viscosity[level], jnp.float32(0.0))
    return result


def local(count_x, count_y, traces, dirichlet, visc_class, viscosity, coarse_diag, solve_map, flux_map):
    faces, wx, wy, depth = traces.shape[1:]
    keep = (1 - dirichlet).astype(jnp.bfloat16)
    lifted = jnp.transpose(traces, (0, 2, 3, 1, 4)) * keep[:, :, :, None]
    operands = (
        lifted,
        keep.astype(jnp.float32)[:, :, :, None],
        cell_viscosity(visc_class, viscosity)[:, :, None],
        coarse_diag[:, :, None],
        solve_map.T,
        flux_map,
        jnp.asarray(gather_table()),
        jnp.asarray(spread_table()),
    )
    whole = pl.BlockSpec(memory_space=pltpu.VMEM)
    exchanges = 14
    result = pl.pallas_call(
        functools.partial(kernel, count_x, count_y),
        out_shape=jax.ShapeDtypeStruct((3, wx, wy, faces, depth), jnp.bfloat16),
        in_specs=[whole] * len(operands),
        out_specs=whole,
        scratch_shapes=[
            pltpu.VMEM((wy, faces, depth), jnp.bfloat16),
            pltpu.VMEM((wx, faces, depth), jnp.bfloat16),
            pltpu.VMEM((wy, 1, depth), jnp.float32),
            pltpu.VMEM((wx, 1, depth), jnp.float32),
            pltpu.VMEM((3, wx, wy, faces, depth), jnp.float32),
            pltpu.VMEM((2, wx, wy, faces, depth), jnp.float32),
            pltpu.VMEM((wy, faces, depth), jnp.bfloat16),
            pltpu.VMEM((wx, faces, depth), jnp.bfloat16),
            pltpu.VMEM((wy, faces, depth), jnp.bfloat16),
            pltpu.VMEM((wx, faces, depth), jnp.bfloat16),
            pltpu.VMEM((wx + 1, wy + 1, 8, depth), jnp.float32),
            pltpu.VMEM((2, wy + 1, 8, depth), jnp.float32),
            pltpu.VMEM((2, wx + 1, 8, depth), jnp.float32),
            pltpu.VMEM((2, 2, 8, depth), jnp.float32),
            pltpu.SemaphoreType.DMA((exchanges,)),
            pltpu.SemaphoreType.DMA((exchanges,)),
        ],
        compiler_params=pltpu.CompilerParams(collective_id=0, has_side_effects=True),
        name="apply",
    )(*operands)
    return jnp.transpose(result, (0, 3, 1, 2, 4))


def solution(mesh):
    count_x, count_y = mesh.shape["gx"], mesh.shape["gy"]
    in_specs = (
        P(None, None, "gx", "gy", None),
        P(None, "gx", "gy", None),
        P("gx", "gy", None),
        P(),
        P("gx", "gy", None),
        P(),
        P(),
    )
    out_specs = P(None, None, "gx", "gy", None)
    return jax.shard_map(
        functools.partial(local, count_x, count_y), mesh=mesh, in_specs=in_specs, out_specs=out_specs, check_vma=False
    )
```

```python
import functools
import itertools
import math

import jax
import jax.numpy as jnp
import ml_dtypes
import numpy as np
from jax import lax
from jax.experimental import pallas as pl
from jax.experimental.pallas import tpu as pltpu
from jax.sharding import PartitionSpec as P

MESH = pl.DeviceIdType.MESH
penalty = 0.5
CORNER = 4


def corner_table():
    points = [-1.0, -math.sqrt(0.2), math.sqrt(0.2), 1.0]
    table = np.zeros((16, 4), np.float64)
    for a, b, p, q in itertools.product(range(4), range(4), range(2), range(2)):
        table[4 * a + b, 2 * p + q] = (1 + (2 * p - 1) * points[a]) * (1 + (2 * q - 1) * points[b]) / 4
    return table.astype(np.float32)


def in_two(table):
    high = table.astype(ml_dtypes.bfloat16)
    low = (table - high.astype(np.float32)).astype(ml_dtypes.bfloat16)
    return high, low


def gather_table():
    weights = corner_table()
    table = np.zeros((32, 6, 3, 16), np.float32)
    for dx, dy, dz, m in itertools.product(range(2), range(2), range(2), range(3)):
        row = 16 * dx + 8 * dy + CORNER * dz + m
        table[row, dx, m] = weights[:, 2 * dy + dz]
        table[row, 2 + dy, m] = weights[:, 2 * dx + dz]
        table[row, 4 + dz, m] = weights[:, 2 * dx + dy]
    return np.concatenate(in_two(table.reshape(32, 288)), axis=0)


def spread_table():
    weights = corner_table()
    table = np.zeros((3, 3, 16, 32), np.float32)
    for dx, dy, dz, m in itertools.product(range(2), range(2), range(2), range(3)):
        column = 16 * dx + 8 * dy + CORNER * dz + m
        if dx == 0:
            table[0, m, :, column] = weights[:, 2 * dy + dz]
        if dy == 0:
            table[1, m, :, column] = weights[:, 2 * dx + dz]
        if dz == 0:
            table[2, m, :, column] = weights[:, 2 * dx + dy]
    high, low = in_two(table.reshape(144, 32))
    return np.concatenate([high, high, low], axis=1)


def one_hot(rows):
    i = lax.broadcasted_iota(jnp.int32, (rows, rows), 0)
    j = lax.broadcasted_iota(jnp.int32, (rows, rows), 1)
    hit = jnp.logical_and((i & 15) == (j >> 4), (i >> 4) == (j & 15))
    return jnp.where(hit, 1.0, 0.0).astype(jnp.bfloat16)


def kernel(
    count_x, count_y, wx, wy,
    traces_hbm, dirichlet_hbm, class_hbm, viscosity_hbm, diag_hbm, solve_hbm, flux_hbm, gather_hbm, spread_hbm,
    out_hbm,
    traces, dirichlet, classes, viscosity, diag, solve_t, flux_map, gather, spread, result,
    swap, solve_map, lifted, keep, scale, halo_x, halo_y, first_y, flag_x, flag_y, keep_x, keep_y,
    residual, high, final, send_x, send_y, recv_x, recv_y,
    edge_x, edge_y, edge_c, rim_x, rim_y, rim_c,
    load_sem, store_sem, send_sem, recv_sem, ready,
):
    columns, depth = wx * wy, traces.shape[3]
    faces = traces.shape[1]
    groups = faces // 16
    me_x, me_y = lax.axis_index("gx"), lax.axis_index("gy")
    there = {-1: (me_x > 0, me_y > 0), 0: (None, None), 1: (me_x < count_x - 1, me_y < count_y - 1)}

    def present(dx, dy):
        a, b = there[dx][0], there[dy][1]
        if a is None:
            return b
        return a if b is None else jnp.logical_and(a, b)

    def device(dx, dy):
        return {"gx": me_x + dx, "gy": me_y + dy}

    around = [(-1, -1), (1, -1), (-1, 1), (1, 1), (0, -1), (0, 1), (-1, 0), (1, 0)]
    barrier = pltpu.get_barrier_semaphore()
    total = 0
    for dx, dy in around[4:]:
        here = present(dx, dy)
        total = total + here.astype(jnp.int32)

        @pl.when(here)
        def _():
            pl.semaphore_signal(barrier, inc=1, device_id=device(dx, dy), device_id_type=MESH)

    loads = [
        (dirichlet_hbm, dirichlet), (traces_hbm.at[0], traces.at[0]), (traces_hbm.at[1], traces.at[1]),
        (traces_hbm.at[2], traces.at[2]), (viscosity_hbm, viscosity), (class_hbm, classes), (solve_hbm, solve_t),
        (flux_hbm, flux_map), (gather_hbm, gather), (diag_hbm, diag), (spread_hbm, spread),
    ]
    loads = [pltpu.make_async_copy(a, b, load_sem.at[i]) for i, (a, b) in enumerate(loads)]
    for load in loads:
        load.start()

    class Exchange:
        def __init__(self, slot, dx, dy, source, target):
            self.to, self.origin, self.target = present(dx, dy), present(-dx, -dy), target
            self.copy = pltpu.make_async_remote_copy(
                src_ref=source, dst_ref=target, send_sem=send_sem.at[slot], recv_sem=recv_sem.at[slot],
                device_id=device(dx, dy), device_id_type=MESH,
            )

        def clear(self):
            @pl.when(jnp.logical_not(self.origin))
            def _():
                self.target[...] = jnp.zeros(self.target.shape, self.target.dtype)

        def start(self):
            pl.when(self.to)(self.copy.start)

        def arrive(self):
            pl.when(self.origin)(self.copy.wait_recv)

        def drain(self):
            pl.when(self.to)(self.copy.wait_send)

    traces_x = Exchange(0, -1, 0, lifted.at[0, pl.ds(0, wy)], halo_x)
    flags_x = Exchange(1, -1, 0, flag_x, keep_x)
    traces_y = Exchange(2, 0, -1, first_y, halo_y)
    flags_y = Exchange(3, 0, -1, flag_y, keep_y)
    terms_x = Exchange(4, 1, 0, send_x, recv_x)
    terms_y = Exchange(5, 0, 1, send_y, recv_y)
    first = [flags_y, traces_y, flags_x, traces_x]
    rims = []
    for slot, (dx, dy) in enumerate(around):
        if dy == 0:
            source, target = edge_x.at[(dx + 1) // 2], rim_x.at[(dx + 1) // 2]
        elif dx == 0:
            source, target = edge_y.at[(dy + 1) // 2], rim_y.at[(dy + 1) // 2]
        else:
            source, target = edge_c.at[(dx + 1) // 2, (dy + 1) // 2], rim_c.at[(dx + 1) // 2, (dy + 1) // 2]
        rims.append(Exchange(6 + slot, dx, dy, source, target))
    for exchange in first + [terms_x, terms_y] + rims:
        exchange.clear()

    swap[...] = one_hot(256)
    lane = lax.broadcasted_iota(jnp.int32, (8, depth), 1)
    row = lax.broadcasted_iota(jnp.int32, (8, depth), 0)
    lane_faces = lax.broadcasted_iota(jnp.int32, (faces, depth), 1)

    def to_columns(pairs):
        moved = jnp.concatenate([traces[d, 16 * g : 16 * g + 16].reshape(256, depth) for d, g in pairs], axis=1)
        moved = jnp.dot(swap[...], moved, preferred_element_type=jnp.float32)
        for index, (d, g) in enumerate(pairs):
            for c in range(columns):
                piece = moved[16 * c : 16 * c + 16, index * depth : (index + 1) * depth]
                lifted[d, c, 16 * g : 16 * g + 16] = (piece * keep[d, c : c + 1]).astype(jnp.bfloat16)

    def in_pairs(items):
        return [items[i : i + 2] for i in range(0, len(items), 2)]

    loads[0].wait()
    keep[...] = 1.0 - dirichlet[...].astype(jnp.float32)
    flag_x[...] = keep[0, :wy]
    for x in range(wx):
        flag_y[x : x + 1] = keep[1, x * wy : x * wy + 1]
    loads[1].wait()
    loads[2].wait()
    for pair in in_pairs([(d, g) for d in (1, 0) for g in range(groups)]):
        to_columns(pair)
    for x in range(wx):
        first_y[x] = lifted[1, x * wy]
    pl.semaphore_wait(barrier, total)
    for exchange in first:
        exchange.start()
    for dx in (-1, 1):

        @pl.when(present(dx, 0))
        def _():
            pl.semaphore_signal(ready, inc=1, device_id=device(dx, 0), device_id_type=MESH)

    loads[3].wait()
    for pair in in_pairs([(2, g) for g in range(groups)]):
        to_columns(pair)
    for load in loads[4:7]:
        load.wait()
    solve_map[...] = solve_t[...].T
    visc = jnp.zeros(classes.shape, jnp.float32)
    for level in range(viscosity.shape[0]):
        visc = visc + jnp.where(classes[...] == level, viscosity[level], 0.0)
    lanes_c = lax.broadcasted_iota(jnp.int32, (columns, depth), 1)
    for d in range(3):
        scale[2 * d] = visc * keep[d]
    scale[5] = visc * jnp.where(lanes_c == depth - 1, 0.0, pltpu.roll(keep[2], depth - 1, 1))
    scale[1, : columns - wy] = visc[: columns - wy] * keep[0, wy:]
    scale[3, : columns - 1] = visc[: columns - 1] * keep[1, 1:]
    for load in loads[7:]:
        load.wait()

    corners = {}

    def process(chosen, after_terms=lambda: None):
        pieces = []
        for c in chosen:
            x, y = c // wy, c % wy
            low_z = lifted[2, c].astype(jnp.float32)
            high_z = jnp.where(lane_faces == depth - 1, 0.0, pltpu.roll(low_z, depth - 1, 1)).astype(jnp.bfloat16)
            pieces.append(
                jnp.concatenate(
                    [
                        lifted[0, c],
                        lifted[0, c + wy] if x + 1 < wx else halo_x[y],
                        lifted[1, c],
                        lifted[1, c + 1] if y + 1 < wy else halo_y[x],
                        lifted[2, c],
                        high_z,
                    ],
                    axis=0,
                )
            )
        element = jnp.concatenate(pieces, axis=1)
        interior = jnp.dot(solve_map[...], element, preferred_element_type=jnp.float32).astype(jnp.bfloat16)
        flux = jnp.dot(flux_map[...], interior, preferred_element_type=jnp.float32)
        rounded = []
        for index, c in enumerate(chosen):
            x, y = c // wy, c % wy
            lanes = slice(index * depth, (index + 1) * depth)
            parts = []
            for face_slot in range(6):
                rows = slice(face_slot * faces, (face_slot + 1) * faces)
                term = flux[rows, lanes] + penalty * pieces[index][rows].astype(jnp.float32)
                parts.append(term * scale[face_slot, c : c + 1])
            residual[0, c] = parts[0]
            residual[1, c] = parts[2]
            residual[2, c] = parts[4] + pltpu.roll(parts[5], 1, 1)
            cut = jnp.concatenate(parts, axis=0).astype(jnp.bfloat16)
            if x + 1 < wx:
                high[0, c] = parts[1]
            else:
                send_x[y] = cut[faces : 2 * faces]
            if y + 1 < wy:
                high[1, c] = parts[3]
            else:
                send_y[x] = cut[3 * faces : 4 * faces]
            rounded.append(cut)
        after_terms()
        both = jnp.dot(gather[...], jnp.concatenate(rounded, axis=1), preferred_element_type=jnp.float32)
        sums = both[:32] + both[32:]
        for index, c in enumerate(chosen):
            x, y = c // wy, c % wy
            for dx, dy in itertools.product(range(2), range(2)):
                part = sums[16 * dx + 8 * dy : 16 * dx + 8 * dy + 8, index * depth : (index + 1) * depth]
                key = (x + dx, y + dy)
                corners[key] = part if key not in corners else corners[key] + part

    inner = [c for c in range(columns) if c + wy < columns and c % wy + 1 < wy]
    need_x = [c for c in range(columns) if c + wy >= columns and c % wy + 1 < wy]
    need_y = [c for c in range(columns) if c % wy + 1 == wy]
    early = len(inner) // 4 * 4
    for start in range(0, early, 4):
        process(inner[start : start + 4])
    flags_x.arrive()
    traces_x.arrive()
    scale[1, columns - wy :] = visc[columns - wy :] * keep_x[...]
    process(inner[early:] + need_x)
    flags_y.arrive()
    traces_y.arrive()
    for x in range(wx):
        c = x * wy + wy - 1
        scale[3, c : c + 1] = visc[c : c + 1] * keep_y[x : x + 1]

    def terms_out():
        terms_y.start()
        terms_x.start()

    process(need_y, terms_out)

    vertices = list(itertools.product(range(wx + 1), range(wy + 1)))
    for x, y in vertices:
        value = corners[x, y]
        above = pltpu.roll(jnp.where(lane == depth - 1, 0.0, value), 1, 1)
        value = value + pltpu.roll(above, 4, 0)
        if x < wx and y < wy:
            corners[x, y] = jnp.where(row == CORNER - 1, diag[x * wy + y : x * wy + y + 1], value)
        else:
            corners[x, y] = jnp.where(row == CORNER - 1, 0.0, value)

    def pack(target, values):
        for i in range(0, len(values), 2):
            value = values[i]
            if i + 1 < len(values):
                value = jnp.where(row < CORNER, value, pltpu.roll(values[i + 1], 4, 0))
            target[i // 2] = value

    for side in range(2):
        for other in range(2):
            edge_c[side, other] = corners[side * wx, other * wy]
    for side in range(2):
        pack(edge_y.at[side], [corners[x, side * wy] for x in range(wx + 1)])
        pack(edge_x.at[side], [corners[side * wx, y] for y in range(wy + 1)])
    pl.semaphore_wait(ready, there[-1][0].astype(jnp.int32) + there[1][0].astype(jnp.int32))
    for exchange in rims:
        exchange.start()

    for c in range(columns):
        if c >= wy:
            residual[0, c] += high[0, c - wy]
        if c % wy:
            residual[1, c] += high[1, c - 1]

    for exchange in rims:
        exchange.arrive()

    def unpack(source, index):
        value = source[index // 2]
        return pltpu.roll(value, 4, 0) if index % 2 else value

    fixes = {}
    for x, y in vertices:
        value = corners[x, y]
        side_x = {0: 0, wx: 1}.get(x)
        side_y = {0: 0, wy: 1}.get(y)
        if side_x is not None:
            value = value + unpack(rim_x.at[1 - side_x], y)
        if side_y is not None:
            value = value + unpack(rim_y.at[1 - side_y], x)
        if side_x is not None and side_y is not None:
            value = value + rim_c[1 - side_x, 1 - side_y]
        inside = present(int(x == wx), int(y == wy))
        below = jnp.broadcast_to(value[CORNER - 1 : CORNER], value.shape)
        if inside is not None:
            value = jnp.where(inside, value, 0.0)
            below = jnp.where(inside, below, 1.0)
        fix = value / below
        above = jnp.where(lane == depth - 1, 0.0, pltpu.roll(fix, depth - 1, 1))
        fixes[x, y] = jnp.where(row < CORNER, fix, pltpu.roll(above, 4, 0))

    stacks = []
    for c in range(columns):
        x, y = c // wy, c % wy
        value = jnp.concatenate([fixes[x, y], fixes[x, y + 1], fixes[x + 1, y], fixes[x + 1, y + 1]], axis=0)
        upper = value.astype(jnp.bfloat16)
        lower = (value - upper.astype(jnp.float32)).astype(jnp.bfloat16)
        stacks.append(jnp.concatenate([upper, lower, upper], axis=0))
    stores = []
    for d in (2, 0, 1):
        if d == 0:
            terms_x.arrive()
        if d == 1:
            terms_y.arrive()
        for start in range(0, columns, 4):
            chosen = range(start, start + 4)
            lift = jnp.dot(
                spread[d * faces : (d + 1) * faces],
                jnp.concatenate([stacks[c] for c in chosen], axis=1),
                preferred_element_type=jnp.float32,
            )
            for index, c in enumerate(chosen):
                x, y = c // wy, c % wy
                value = residual[d, c]
                if d == 0 and x == 0:
                    value = value + recv_x[y].astype(jnp.float32)
                if d == 1 and y == 0:
                    value = value + recv_y[x].astype(jnp.float32)
                piece = lift[:, index * depth : (index + 1) * depth]
                final[d, c] = (value + keep[d, c : c + 1] * piece).astype(jnp.bfloat16)
        for pair in in_pairs(list(range(groups))):
            moved = jnp.concatenate(
                [final[d, :, 16 * g : 16 * g + 16].reshape(256, depth) for g in pair], axis=1
            )
            moved = jnp.dot(swap[...], moved, preferred_element_type=jnp.float32).astype(jnp.bfloat16)
            for index, g in enumerate(pair):
                piece = moved[:, index * depth : (index + 1) * depth]
                result[d, 16 * g : 16 * g + 16] = piece.reshape(16, columns, depth)
        stores.append(pltpu.make_async_copy(result.at[d], out_hbm.at[d], store_sem.at[d]))
        stores[-1].start()

    for exchange in first + rims + [terms_x, terms_y]:
        exchange.drain()
    for store in stores:
        store.wait()


def local(count_x, count_y, traces, dirichlet, visc_class, viscosity, coarse_diag, solve_map, flux_map):
    faces, wx, wy, depth = traces.shape[1:]
    columns = wx * wy
    inner = solve_map.shape[0]
    operands = (
        traces.reshape(3, faces, columns, depth),
        dirichlet.reshape(3, columns, depth),
        visc_class.reshape(columns, depth),
        viscosity,
        coarse_diag.reshape(columns, depth),
        solve_map.T,
        flux_map,
        jnp.asarray(gather_table()),
        jnp.asarray(spread_table()),
    )
    anywhere = pl.BlockSpec(memory_space=pl.ANY)
    exchanges = 14
    rims_x, rims_y = wy // 2 + 1, wx // 2 + 1
    f32, bf16 = jnp.float32, jnp.bfloat16
    scratch = [
        pltpu.SMEM(a.shape, a.dtype) if index == 3 else pltpu.VMEM(a.shape, a.dtype) for index, a in enumerate(operands)
    ] + [
        pltpu.VMEM((3, faces, columns, depth), bf16),
        pltpu.VMEM((256, 256), bf16),
        pltpu.VMEM((inner, 6 * faces), bf16),
        pltpu.VMEM((3, columns, faces, depth), bf16),
        pltpu.VMEM((3, columns, depth), f32),
        pltpu.VMEM((6, columns, depth), f32),
        pltpu.VMEM((wy, faces, depth), bf16),
        pltpu.VMEM((wx, faces, depth), bf16),
        pltpu.VMEM((wx, faces, depth), bf16),
        pltpu.VMEM((wy, depth), f32),
        pltpu.VMEM((wx, depth), f32),
        pltpu.VMEM((wy, depth), f32),
        pltpu.VMEM((wx, depth), f32),
        pltpu.VMEM((3, columns, faces, depth), f32),
        pltpu.VMEM((2, columns, faces, depth), f32),
        pltpu.VMEM((3, columns, faces, depth), bf16),
        pltpu.VMEM((wy, faces, depth), bf16),
        pltpu.VMEM((wx, faces, depth), bf16),
        pltpu.VMEM((wy, faces, depth), bf16),
        pltpu.VMEM((wx, faces, depth), bf16),
        pltpu.VMEM((2, rims_x, 8, depth), f32),
        pltpu.VMEM((2, rims_y, 8, depth), f32),
        pltpu.VMEM((2, 2, 8, depth), f32),
        pltpu.VMEM((2, rims_x, 8, depth), f32),
        pltpu.VMEM((2, rims_y, 8, depth), f32),
        pltpu.VMEM((2, 2, 8, depth), f32),
        pltpu.SemaphoreType.DMA((len(operands) + 2,)),
        pltpu.SemaphoreType.DMA((3,)),
        pltpu.SemaphoreType.DMA((exchanges,)),
        pltpu.SemaphoreType.DMA((exchanges,)),
        pltpu.SemaphoreType.REGULAR,
    ]
    result = pl.pallas_call(
        functools.partial(kernel, count_x, count_y, wx, wy),
        out_shape=jax.ShapeDtypeStruct((3, faces, columns, depth), bf16),
        in_specs=[anywhere] * len(operands),
        out_specs=anywhere,
        scratch_shapes=scratch,
        compiler_params=pltpu.CompilerParams(collective_id=0, has_side_effects=True),
        name="apply",
    )(*operands)
    return result.reshape(3, faces, wx, wy, depth)


def solution(mesh):
    count_x, count_y = mesh.shape["gx"], mesh.shape["gy"]
    in_specs = (
        P(None, None, "gx", "gy", None),
        P(None, "gx", "gy", None),
        P("gx", "gy", None),
        P(),
        P("gx", "gy", None),
        P(),
        P(),
    )
    out_specs = P(None, None, "gx", "gy", None)
    return jax.shard_map(
        functools.partial(local, count_x, count_y), mesh=mesh, in_specs=in_specs, out_specs=out_specs, check_vma=False
    )
```

```python
import functools
import itertools
import math

import jax
import jax.numpy as jnp
import ml_dtypes
import numpy as np
from jax import lax
from jax.experimental import pallas as pl
from jax.experimental.pallas import tpu as pltpu
from jax.sharding import PartitionSpec as P

MESH = pl.DeviceIdType.MESH
penalty = 0.5
CORNER = 4


def corner_table():
    points = [-1.0, -math.sqrt(0.2), math.sqrt(0.2), 1.0]
    table = np.zeros((16, 4), np.float64)
    for a, b, p, q in itertools.product(range(4), range(4), range(2), range(2)):
        table[4 * a + b, 2 * p + q] = (1 + (2 * p - 1) * points[a]) * (1 + (2 * q - 1) * points[b]) / 4
    return table.astype(np.float32)


def in_two(table):
    high = table.astype(ml_dtypes.bfloat16)
    low = (table - high.astype(np.float32)).astype(ml_dtypes.bfloat16)
    return high, low


def gather_table():
    weights = corner_table()
    table = np.zeros((32, 6, 3, 16), np.float32)
    for dx, dy, dz, m in itertools.product(range(2), range(2), range(2), range(3)):
        row = 16 * dx + 8 * dy + CORNER * dz + m
        table[row, dx, m] = weights[:, 2 * dy + dz]
        table[row, 2 + dy, m] = weights[:, 2 * dx + dz]
        table[row, 4 + dz, m] = weights[:, 2 * dx + dy]
    return np.concatenate(in_two(table.reshape(32, 288)), axis=0)


def spread_table():
    weights = corner_table()
    table = np.zeros((3, 3, 16, 32), np.float32)
    for dx, dy, dz, m in itertools.product(range(2), range(2), range(2), range(3)):
        column = 16 * dx + 8 * dy + CORNER * dz + m
        if dx == 0:
            table[0, m, :, column] = weights[:, 2 * dy + dz]
        if dy == 0:
            table[1, m, :, column] = weights[:, 2 * dx + dz]
        if dz == 0:
            table[2, m, :, column] = weights[:, 2 * dx + dy]
    high, low = in_two(table.reshape(144, 32))
    return np.concatenate([high, high, low], axis=1)


def kernel(
    count_x, count_y, wx, wy,
    traces_hbm, dirichlet_hbm, class_hbm, viscosity_hbm, diag_hbm, solve_hbm, flux_hbm, gather_hbm, spread_hbm,
    out,
    traces, dirichlet, classes, viscosity, diag, solve_t, flux_map, gather, spread,
    staged, solve_map, lifted, keep, scale, halo_x, halo_y, first_y, flag_x, flag_y, keep_x, keep_y,
    residual, high, send_x, send_y, recv_x, recv_y,
    edge_x, edge_y, edge_c, rim_x, rim_y, rim_c,
    load_sem, send_sem, recv_sem, ready,
):
    columns, depth = wx * wy, traces.shape[3]
    faces = traces.shape[1]
    me_x, me_y = lax.axis_index("gx"), lax.axis_index("gy")
    there = {-1: (me_x > 0, me_y > 0), 0: (None, None), 1: (me_x < count_x - 1, me_y < count_y - 1)}

    def present(dx, dy):
        a, b = there[dx][0], there[dy][1]
        if a is None:
            return b
        return a if b is None else jnp.logical_and(a, b)

    def device(dx, dy):
        return {"gx": me_x + dx, "gy": me_y + dy}

    around = [(-1, -1), (1, -1), (-1, 1), (1, 1), (0, -1), (0, 1), (-1, 0), (1, 0)]
    barrier = pltpu.get_barrier_semaphore()
    total = 0
    for dx, dy in around[4:]:
        here = present(dx, dy)
        total = total + here.astype(jnp.int32)

        @pl.when(here)
        def _():
            pl.semaphore_signal(barrier, inc=1, device_id=device(dx, dy), device_id_type=MESH)

    loads = [
        (dirichlet_hbm, dirichlet), (traces_hbm.at[0], traces.at[0]), (traces_hbm.at[1], traces.at[1]),
        (traces_hbm.at[2], traces.at[2]), (viscosity_hbm, viscosity), (class_hbm, classes), (solve_hbm, solve_t),
        (flux_hbm, flux_map), (gather_hbm, gather), (diag_hbm, diag), (spread_hbm, spread),
    ]
    loads = [pltpu.make_async_copy(a, b, load_sem.at[i]) for i, (a, b) in enumerate(loads)]
    for load in loads:
        load.start()

    class Exchange:
        def __init__(self, slot, dx, dy, source, target):
            self.to, self.origin, self.target = present(dx, dy), present(-dx, -dy), target
            self.copy = pltpu.make_async_remote_copy(
                src_ref=source, dst_ref=target, send_sem=send_sem.at[slot], recv_sem=recv_sem.at[slot],
                device_id=device(dx, dy), device_id_type=MESH,
            )

        def clear(self):
            @pl.when(jnp.logical_not(self.origin))
            def _():
                self.target[...] = jnp.zeros(self.target.shape, self.target.dtype)

        def start(self):
            pl.when(self.to)(self.copy.start)

        def arrive(self):
            pl.when(self.origin)(self.copy.wait_recv)

        def drain(self):
            pl.when(self.to)(self.copy.wait_send)

    traces_x = Exchange(0, -1, 0, lifted.at[0, pl.ds(0, wy)], halo_x)
    flags_x = Exchange(1, -1, 0, flag_x, keep_x)
    traces_y = Exchange(2, 0, -1, first_y, halo_y)
    flags_y = Exchange(3, 0, -1, flag_y, keep_y)
    terms_x = Exchange(4, 1, 0, send_x, recv_x)
    terms_y = Exchange(5, 0, 1, send_y, recv_y)
    first = [flags_y, traces_y, flags_x, traces_x]
    rims = []
    for slot, (dx, dy) in enumerate(around):
        if dy == 0:
            source, target = edge_x.at[(dx + 1) // 2], rim_x.at[(dx + 1) // 2]
        elif dx == 0:
            source, target = edge_y.at[(dy + 1) // 2], rim_y.at[(dy + 1) // 2]
        else:
            source, target = edge_c.at[(dx + 1) // 2, (dy + 1) // 2], rim_c.at[(dx + 1) // 2, (dy + 1) // 2]
        rims.append(Exchange(6 + slot, dx, dy, source, target))
    for exchange in first + [terms_x, terms_y] + rims:
        exchange.clear()

    lane = lax.broadcasted_iota(jnp.int32, (8, depth), 1)
    row = lax.broadcasted_iota(jnp.int32, (8, depth), 0)
    lane_faces = lax.broadcasted_iota(jnp.int32, (faces, depth), 1)

    def to_columns(d):
        for n in range(faces):
            staged[d, n * columns : (n + 1) * columns] = traces[d, n].astype(jnp.float32) * keep[d]
        for c in range(columns):
            lifted[d, c] = staged[d, pl.ds(c, faces, stride=columns)].astype(jnp.bfloat16)

    loads[0].wait()
    keep[...] = 1.0 - dirichlet[...].astype(jnp.float32)
    flag_x[...] = keep[0, :wy]
    for x in range(wx):
        flag_y[x : x + 1] = keep[1, x * wy : x * wy + 1]
    loads[1].wait()
    loads[2].wait()
    to_columns(1)
    to_columns(0)
    for x in range(wx):
        first_y[x] = lifted[1, x * wy]
    pl.semaphore_wait(barrier, total)
    for exchange in first:
        exchange.start()
    for dx in (-1, 1):

        @pl.when(present(dx, 0))
        def _():
            pl.semaphore_signal(ready, inc=1, device_id=device(dx, 0), device_id_type=MESH)

    loads[3].wait()
    to_columns(2)
    for load in loads[4:7]:
        load.wait()
    solve_map[...] = solve_t[...].T
    visc = jnp.zeros(classes.shape, jnp.float32)
    for level in range(viscosity.shape[0]):
        visc = visc + jnp.where(classes[...] == level, viscosity[level], 0.0)
    lanes_c = lax.broadcasted_iota(jnp.int32, (columns, depth), 1)
    for d in range(3):
        scale[2 * d] = visc * keep[d]
    scale[5] = visc * jnp.where(lanes_c == depth - 1, 0.0, pltpu.roll(keep[2], depth - 1, 1))
    scale[1, : columns - wy] = visc[: columns - wy] * keep[0, wy:]
    scale[3, : columns - 1] = visc[: columns - 1] * keep[1, 1:]
    for load in loads[7:]:
        load.wait()

    corners = {}

    def process(chosen, after_terms=lambda: None):
        pieces = []
        for c in chosen:
            x, y = c // wy, c % wy
            low_z = lifted[2, c].astype(jnp.float32)
            high_z = jnp.where(lane_faces == depth - 1, 0.0, pltpu.roll(low_z, depth - 1, 1)).astype(jnp.bfloat16)
            pieces.append(
                jnp.concatenate(
                    [
                        lifted[0, c],
                        lifted[0, c + wy] if x + 1 < wx else halo_x[y],
                        lifted[1, c],
                        lifted[1, c + 1] if y + 1 < wy else halo_y[x],
                        lifted[2, c],
                        high_z,
                    ],
                    axis=0,
                )
            )
        element = jnp.concatenate(pieces, axis=1)
        interior = jnp.dot(solve_map[...], element, preferred_element_type=jnp.float32).astype(jnp.bfloat16)
        flux = jnp.dot(flux_map[...], interior, preferred_element_type=jnp.float32)
        rounded = []
        for index, c in enumerate(chosen):
            x, y = c // wy, c % wy
            lanes = slice(index * depth, (index + 1) * depth)
            parts = []
            for face_slot in range(6):
                rows = slice(face_slot * faces, (face_slot + 1) * faces)
                term = flux[rows, lanes] + penalty * pieces[index][rows].astype(jnp.float32)
                parts.append(term * scale[face_slot, c : c + 1])
            residual[0, c] = parts[0]
            residual[1, c] = parts[2]
            residual[2, c] = parts[4] + pltpu.roll(parts[5], 1, 1)
            cut = jnp.concatenate(parts, axis=0).astype(jnp.bfloat16)
            if x + 1 < wx:
                high[0, c] = parts[1]
            else:
                send_x[y] = cut[faces : 2 * faces]
            if y + 1 < wy:
                high[1, c] = parts[3]
            else:
                send_y[x] = cut[3 * faces : 4 * faces]
            rounded.append(cut)
        after_terms()
        both = jnp.dot(gather[...], jnp.concatenate(rounded, axis=1), preferred_element_type=jnp.float32)
        sums = both[:32] + both[32:]
        for index, c in enumerate(chosen):
            x, y = c // wy, c % wy
            for dx, dy in itertools.product(range(2), range(2)):
                part = sums[16 * dx + 8 * dy : 16 * dx + 8 * dy + 8, index * depth : (index + 1) * depth]
                key = (x + dx, y + dy)
                corners[key] = part if key not in corners else corners[key] + part

    inner = [c for c in range(columns) if c + wy < columns and c % wy + 1 < wy]
    need_x = [c for c in range(columns) if c + wy >= columns and c % wy + 1 < wy]
    need_y = [c for c in range(columns) if c % wy + 1 == wy]
    early = len(inner) // 4 * 4
    for start in range(0, early, 4):
        process(inner[start : start + 4])
    flags_x.arrive()
    traces_x.arrive()
    scale[1, columns - wy :] = visc[columns - wy :] * keep_x[...]
    process(inner[early:] + need_x)
    flags_y.arrive()
    traces_y.arrive()
    for x in range(wx):
        c = x * wy + wy - 1
        scale[3, c : c + 1] = visc[c : c + 1] * keep_y[x : x + 1]

    def terms_out():
        terms_y.start()
        terms_x.start()

    process(need_y, terms_out)

    vertices = list(itertools.product(range(wx + 1), range(wy + 1)))
    for x, y in vertices:
        value = corners[x, y]
        above = pltpu.roll(jnp.where(lane == depth - 1, 0.0, value), 1, 1)
        value = value + pltpu.roll(above, 4, 0)
        if x < wx and y < wy:
            corners[x, y] = jnp.where(row == CORNER - 1, diag[x * wy + y : x * wy + y + 1], value)
        else:
            corners[x, y] = jnp.where(row == CORNER - 1, 0.0, value)

    def pack(target, values):
        for i in range(0, len(values), 2):
            value = values[i]
            if i + 1 < len(values):
                value = jnp.where(row < CORNER, value, pltpu.roll(values[i + 1], 4, 0))
            target[i // 2] = value

    for side in range(2):
        for other in range(2):
            edge_c[side, other] = corners[side * wx, other * wy]
    for side in range(2):
        pack(edge_y.at[side], [corners[x, side * wy] for x in range(wx + 1)])
        pack(edge_x.at[side], [corners[side * wx, y] for y in range(wy + 1)])
    pl.semaphore_wait(ready, there[-1][0].astype(jnp.int32) + there[1][0].astype(jnp.int32))
    for exchange in rims:
        exchange.start()

    for c in range(columns):
        if c >= wy:
            residual[0, c] += high[0, c - wy]
        if c % wy:
            residual[1, c] += high[1, c - 1]

    for exchange in rims:
        exchange.arrive()

    def unpack(source, index):
        value = source[index // 2]
        return pltpu.roll(value, 4, 0) if index % 2 else value

    fixes = {}
    for x, y in vertices:
        value = corners[x, y]
        side_x = {0: 0, wx: 1}.get(x)
        side_y = {0: 0, wy: 1}.get(y)
        if side_x is not None:
            value = value + unpack(rim_x.at[1 - side_x], y)
        if side_y is not None:
            value = value + unpack(rim_y.at[1 - side_y], x)
        if side_x is not None and side_y is not None:
            value = value + rim_c[1 - side_x, 1 - side_y]
        inside = present(int(x == wx), int(y == wy))
        below = jnp.broadcast_to(value[CORNER - 1 : CORNER], value.shape)
        if inside is not None:
            value = jnp.where(inside, value, 0.0)
            below = jnp.where(inside, below, 1.0)
        fix = value / below
        above = jnp.where(lane == depth - 1, 0.0, pltpu.roll(fix, depth - 1, 1))
        fixes[x, y] = jnp.where(row < CORNER, fix, pltpu.roll(above, 4, 0))

    stacks = []
    for c in range(columns):
        x, y = c // wy, c % wy
        value = jnp.concatenate([fixes[x, y], fixes[x, y + 1], fixes[x + 1, y], fixes[x + 1, y + 1]], axis=0)
        upper = value.astype(jnp.bfloat16)
        lower = (value - upper.astype(jnp.float32)).astype(jnp.bfloat16)
        stacks.append(jnp.concatenate([upper, lower, upper], axis=0))
    terms_x.arrive()
    terms_y.arrive()
    for start in range(0, columns, 4):
        chosen = range(start, start + 4)
        lift = jnp.dot(
            spread[...], jnp.concatenate([stacks[c] for c in chosen], axis=1), preferred_element_type=jnp.float32
        )
        for index, c in enumerate(chosen):
            x, y = c // wy, c % wy
            for d in range(3):
                value = residual[d, c]
                if d == 0 and x == 0:
                    value = value + recv_x[y].astype(jnp.float32)
                if d == 1 and y == 0:
                    value = value + recv_y[x].astype(jnp.float32)
                piece = lift[d * faces : (d + 1) * faces, index * depth : (index + 1) * depth]
                out[d, c * faces : (c + 1) * faces] = value + keep[d, c : c + 1] * piece

    for exchange in first + rims + [terms_x, terms_y]:
        exchange.drain()

def deliver(faces, columns, values, out_hbm, rounded, store_sem):
    stores = []
    for d in range(3):
        for n in range(faces):
            rounded[d, n] = values[d, pl.ds(n, columns, stride=faces)].astype(jnp.bfloat16)
        stores.append(pltpu.make_async_copy(rounded.at[d], out_hbm.at[d], store_sem.at[d]))
        stores[-1].start()
    for store in stores:
        store.wait()


def local(count_x, count_y, traces, dirichlet, visc_class, viscosity, coarse_diag, solve_map, flux_map):
    faces, wx, wy, depth = traces.shape[1:]
    columns = wx * wy
    inner = solve_map.shape[0]
    operands = (
        traces.reshape(3, faces, columns, depth),
        dirichlet.reshape(3, columns, depth),
        visc_class.reshape(columns, depth),
        viscosity,
        coarse_diag.reshape(columns, depth),
        solve_map.T,
        flux_map,
        jnp.asarray(gather_table()),
        jnp.asarray(spread_table()),
    )
    anywhere = pl.BlockSpec(memory_space=pl.ANY)
    exchanges = 14
    rims_x, rims_y = wy // 2 + 1, wx // 2 + 1
    f32, bf16 = jnp.float32, jnp.bfloat16
    scratch = [
        pltpu.SMEM(a.shape, a.dtype) if index == 3 else pltpu.VMEM(a.shape, a.dtype) for index, a in enumerate(operands)
    ] + [
        pltpu.VMEM((3, faces * columns, depth), f32),
        pltpu.VMEM((inner, 6 * faces), bf16),
        pltpu.VMEM((3, columns, faces, depth), bf16),
        pltpu.VMEM((3, columns, depth), f32),
        pltpu.VMEM((6, columns, depth), f32),
        pltpu.VMEM((wy, faces, depth), bf16),
        pltpu.VMEM((wx, faces, depth), bf16),
        pltpu.VMEM((wx, faces, depth), bf16),
        pltpu.VMEM((wy, depth), f32),
        pltpu.VMEM((wx, depth), f32),
        pltpu.VMEM((wy, depth), f32),
        pltpu.VMEM((wx, depth), f32),
        pltpu.VMEM((3, columns, faces, depth), f32),
        pltpu.VMEM((2, columns, faces, depth), f32),
        pltpu.VMEM((wy, faces, depth), bf16),
        pltpu.VMEM((wx, faces, depth), bf16),
        pltpu.VMEM((wy, faces, depth), bf16),
        pltpu.VMEM((wx, faces, depth), bf16),
        pltpu.VMEM((2, rims_x, 8, depth), f32),
        pltpu.VMEM((2, rims_y, 8, depth), f32),
        pltpu.VMEM((2, 2, 8, depth), f32),
        pltpu.VMEM((2, rims_x, 8, depth), f32),
        pltpu.VMEM((2, rims_y, 8, depth), f32),
        pltpu.VMEM((2, 2, 8, depth), f32),
        pltpu.SemaphoreType.DMA((len(operands) + 2,)),
        pltpu.SemaphoreType.DMA((exchanges,)),
        pltpu.SemaphoreType.DMA((exchanges,)),
        pltpu.SemaphoreType.REGULAR,
    ]
    result = pl.pallas_call(
        functools.partial(kernel, count_x, count_y, wx, wy),
        out_shape=pltpu.VMEM((3, columns * faces, depth), f32),
        in_specs=[anywhere] * len(operands),
        out_specs=pl.BlockSpec(memory_space=pltpu.VMEM),
        scratch_shapes=scratch,
        compiler_params=pltpu.CompilerParams(collective_id=0, has_side_effects=True),
        name="apply",
    )(*operands)
    result = pl.pallas_call(
        functools.partial(deliver, faces, columns),
        out_shape=jax.ShapeDtypeStruct((3, faces, columns, depth), bf16),
        in_specs=[pl.BlockSpec(memory_space=pltpu.VMEM)],
        out_specs=anywhere,
        scratch_shapes=[pltpu.VMEM((3, faces, columns, depth), bf16), pltpu.SemaphoreType.DMA((3,))],
        compiler_params=pltpu.CompilerParams(vmem_limit_bytes=16 * 2**20),
        name="deliver",
    )(result)
    return result.reshape(3, faces, wx, wy, depth)


def solution(mesh):
    count_x, count_y = mesh.shape["gx"], mesh.shape["gy"]
    in_specs = (
        P(None, None, "gx", "gy", None),
        P(None, "gx", "gy", None),
        P("gx", "gy", None),
        P(),
        P("gx", "gy", None),
        P(),
        P(),
    )
    out_specs = P(None, None, "gx", "gy", None)
    return jax.shard_map(
        functools.partial(local, count_x, count_y), mesh=mesh, in_specs=in_specs, out_specs=out_specs, check_vma=False
    )
```

```python
import functools
import itertools
import math

import jax
import jax.numpy as jnp
import ml_dtypes
import numpy as np
from jax import lax
from jax.experimental import pallas as pl
from jax.experimental.pallas import tpu as pltpu
from jax.sharding import PartitionSpec as P

MESH = pl.DeviceIdType.MESH
penalty = 0.5
ORDER = (0, 2, 4, 5, 1, 3)
CORNER = 4


def corner_table():
    points = [-1.0, -math.sqrt(0.2), math.sqrt(0.2), 1.0]
    table = np.zeros((16, 4), np.float64)
    for a, b, p, q in itertools.product(range(4), range(4), range(2), range(2)):
        table[4 * a + b, 2 * p + q] = (1 + (2 * p - 1) * points[a]) * (1 + (2 * q - 1) * points[b]) / 4
    return table.astype(np.float32)


def in_two(table):
    high = table.astype(ml_dtypes.bfloat16)
    low = (table - high.astype(np.float32)).astype(ml_dtypes.bfloat16)
    return high, low


def gather_table():
    weights = corner_table()
    table = np.zeros((32, 6, 3, 16), np.float32)
    for dx, dy, dz, m in itertools.product(range(2), range(2), range(2), range(3)):
        row = 16 * dx + 8 * dy + CORNER * dz + m
        table[row, dx, m] = weights[:, 2 * dy + dz]
        table[row, 2 + dy, m] = weights[:, 2 * dx + dz]
        table[row, 4 + dz, m] = weights[:, 2 * dx + dy]
    return np.concatenate(in_two(table.reshape(32, 288)), axis=0)


def spread_table():
    weights = corner_table()
    table = np.zeros((3, 3, 16, 32), np.float32)
    for dx, dy, dz, m in itertools.product(range(2), range(2), range(2), range(3)):
        column = 16 * dx + 8 * dy + CORNER * dz + m
        if dx == 0:
            table[0, m, :, column] = weights[:, 2 * dy + dz]
        if dy == 0:
            table[1, m, :, column] = weights[:, 2 * dx + dz]
        if dz == 0:
            table[2, m, :, column] = weights[:, 2 * dx + dy]
    high, low = in_two(table.reshape(144, 32))
    return np.concatenate([high, high, low], axis=1)


def kernel(
    count_x, count_y, wx, wy,
    traces_hbm, dirichlet_hbm, class_hbm, viscosity_hbm, diag_hbm, solve_hbm, flux_hbm, gather_hbm, spread_hbm,
    out,
    traces, dirichlet, classes, viscosity, diag, solve_t, flux_map, gather, spread,
    staged, product, lifted, keep, scale, visc, halo_x, halo_y, first_y, flag_x, flag_y, keep_x, keep_y,
    residual, high, base, send_x, send_y, recv_x, recv_y, visc_x, visc_y, prev_x, prev_y, last_x, last_y, corner_x, corner_y,
    edge_x, edge_y, edge_c, rim_x, rim_y, rim_c,
    load_sem, send_sem, recv_sem, ready,
):
    columns, depth = wx * wy, traces.shape[3]
    faces = traces.shape[1]
    me_x, me_y = lax.axis_index("gx"), lax.axis_index("gy")
    there = {-1: (me_x > 0, me_y > 0), 0: (None, None), 1: (me_x < count_x - 1, me_y < count_y - 1)}

    def present(dx, dy):
        a, b = there[dx][0], there[dy][1]
        if a is None:
            return b
        return a if b is None else jnp.logical_and(a, b)

    def device(dx, dy):
        return {"gx": me_x + dx, "gy": me_y + dy}

    around = [(-1, -1), (1, -1), (-1, 1), (1, 1), (0, -1), (0, 1), (-1, 0), (1, 0)]
    barrier = pltpu.get_barrier_semaphore()
    total = 0
    for dx, dy in around[4:]:
        here = present(dx, dy)
        total = total + here.astype(jnp.int32)

        @pl.when(here)
        def _():
            pl.semaphore_signal(barrier, inc=1, device_id=device(dx, dy), device_id_type=MESH)

    loads = [
        (dirichlet_hbm, dirichlet), (traces_hbm.at[0], traces.at[0]), (traces_hbm.at[1], traces.at[1]),
        (traces_hbm.at[2], traces.at[2]), (viscosity_hbm, viscosity), (class_hbm, classes), (solve_hbm, solve_t),
        (flux_hbm, flux_map), (gather_hbm, gather), (diag_hbm, diag), (spread_hbm, spread),
    ]
    loads = [pltpu.make_async_copy(a, b, load_sem.at[i]) for i, (a, b) in enumerate(loads)]
    for load in loads:
        load.start()

    class Exchange:
        def __init__(self, slot, dx, dy, source, target):
            self.to, self.origin, self.target = present(dx, dy), present(-dx, -dy), target
            self.copy = pltpu.make_async_remote_copy(
                src_ref=source, dst_ref=target, send_sem=send_sem.at[slot], recv_sem=recv_sem.at[slot],
                device_id=device(dx, dy), device_id_type=MESH,
            )

        def clear(self):
            @pl.when(jnp.logical_not(self.origin))
            def _():
                self.target[...] = jnp.zeros(self.target.shape, self.target.dtype)

        def start(self):
            pl.when(self.to)(self.copy.start)

        def arrive(self):
            pl.when(self.origin)(self.copy.wait_recv)

        def drain(self):
            pl.when(self.to)(self.copy.wait_send)

    traces_x = Exchange(0, -1, 0, lifted.at[0, pl.ds(0, wy)], halo_x)
    flags_x = Exchange(1, -1, 0, flag_x, keep_x)
    traces_y = Exchange(2, 0, -1, first_y, halo_y)
    flags_y = Exchange(3, 0, -1, flag_y, keep_y)
    terms_x = Exchange(4, 1, 0, send_x, recv_x)
    terms_y = Exchange(5, 0, 1, send_y, recv_y)
    class_x = Exchange(6, 1, 0, visc_x, prev_x)
    class_y = Exchange(7, 0, 1, visc_y, prev_y)
    final_x = Exchange(8, 1, 0, last_x, corner_x)
    final_y = Exchange(9, 0, 1, last_y, corner_y)
    upward = [class_x, class_y, terms_x, terms_y]
    first = [flags_y, traces_y, flags_x, traces_x]
    rims = []
    for slot, (dx, dy) in enumerate(around):
        if dy == 0:
            source, target = edge_x.at[(dx + 1) // 2], rim_x.at[(dx + 1) // 2]
        elif dx == 0:
            source, target = edge_y.at[(dy + 1) // 2], rim_y.at[(dy + 1) // 2]
        else:
            source, target = edge_c.at[(dx + 1) // 2, (dy + 1) // 2], rim_c.at[(dx + 1) // 2, (dy + 1) // 2]
        rims.append(Exchange(10 + slot, dx, dy, source, target))
    for exchange in first + upward + [final_x, final_y] + rims:
        exchange.clear()

    lane = lax.broadcasted_iota(jnp.int32, (8, depth), 1)
    row = lax.broadcasted_iota(jnp.int32, (8, depth), 0)
    lane_faces = lax.broadcasted_iota(jnp.int32, (faces, depth), 1)

    def to_columns(d):
        for n in range(faces):
            staged[d, n * columns : (n + 1) * columns] = traces[d, n].astype(jnp.float32) * keep[d]
        for c in range(columns):
            lifted[d, c] = staged[d, pl.ds(c, faces, stride=columns)].astype(jnp.bfloat16)

    loads[0].wait()
    keep[...] = 1.0 - dirichlet[...].astype(jnp.float32)
    flag_x[...] = keep[0, :wy]
    for x in range(wx):
        flag_y[x : x + 1] = keep[1, x * wy : x * wy + 1]
    loads[1].wait()
    loads[2].wait()
    to_columns(1)
    to_columns(0)
    for x in range(wx):
        first_y[x] = lifted[1, x * wy]
    pl.semaphore_wait(barrier, total)
    for exchange in first:
        exchange.start()
    for dx in (-1, 1):

        @pl.when(present(dx, 0))
        def _():
            pl.semaphore_signal(ready, inc=1, device_id=device(dx, 0), device_id_type=MESH)

    loads[3].wait()
    to_columns(2)
    for load in loads[4:7]:
        load.wait()
    level_sum = jnp.zeros(classes.shape, jnp.float32)
    for level in range(viscosity.shape[0]):
        level_sum = level_sum + jnp.where(classes[...] == level, viscosity[level], 0.0)
    visc[...] = level_sum
    visc_x[...] = level_sum[columns - wy :]
    for x in range(wx):
        c = x * wy + wy - 1
        visc_y[x : x + 1] = level_sum[c : c + 1]
    class_x.start()
    class_y.start()
    lanes_c = lax.broadcasted_iota(jnp.int32, (columns, depth), 1)
    for d in range(3):
        scale[2 * d] = level_sum * keep[d]
    scale[5] = level_sum * jnp.where(lanes_c == depth - 1, 0.0, pltpu.roll(keep[2], depth - 1, 1))
    scale[1, : columns - wy] = level_sum[: columns - wy] * keep[0, wy:]
    scale[3, : columns - 1] = level_sum[: columns - 1] * keep[1, 1:]
    for load in loads[7:]:
        load.wait()
    turned = jnp.concatenate([solve_t[f * faces : (f + 1) * faces] for f in ORDER], axis=0).T
    product[...] = jnp.dot(flux_map[...], turned, preferred_element_type=jnp.float32).astype(jnp.bfloat16)

    known = 4 * faces
    late = known // 128 * 128
    filler = jnp.zeros((known - late, depth), jnp.bfloat16)
    nothing = jnp.zeros((faces, depth), jnp.bfloat16)

    def rows_of(face_slot):
        return slice(face_slot * faces, (face_slot + 1) * faces)

    def lanes_of(index):
        return slice(index * depth, (index + 1) * depth)

    def z_above(c):
        low_z = lifted[2, c].astype(jnp.float32)
        return jnp.where(lane_faces == depth - 1, 0.0, pltpu.roll(low_z, depth - 1, 1)).astype(jnp.bfloat16)

    def low_part(c):
        return [lifted[0, c], lifted[1, c], lifted[2, c], z_above(c)]

    def high_x(c):
        return lifted[0, c + wy] if c + wy < columns else halo_x[c % wy]

    def high_y(c):
        return lifted[1, c + 1] if c % wy + 1 < wy else halo_y[c // wy]

    def side_by_side(blocks):
        return jnp.concatenate([jnp.concatenate(block, axis=0) for block in blocks], axis=1)

    def late_dot(left_rows, blocks):
        return jnp.dot(
            product[left_rows, late:],
            side_by_side([[filler, a, b] for a, b in blocks]),
            preferred_element_type=jnp.float32,
        )

    corners = {}

    def finish(chosen, flux, faces_in):
        rounded = []
        for index, c in enumerate(chosen):
            x, y = c // wy, c % wy
            parts = []
            for face_slot in range(6):
                term = flux(index, face_slot)
                trace = faces_in[index][face_slot]
                if trace is not None:
                    term = term + penalty * trace.astype(jnp.float32)
                parts.append(term * scale[face_slot, c : c + 1])
            residual[0, c] = parts[0]
            residual[1, c] = parts[2]
            residual[2, c] = parts[4] + pltpu.roll(parts[5], 1, 1)
            cut = jnp.concatenate(parts, axis=0).astype(jnp.bfloat16)
            if x + 1 < wx:
                high[0, c] = parts[1]
            elif y + 1 == wy:
                last_x[...] = cut[rows_of(1)]
            if y + 1 < wy:
                high[1, c] = parts[3]
            elif x + 1 == wx:
                last_y[...] = cut[rows_of(3)]
            rounded.append(cut)
        both = jnp.dot(gather[...], jnp.concatenate(rounded, axis=1), preferred_element_type=jnp.float32)
        sums = both[:32] + both[32:]
        for index, c in enumerate(chosen):
            x, y = c // wy, c % wy
            for dx, dy in itertools.product(range(2), range(2)):
                part = sums[16 * dx + 8 * dy : 16 * dx + 8 * dy + 8, lanes_of(index)]
                key = (x + dx, y + dy)
                corners[key] = part if key not in corners else corners[key] + part

    def process(chosen):
        slots = [low_part(c) + [high_x(c), high_y(c)] for c in chosen]
        flux = jnp.dot(product[...], side_by_side(slots), preferred_element_type=jnp.float32)
        by_slot = [[block[ORDER.index(f)] for f in range(6)] for block in slots]
        finish(chosen, lambda index, f: flux[rows_of(f), lanes_of(index)], by_slot)

    def prepare(which, chosen):
        slots = [low_part(c) for c in chosen]
        flux = jnp.dot(product[:, :known], side_by_side(slots), preferred_element_type=jnp.float32)
        for index in range(len(chosen)):
            for f in range(6):
                term = flux[rows_of(f), lanes_of(index)]
                if f in ORDER[:4]:
                    term = term + penalty * slots[index][ORDER.index(f)].astype(jnp.float32)
                base[which, rows_of(f), lanes_of(index)] = term

    def complete(which, chosen):
        pairs = [[high_x(c), high_y(c)] for c in chosen]
        flux = late_dot(slice(None), pairs)
        by_slot = [[None, a, None, b, None, None] for a, b in pairs]
        finish(
            chosen,
            lambda index, f: base[which, rows_of(f), lanes_of(index)] + flux[rows_of(f), lanes_of(index)],
            by_slot,
        )

    inner = [c for c in range(columns) if c + wy < columns and c % wy + 1 < wy]
    need_x = [c for c in range(columns) if c + wy >= columns and c % wy + 1 < wy]
    need_y = [c for c in range(columns) if c % wy + 1 == wy]
    early = len(inner) // 4 * 4
    rim_a, rim_b = need_x + inner[early:], need_y
    prepare(1, rim_b)
    prepare(0, rim_a)
    beside_y = late_dot(rows_of(3), [[high_x(c), nothing] for c in need_y[: wx - 1]])
    for x, c in enumerate(need_y[: wx - 1]):
        value = base[1, rows_of(3), lanes_of(x)] + beside_y[:, lanes_of(x)]
        send_y[x] = (value * visc[c : c + 1]).astype(jnp.bfloat16)
    beside_x = late_dot(rows_of(1), [[nothing, high_y(c)] for c in need_x])
    for y, c in enumerate(need_x):
        value = base[0, rows_of(1), lanes_of(y)] + beside_x[:, lanes_of(y)]
        send_x[y] = (value * visc[c : c + 1]).astype(jnp.bfloat16)
    terms_y.start()
    terms_x.start()
    for start in range(0, early, 4):
        process(inner[start : start + 4])
    flags_x.arrive()
    traces_x.arrive()
    scale[1, columns - wy :] = visc[columns - wy :] * keep_x[...]
    complete(0, rim_a)
    flags_y.arrive()
    traces_y.arrive()
    for x in range(wx):
        c = x * wy + wy - 1
        scale[3, c : c + 1] = visc[c : c + 1] * keep_y[x : x + 1]
    complete(1, rim_b)

    vertices = list(itertools.product(range(wx + 1), range(wy + 1)))
    for x, y in vertices:
        value = corners[x, y]
        above = pltpu.roll(jnp.where(lane == depth - 1, 0.0, value), 1, 1)
        value = value + pltpu.roll(above, 4, 0)
        if x < wx and y < wy:
            corners[x, y] = jnp.where(row == CORNER - 1, diag[x * wy + y : x * wy + y + 1], value)
        else:
            corners[x, y] = jnp.where(row == CORNER - 1, 0.0, value)

    def pack(target, values):
        for i in range(0, len(values), 2):
            value = values[i]
            if i + 1 < len(values):
                value = jnp.where(row < CORNER, value, pltpu.roll(values[i + 1], 4, 0))
            target[i // 2] = value

    for side in range(2):
        for other in range(2):
            edge_c[side, other] = corners[side * wx, other * wy]
    for side in range(2):
        pack(edge_y.at[side], [corners[x, side * wy] for x in range(wx + 1)])
        pack(edge_x.at[side], [corners[side * wx, y] for y in range(wy + 1)])
    pl.semaphore_wait(ready, there[-1][0].astype(jnp.int32) + there[1][0].astype(jnp.int32))
    for exchange in rims:
        exchange.start()

    final_y.start()
    final_x.start()

    for c in range(columns):
        if c >= wy:
            residual[0, c] += high[0, c - wy]
        if c % wy:
            residual[1, c] += high[1, c - 1]
    for exchange in upward:
        exchange.arrive()
    mine_x = late_dot(rows_of(1), [[lifted[0, y], nothing] for y in range(wy - 1)])
    for y in range(wy - 1):
        value = mine_x[:, lanes_of(y)] + penalty * lifted[0, y].astype(jnp.float32)
        value = value * prev_x[y : y + 1] + recv_x[y].astype(jnp.float32)
        residual[0, y] += value * keep[0, y : y + 1]
    mine_y = late_dot(rows_of(3), [[nothing, lifted[1, x * wy]] for x in range(wx - 1)])
    for x in range(wx - 1):
        c = x * wy
        value = mine_y[:, lanes_of(x)] + penalty * lifted[1, c].astype(jnp.float32)
        value = value * prev_y[x : x + 1] + recv_y[x].astype(jnp.float32)
        residual[1, c] += value * keep[1, c : c + 1]

    fixes = {}

    def correct(value, inside):
        below = jnp.broadcast_to(value[CORNER - 1 : CORNER], value.shape)
        if inside is not None:
            value = jnp.where(inside, value, 0.0)
            below = jnp.where(inside, below, 1.0)
        fix = value / below
        above = jnp.where(lane == depth - 1, 0.0, pltpu.roll(fix, depth - 1, 1))
        return jnp.where(row < CORNER, fix, pltpu.roll(above, 4, 0))

    def emit(chosen):
        stacks = []
        for c in chosen:
            x, y = c // wy, c % wy
            value = jnp.concatenate([fixes[x, y], fixes[x, y + 1], fixes[x + 1, y], fixes[x + 1, y + 1]], axis=0)
            upper = value.astype(jnp.bfloat16)
            lower = (value - upper.astype(jnp.float32)).astype(jnp.bfloat16)
            stacks.append(jnp.concatenate([upper, lower, upper], axis=0))
        lift = jnp.dot(spread[...], jnp.concatenate(stacks, axis=1), preferred_element_type=jnp.float32)
        for index, c in enumerate(chosen):
            x, y = c // wy, c % wy
            for d in range(3):
                value = residual[d, c]
                if d == 0 and x == 0 and y + 1 == wy:
                    value = value + corner_x[...].astype(jnp.float32)
                if d == 1 and y == 0 and x + 1 == wx:
                    value = value + corner_y[...].astype(jnp.float32)
                piece = lift[d * faces : (d + 1) * faces, lanes_of(index)]
                out[d, c * faces : (c + 1) * faces] = value + keep[d, c : c + 1] * piece

    for x, y in vertices:
        if 0 < x < wx and 0 < y < wy:
            fixes[x, y] = correct(corners[x, y], None)
    middle = [c for c in range(columns) if 0 < c // wy < wx - 1 and 0 < c % wy < wy - 1]
    outer = [c for c in range(columns) if c not in middle]
    emit(middle)

    for exchange in rims:
        exchange.arrive()

    def unpack(source, index):
        value = source[index // 2]
        return pltpu.roll(value, 4, 0) if index % 2 else value

    for x, y in vertices:
        if (x, y) in fixes:
            continue
        value = corners[x, y]
        side_x = {0: 0, wx: 1}.get(x)
        side_y = {0: 0, wy: 1}.get(y)
        if side_x is not None:
            value = value + unpack(rim_x.at[1 - side_x], y)
        if side_y is not None:
            value = value + unpack(rim_y.at[1 - side_y], x)
        if side_x is not None and side_y is not None:
            value = value + rim_c[1 - side_x, 1 - side_y]
        fixes[x, y] = correct(value, present(int(x == wx), int(y == wy)))
    final_x.arrive()
    final_y.arrive()
    for start in range(0, len(outer), 4):
        emit(outer[start : start + 4])

    for exchange in first + upward + rims + [final_x, final_y]:
        exchange.drain()

def deliver(faces, columns, values, out_hbm, rounded, store_sem):
    stores = []
    for d in range(3):
        for n in range(faces):
            rounded[d, n] = values[d, pl.ds(n, columns, stride=faces)].astype(jnp.bfloat16)
        stores.append(pltpu.make_async_copy(rounded.at[d], out_hbm.at[d], store_sem.at[d]))
        stores[-1].start()
    for store in stores:
        store.wait()


def local(count_x, count_y, traces, dirichlet, visc_class, viscosity, coarse_diag, solve_map, flux_map):
    faces, wx, wy, depth = traces.shape[1:]
    columns = wx * wy
    operands = (
        traces.reshape(3, faces, columns, depth),
        dirichlet.reshape(3, columns, depth),
        visc_class.reshape(columns, depth),
        viscosity,
        coarse_diag.reshape(columns, depth),
        solve_map.T,
        flux_map,
        jnp.asarray(gather_table()),
        jnp.asarray(spread_table()),
    )
    anywhere = pl.BlockSpec(memory_space=pl.ANY)
    exchanges = 18
    rims_x, rims_y = wy // 2 + 1, wx // 2 + 1
    f32, bf16 = jnp.float32, jnp.bfloat16
    scratch = [
        pltpu.SMEM(a.shape, a.dtype) if index == 3 else pltpu.VMEM(a.shape, a.dtype) for index, a in enumerate(operands)
    ] + [
        pltpu.VMEM((3, faces * columns, depth), f32),
        pltpu.VMEM((6 * faces, 6 * faces), bf16),
        pltpu.VMEM((3, columns, faces, depth), bf16),
        pltpu.VMEM((3, columns, depth), f32),
        pltpu.VMEM((6, columns, depth), f32),
        pltpu.VMEM((columns, depth), f32),
        pltpu.VMEM((wy, faces, depth), bf16),
        pltpu.VMEM((wx, faces, depth), bf16),
        pltpu.VMEM((wx, faces, depth), bf16),
        pltpu.VMEM((wy, depth), f32),
        pltpu.VMEM((wx, depth), f32),
        pltpu.VMEM((wy, depth), f32),
        pltpu.VMEM((wx, depth), f32),
        pltpu.VMEM((3, columns, faces, depth), f32),
        pltpu.VMEM((2, columns, faces, depth), f32),
        pltpu.VMEM((2, 6 * faces, 4 * depth), f32),
        pltpu.VMEM((wy - 1, faces, depth), bf16),
        pltpu.VMEM((wx - 1, faces, depth), bf16),
        pltpu.VMEM((wy - 1, faces, depth), bf16),
        pltpu.VMEM((wx - 1, faces, depth), bf16),
        pltpu.VMEM((wy, depth), f32),
        pltpu.VMEM((wx, depth), f32),
        pltpu.VMEM((wy, depth), f32),
        pltpu.VMEM((wx, depth), f32),
        pltpu.VMEM((faces, depth), bf16),
        pltpu.VMEM((faces, depth), bf16),
        pltpu.VMEM((faces, depth), bf16),
        pltpu.VMEM((faces, depth), bf16),
        pltpu.VMEM((2, rims_x, 8, depth), f32),
        pltpu.VMEM((2, rims_y, 8, depth), f32),
        pltpu.VMEM((2, 2, 8, depth), f32),
        pltpu.VMEM((2, rims_x, 8, depth), f32),
        pltpu.VMEM((2, rims_y, 8, depth), f32),
        pltpu.VMEM((2, 2, 8, depth), f32),
        pltpu.SemaphoreType.DMA((len(operands) + 2,)),
        pltpu.SemaphoreType.DMA((exchanges,)),
        pltpu.SemaphoreType.DMA((exchanges,)),
        pltpu.SemaphoreType.REGULAR,
    ]
    result = pl.pallas_call(
        functools.partial(kernel, count_x, count_y, wx, wy),
        out_shape=pltpu.VMEM((3, columns * faces, depth), f32),
        in_specs=[anywhere] * len(operands),
        out_specs=pl.BlockSpec(memory_space=pltpu.VMEM),
        scratch_shapes=scratch,
        compiler_params=pltpu.CompilerParams(collective_id=0, has_side_effects=True),
        name="apply",
    )(*operands)
    result = pl.pallas_call(
        functools.partial(deliver, faces, columns),
        out_shape=jax.ShapeDtypeStruct((3, faces, columns, depth), bf16),
        in_specs=[pl.BlockSpec(memory_space=pltpu.VMEM)],
        out_specs=anywhere,
        scratch_shapes=[pltpu.VMEM((3, faces, columns, depth), bf16), pltpu.SemaphoreType.DMA((3,))],
        compiler_params=pltpu.CompilerParams(vmem_limit_bytes=16 * 2**20),
        name="deliver",
    )(result)
    return result.reshape(3, faces, wx, wy, depth)


def solution(mesh):
    count_x, count_y = mesh.shape["gx"], mesh.shape["gy"]
    in_specs = (
        P(None, None, "gx", "gy", None),
        P(None, "gx", "gy", None),
        P("gx", "gy", None),
        P(),
        P("gx", "gy", None),
        P(),
        P(),
    )
    out_specs = P(None, None, "gx", "gy", None)
    return jax.shard_map(
        functools.partial(local, count_x, count_y), mesh=mesh, in_specs=in_specs, out_specs=out_specs, check_vma=False
    )
```

```python
import functools
import itertools
import math

import jax
import jax.numpy as jnp
import ml_dtypes
import numpy as np
from jax import lax
from jax.experimental import pallas as pl
from jax.experimental.pallas import tpu as pltpu
from jax.sharding import PartitionSpec as P

MESH = pl.DeviceIdType.MESH
penalty = 0.5
ORDER = (0, 2, 4, 5, 1, 3)
CORNER = 4


def corner_table():
    points = [-1.0, -math.sqrt(0.2), math.sqrt(0.2), 1.0]
    table = np.zeros((16, 4), np.float64)
    for a, b, p, q in itertools.product(range(4), range(4), range(2), range(2)):
        table[4 * a + b, 2 * p + q] = (1 + (2 * p - 1) * points[a]) * (1 + (2 * q - 1) * points[b]) / 4
    return table.astype(np.float32)


def in_two(table):
    high = table.astype(ml_dtypes.bfloat16)
    low = (table - high.astype(np.float32)).astype(ml_dtypes.bfloat16)
    return high, low


def gather_table():
    weights = corner_table()
    table = np.zeros((32, 6, 3, 16), np.float32)
    for dx, dy, dz, m in itertools.product(range(2), range(2), range(2), range(3)):
        row = 16 * dx + 8 * dy + CORNER * dz + m
        table[row, dx, m] = weights[:, 2 * dy + dz]
        table[row, 2 + dy, m] = weights[:, 2 * dx + dz]
        table[row, 4 + dz, m] = weights[:, 2 * dx + dy]
    return np.concatenate(in_two(table.reshape(32, 288)), axis=0)


def spread_table():
    weights = corner_table()
    table = np.zeros((3, 3, 16, 32), np.float32)
    for dx, dy, dz, m in itertools.product(range(2), range(2), range(2), range(3)):
        column = 16 * dx + 8 * dy + CORNER * dz + m
        if dx == 0:
            table[0, m, :, column] = weights[:, 2 * dy + dz]
        if dy == 0:
            table[1, m, :, column] = weights[:, 2 * dx + dz]
        if dz == 0:
            table[2, m, :, column] = weights[:, 2 * dx + dy]
    high, low = in_two(table.reshape(144, 32))
    return np.concatenate([high, high, low], axis=1)


AROUND = [(-1, -1), (1, -1), (-1, 1), (1, 1), (0, -1), (0, 1), (-1, 0), (1, 0)]
BELOW = [(-1, -1), (0, -1), (-1, 0)]


def outgoing(wx, wy):
    top_x, top_y = (wx - 1) * wy, wy - 1
    last = wx * wy - 1
    low_x, low_y = [(0, y) for y in range(wy)], [(1, x * wy) for x in range(wx)]
    rim_x, rim_y = [top_x + y for y in range(wy)], [x * wy + top_y for x in range(wx)]
    return {
        (-1, 0): (low_x + [(1, 0)], [top_y], [(3, top_y)]),
        (0, -1): (low_y + [(0, 0)], [top_x], [(1, top_x)]),
        (1, 0): ([(1, top_x)], rim_x, [(1, c) for c in rim_x] + [(3, last)]),
        (0, 1): ([(0, top_y)], rim_y, [(3, c) for c in rim_y] + [(1, last)]),
        (-1, -1): ([(1, 0), (0, 0)], [], []),
        (1, 1): ([], [last], [(1, last), (3, last)]),
        (1, -1): ([(1, top_x)], [top_x], [(1, top_x)]),
        (-1, 1): ([(0, top_y)], [top_y], [(3, top_y)]),
    }


def row_count(faces_out, hexes):
    return -(-(len(faces_out) + 6 * len(hexes)) // 8) * 8


def kernel(
    count_x, count_y, wx, wy,
    traces_hbm, dirichlet_hbm, class_hbm, viscosity_hbm, diag_hbm, solve_hbm, flux_hbm, gather_hbm, spread_hbm,
    out,
    traces, dirichlet, classes, viscosity, diag, solve_t, flux_map, gather, spread,
    staged, product, lifted, keep, scale, visc, residual, high, edge_x, edge_y, edge_c, rim_x, rim_y, rim_c,
    load_sem, send_sem, recv_sem, ready,
    *packs,
):
    columns, depth = wx * wy, traces.shape[3]
    faces = traces.shape[1]
    me_x, me_y = lax.axis_index("gx"), lax.axis_index("gy")
    there = {-1: (me_x > 0, me_y > 0), 0: (None, None), 1: (me_x < count_x - 1, me_y < count_y - 1)}

    def present(dx, dy):
        a, b = there[dx][0], there[dy][1]
        if a is None:
            return b
        return a if b is None else jnp.logical_and(a, b)

    def device(dx, dy):
        return {"gx": me_x + dx, "gy": me_y + dy}

    plan = outgoing(wx, wy)
    barrier = pltpu.get_barrier_semaphore()
    total = 0
    for dx, dy in BELOW:
        total = total + present(dx, dy).astype(jnp.int32)

        @pl.when(present(-dx, -dy))
        def _():
            pl.semaphore_signal(barrier, inc=1, device_id=device(-dx, -dy), device_id_type=MESH)

    loads = [
        (dirichlet_hbm, dirichlet), (traces_hbm.at[0], traces.at[0]), (traces_hbm.at[1], traces.at[1]),
        (viscosity_hbm, viscosity), (class_hbm, classes), (traces_hbm.at[2], traces.at[2]), (solve_hbm, solve_t),
        (flux_hbm, flux_map), (gather_hbm, gather), (diag_hbm, diag), (spread_hbm, spread),
    ]
    loads = [pltpu.make_async_copy(a, b, load_sem.at[i]) for i, (a, b) in enumerate(loads)]
    for load in loads:
        load.start()

    class Exchange:
        def __init__(self, slot, dx, dy, source, target):
            self.to, self.origin, self.target = present(dx, dy), present(-dx, -dy), target
            self.copy = pltpu.make_async_remote_copy(
                src_ref=source, dst_ref=target, send_sem=send_sem.at[slot], recv_sem=recv_sem.at[slot],
                device_id=device(dx, dy), device_id_type=MESH,
            )

        def clear(self):
            @pl.when(jnp.logical_not(self.origin))
            def _():
                self.target[...] = jnp.zeros(self.target.shape, self.target.dtype)

        def start(self):
            pl.when(self.to)(self.copy.start)

        def arrive(self):
            pl.when(self.origin)(self.copy.wait_recv)

        def drain(self):
            pl.when(self.to)(self.copy.wait_send)

    packs = list(packs)
    sent, got, exchanges = {}, {}, {}
    for direction in AROUND:
        for kind, present_here in zip(("trace", "rows", "term"), plan[direction]):
            if kind == "rows":
                present_here = plan[direction][0] + plan[direction][1]
            if present_here:
                sent[kind, direction] = packs.pop(0)
                target = packs.pop(0)
                got[kind, (-direction[0], -direction[1])] = target
                exchanges[kind, direction] = Exchange(len(exchanges), *direction, sent[kind, direction], target)
    for dx, dy in AROUND:
        if dy == 0:
            source, target = edge_x.at[(dx + 1) // 2], rim_x.at[(dx + 1) // 2]
        elif dx == 0:
            source, target = edge_y.at[(dy + 1) // 2], rim_y.at[(dy + 1) // 2]
        else:
            source, target = edge_c.at[(dx + 1) // 2, (dy + 1) // 2], rim_c.at[(dx + 1) // 2, (dy + 1) // 2]
        exchanges["rim", (dx, dy)] = Exchange(len(exchanges), dx, dy, source, target)
    for exchange in exchanges.values():
        exchange.clear()

    def start(kinds, directions):
        for kind in kinds:
            for direction in directions:
                if (kind, direction) in exchanges:
                    exchanges[kind, direction].start()

    def arrive(kind):
        for (name, _), exchange in exchanges.items():
            if name == kind:
                exchange.arrive()

    lane = lax.broadcasted_iota(jnp.int32, (8, depth), 1)
    row = lax.broadcasted_iota(jnp.int32, (8, depth), 0)
    lane_faces = lax.broadcasted_iota(jnp.int32, (faces, depth), 1)

    def to_columns(d):
        for n in range(faces):
            staged[d, n * columns : (n + 1) * columns] = traces[d, n].astype(jnp.float32) * keep[d]
        for c in range(columns):
            lifted[d, c] = staged[d, pl.ds(c, faces, stride=columns)].astype(jnp.bfloat16)

    loads[0].wait()
    keep[...] = 1.0 - dirichlet[...].astype(jnp.float32)
    for load in loads[3:5]:
        load.wait()
    level_sum = jnp.zeros(classes.shape, jnp.float32)
    for level in range(viscosity.shape[0]):
        level_sum = level_sum + jnp.where(classes[...] == level, viscosity[level], 0.0)
    visc[...] = level_sum
    lanes_c = lax.broadcasted_iota(jnp.int32, (columns, depth), 1)
    for d in range(3):
        scale[2 * d] = level_sum * keep[d]
    scale[5] = level_sum * jnp.where(lanes_c == depth - 1, 0.0, pltpu.roll(keep[2], depth - 1, 1))
    scale[1, columns - wy :] = level_sum[columns - wy :]
    scale[1, : columns - wy] = level_sum[: columns - wy] * keep[0, wy:]
    scale[3, : columns - 1] = level_sum[: columns - 1] * keep[1, 1:]
    for x in range(wx):
        c = x * wy + wy - 1
        scale[3, c : c + 1] = visc[c : c + 1]
    for direction, (faces_out, hexes, _) in plan.items():
        target = sent["rows", direction]
        for r, (d, c) in enumerate(faces_out):
            target[r : r + 1] = keep[d, c : c + 1]
        for h, c in enumerate(hexes):
            for f in range(6):
                r = len(faces_out) + 6 * h + f
                target[r : r + 1] = scale[f, c : c + 1]
    loads[1].wait()
    loads[2].wait()
    to_columns(1)
    to_columns(0)
    for direction, (faces_out, _, _) in plan.items():
        for i, (d, c) in enumerate(faces_out):
            sent["trace", direction][i] = lifted[d, c]

    pl.when(total > 0)(lambda: pl.semaphore_wait(barrier, total))
    for slot, (dx, dy) in enumerate(BELOW):

        @pl.when(present(dx, dy))
        def _():
            pl.semaphore_signal(ready.at[slot], inc=1, device_id=device(dx, dy), device_id_type=MESH)

    start(["trace", "rows"], BELOW)
    loads[5].wait()
    to_columns(2)
    for load in loads[6:]:
        load.wait()
    turned = jnp.concatenate([solve_t[f * faces : (f + 1) * faces] for f in ORDER], axis=0).T
    product[...] = jnp.dot(flux_map[...], turned, preferred_element_type=jnp.float32).astype(jnp.bfloat16)

    known = 4 * faces
    late = known // 128 * 128
    filler = jnp.zeros((known - late, depth), jnp.bfloat16)
    nothing = jnp.zeros((faces, depth), jnp.bfloat16)

    def rows_of(face_slot):
        return slice(face_slot * faces, (face_slot + 1) * faces)

    def lanes_of(index):
        return slice(index * depth, (index + 1) * depth)

    def z_above(c):
        low_z = lifted[2, c].astype(jnp.float32)
        return jnp.where(lane_faces == depth - 1, 0.0, pltpu.roll(low_z, depth - 1, 1)).astype(jnp.bfloat16)

    def low_part(c):
        return [lifted[0, c], lifted[1, c], lifted[2, c], z_above(c)]

    def high_x(c):
        return lifted[0, c + wy] if c + wy < columns else nothing

    def high_y(c):
        return lifted[1, c + 1] if c % wy + 1 < wy else nothing

    def side_by_side(blocks):
        return jnp.concatenate([jnp.concatenate(block, axis=0) for block in blocks], axis=1)

    def late_dot(left_rows, blocks):
        return jnp.dot(
            product[left_rows, late:],
            side_by_side([[filler, a, b] for a, b in blocks]),
            preferred_element_type=jnp.float32,
        )

    corners = {}

    def gathered(into, chosen, rounded):
        both = jnp.dot(gather[...], jnp.concatenate(rounded, axis=1), preferred_element_type=jnp.float32)
        sums = both[:32] + both[32:]
        for index, (x, y) in enumerate(chosen):
            for dx, dy in itertools.product(range(2), range(2)):
                key = (x + dx, y + dy)
                if 0 <= key[0] <= wx and 0 <= key[1] <= wy:
                    part = sums[16 * dx + 8 * dy : 16 * dx + 8 * dy + 8, lanes_of(index)]
                    into[key] = part if key not in into else into[key] + part

    def process(chosen):
        slots = [low_part(c) + [high_x(c), high_y(c)] for c in chosen]
        flux = jnp.dot(product[...], side_by_side(slots), preferred_element_type=jnp.float32)
        rounded = []
        for index, c in enumerate(chosen):
            x, y = c // wy, c % wy
            parts = []
            for f in range(6):
                term = flux[rows_of(f), lanes_of(index)]
                term = term + penalty * slots[index][ORDER.index(f)].astype(jnp.float32)
                parts.append(term * scale[f, c : c + 1])
            residual[0, c] = parts[0]
            residual[1, c] = parts[2]
            residual[2, c] = parts[4] + pltpu.roll(parts[5], 1, 1)
            for f, outer_face in ((1, x + 1 == wx), (3, y + 1 == wy)):
                if not outer_face:
                    high[f // 2, c] = parts[f]
                    continue
                sealed = parts[f].astype(jnp.bfloat16)
                for direction in AROUND:
                    if (f, c) in plan[direction][2]:
                        sent["term", direction][plan[direction][2].index((f, c))] = sealed
                parts[f] = jnp.zeros_like(parts[f])
            rounded.append(jnp.concatenate(parts, axis=0).astype(jnp.bfloat16))
        gathered(corners, [(c // wy, c % wy) for c in chosen], rounded)

    def foreign(origin, d, c):
        i = plan[-origin[0], -origin[1]][0].index((d, c))
        return got["trace", origin][i], got["rows", origin][i : i + 1]

    def foreign_scale(origin, c):
        faces_in, hexes, _ = plan[-origin[0], -origin[1]]
        r = len(faces_in) + 6 * hexes.index(c)
        return [got["rows", origin][r + f : r + f + 1] for f in range(6)]

    def foreign_term(origin, f, c):
        return got["term", origin][plan[-origin[0], -origin[1]][2].index((f, c))]

    def own_term(f, c):
        direction = (1, 0) if f == 1 else (0, 1)
        return sent["term", direction][plan[direction][2].index((f, c))]

    top_x, top_y, last = (wx - 1) * wy, wy - 1, columns - 1

    def late_hexes():
        def mine(c):
            return lambda: [scale[f, c : c + 1] for f in range(6)]

        for y in range(wy):
            c = top_x + y
            second = (foreign((0, 1), 1, top_x), own_term(3, c)) if y == top_y else None
            yield (wx - 1, y), (foreign((1, 0), 0, y), own_term(1, c)), second, mine(c)
        for x in range(wx - 1):
            c = x * wy + top_y
            yield (x, top_y), None, (foreign((0, 1), 1, x * wy), own_term(3, c)), mine(c)
        for y in range(wy):
            c = top_x + y
            second = (foreign((-1, 1), 1, top_x), foreign_term((-1, 0), 3, c)) if y == top_y else None
            first = ((lifted[0, y], keep[0, y : y + 1]), foreign_term((-1, 0), 1, c))
            yield (-1, y), first, second, lambda c=c: foreign_scale((-1, 0), c)
        for x in range(wx):
            c = x * wy + top_y
            first = (foreign((1, -1), 0, top_y), foreign_term((0, -1), 1, c)) if x == wx - 1 else None
            second = ((lifted[1, x * wy], keep[1, x * wy : x * wy + 1]), foreign_term((0, -1), 3, c))
            yield (x, -1), first, second, lambda c=c: foreign_scale((0, -1), c)
        yield (
            (-1, -1),
            (foreign((0, -1), 0, top_y), foreign_term((-1, -1), 1, last)),
            (foreign((-1, 0), 1, top_x), foreign_term((-1, -1), 3, last)),
            lambda: foreign_scale((-1, -1), last),
        )
        first = (foreign((0, 1), 0, 0), foreign_term((-1, 1), 1, top_x))
        yield (-1, wy), first, None, lambda: foreign_scale((-1, 1), top_x)
        second = (foreign((1, 0), 1, 0), foreign_term((1, -1), 3, top_y))
        yield (wx, -1), None, second, lambda: foreign_scale((1, -1), top_y)
        second = (foreign((1, 1), 1, 0), foreign_term((1, 0), 3, top_y))
        yield (wx, wy - 1), None, second, lambda: foreign_scale((1, 0), top_y)
        first = (foreign((1, 1), 0, 0), foreign_term((0, 1), 1, top_x))
        yield (wx - 1, wy), first, None, lambda: foreign_scale((0, 1), top_x)

    def act(chosen):
        pairs = [[item[0][0] if item else nothing for item in (first, second)] for _, first, second, _ in chosen]
        flux = late_dot(slice(None), pairs)
        rounded = []
        for index, ((x, y), first, second, scales) in enumerate(chosen):
            scales = scales()
            parts = []
            for f in range(6):
                value = flux[rows_of(f), lanes_of(index)]
                item = {1: first, 3: second}.get(f)
                if item is not None:
                    (trace, flags), term = item
                    value = value + penalty * trace.astype(jnp.float32)
                    value = (value * scales[f] + term.astype(jnp.float32)) * flags
                else:
                    value = value * scales[f]
                parts.append(value)
            if 0 <= x < wx and 0 <= y < wy:
                c = x * wy + y
                residual[0, c] += parts[0]
                residual[1, c] += parts[2]
                residual[2, c] += parts[4] + pltpu.roll(parts[5], 1, 1)
                if x + 1 < wx:
                    residual[0, c + wy] += parts[1]
                if y + 1 < wy:
                    residual[1, c + 1] += parts[3]
            elif x == -1 and 0 <= y < wy:
                residual[0, y] += parts[1]
            elif y == -1 and 0 <= x < wx:
                residual[1, x * wy] += parts[3]
            rounded.append(jnp.concatenate(parts, axis=0).astype(jnp.bfloat16))
        gathered(extra, [item[0] for item in chosen], rounded)

    order = [c for c in range(columns) if c >= top_x] + [c for c in range(columns) if c < top_x and c % wy == top_y]
    order += [c for c in range(columns) if c not in order]
    for start_at in range(0, columns, 4):
        process(order[start_at : start_at + 4])
        if start_at + 4 == 8:
            start(["term"], BELOW)

    vertices = list(itertools.product(range(wx + 1), range(wy + 1)))

    def settle(value):
        above = pltpu.roll(jnp.where(lane == depth - 1, 0.0, value), 1, 1)
        return value + pltpu.roll(above, 4, 0)

    for x, y in vertices:
        value = settle(corners[x, y])
        if x < wx and y < wy:
            corners[x, y] = jnp.where(row == CORNER - 1, diag[x * wy + y : x * wy + y + 1], value)
        else:
            corners[x, y] = jnp.where(row == CORNER - 1, 0.0, value)

    def pack(target, values):
        for i in range(0, len(values), 2):
            value = values[i]
            if i + 1 < len(values):
                value = jnp.where(row < CORNER, value, pltpu.roll(values[i + 1], 4, 0))
            target[i // 2] = value

    for side in range(2):
        for other in range(2):
            edge_c[side, other] = corners[side * wx, other * wy]
    for side in range(2):
        pack(edge_y.at[side], [corners[x, side * wy] for x in range(wx + 1)])
        pack(edge_x.at[side], [corners[side * wx, y] for y in range(wy + 1)])
    start(["rim"], BELOW)
    for slot, directions in ((2, [(1, -1), (1, 0)]), (1, [(-1, 1), (0, 1)]), (0, [(1, 1)])):
        dx, dy = BELOW[slot]
        pl.when(present(-dx, -dy))(lambda: pl.semaphore_wait(ready.at[slot], 1))
        start(["rim", "trace", "rows", "term"], directions)

    for c in range(columns):
        if c >= wy:
            residual[0, c] += high[0, c - wy]
        if c % wy:
            residual[1, c] += high[1, c - 1]
    extra = {}
    arrive("trace")
    arrive("rows")
    arrive("term")
    waiting = list(late_hexes())
    for start_at in range(0, len(waiting), 4):
        act(waiting[start_at : start_at + 4])
    for x, y in vertices:
        if (x, y) in extra:
            corners[x, y] = corners[x, y] + jnp.where(row == CORNER - 1, 0.0, settle(extra[x, y]))

    fixes = {}

    def correct(value, inside):
        below = jnp.broadcast_to(value[CORNER - 1 : CORNER], value.shape)
        if inside is not None:
            value = jnp.where(inside, value, 0.0)
            below = jnp.where(inside, below, 1.0)
        fix = value / below
        above = jnp.where(lane == depth - 1, 0.0, pltpu.roll(fix, depth - 1, 1))
        return jnp.where(row < CORNER, fix, pltpu.roll(above, 4, 0))

    def emit(chosen):
        stacks = []
        for c in chosen:
            x, y = c // wy, c % wy
            value = jnp.concatenate([fixes[x, y], fixes[x, y + 1], fixes[x + 1, y], fixes[x + 1, y + 1]], axis=0)
            upper = value.astype(jnp.bfloat16)
            lower = (value - upper.astype(jnp.float32)).astype(jnp.bfloat16)
            stacks.append(jnp.concatenate([upper, lower, upper], axis=0))
        lift = jnp.dot(spread[...], jnp.concatenate(stacks, axis=1), preferred_element_type=jnp.float32)
        for index, c in enumerate(chosen):
            x, y = c // wy, c % wy
            for d in range(3):
                piece = lift[d * faces : (d + 1) * faces, lanes_of(index)]
                out[d, c * faces : (c + 1) * faces] = residual[d, c] + keep[d, c : c + 1] * piece

    for x, y in vertices:
        if 0 < x < wx and 0 < y < wy:
            fixes[x, y] = correct(corners[x, y], None)
    middle = [c for c in range(columns) if 0 < c // wy < wx - 1 and 0 < c % wy < wy - 1]
    outer = [c for c in range(columns) if c not in middle]
    emit(middle)
    arrive("rim")

    def unpack(source, index):
        value = source[index // 2]
        return pltpu.roll(value, 4, 0) if index % 2 else value

    for x, y in vertices:
        if (x, y) in fixes:
            continue
        value = corners[x, y]
        side_x = {0: 0, wx: 1}.get(x)
        side_y = {0: 0, wy: 1}.get(y)
        if side_x is not None:
            value = value + unpack(rim_x.at[1 - side_x], y)
        if side_y is not None:
            value = value + unpack(rim_y.at[1 - side_y], x)
        if side_x is not None and side_y is not None:
            value = value + rim_c[1 - side_x, 1 - side_y]
        fixes[x, y] = correct(value, present(int(x == wx), int(y == wy)))
    for first_one in range(0, len(outer), 4):
        emit(outer[first_one : first_one + 4])

    for exchange in exchanges.values():
        exchange.drain()


def deliver(faces, columns, values, out_hbm, rounded, store_sem):
    stores = []
    for d in range(3):
        for n in range(faces):
            rounded[d, n] = values[d, pl.ds(n, columns, stride=faces)].astype(jnp.bfloat16)
        stores.append(pltpu.make_async_copy(rounded.at[d], out_hbm.at[d], store_sem.at[d]))
        stores[-1].start()
    for store in stores:
        store.wait()


def local(count_x, count_y, traces, dirichlet, visc_class, viscosity, coarse_diag, solve_map, flux_map):
    faces, wx, wy, depth = traces.shape[1:]
    columns = wx * wy
    operands = (
        traces.reshape(3, faces, columns, depth),
        dirichlet.reshape(3, columns, depth),
        visc_class.reshape(columns, depth),
        viscosity,
        coarse_diag.reshape(columns, depth),
        solve_map.T,
        flux_map,
        jnp.asarray(gather_table()),
        jnp.asarray(spread_table()),
    )
    anywhere = pl.BlockSpec(memory_space=pl.ANY)
    plan = outgoing(wx, wy)
    packs = []
    for direction in AROUND:
        faces_out, hexes, terms = plan[direction]
        shapes = [((len(faces_out), faces, depth), jnp.bfloat16)] if faces_out else []
        shapes.append(((row_count(faces_out, hexes), depth), jnp.float32))
        shapes += [((len(terms), faces, depth), jnp.bfloat16)] if terms else []
        packs += [pltpu.VMEM(*shape) for shape in shapes for _ in range(2)]
    exchanges = len(packs) // 2 + len(AROUND)
    rims_x, rims_y = wy // 2 + 1, wx // 2 + 1
    f32, bf16 = jnp.float32, jnp.bfloat16
    scratch = [
        pltpu.SMEM(a.shape, a.dtype) if index == 3 else pltpu.VMEM(a.shape, a.dtype) for index, a in enumerate(operands)
    ] + [
        pltpu.VMEM((3, faces * columns, depth), f32),
        pltpu.VMEM((6 * faces, 6 * faces), bf16),
        pltpu.VMEM((3, columns, faces, depth), bf16),
        pltpu.VMEM((3, columns, depth), f32),
        pltpu.VMEM((6, columns, depth), f32),
        pltpu.VMEM((columns, depth), f32),
        pltpu.VMEM((3, columns, faces, depth), f32),
        pltpu.VMEM((2, columns, faces, depth), f32),
        pltpu.VMEM((2, rims_x, 8, depth), f32),
        pltpu.VMEM((2, rims_y, 8, depth), f32),
        pltpu.VMEM((2, 2, 8, depth), f32),
        pltpu.VMEM((2, rims_x, 8, depth), f32),
        pltpu.VMEM((2, rims_y, 8, depth), f32),
        pltpu.VMEM((2, 2, 8, depth), f32),
        pltpu.SemaphoreType.DMA((len(operands) + 2,)),
        pltpu.SemaphoreType.DMA((exchanges,)),
        pltpu.SemaphoreType.DMA((exchanges,)),
        pltpu.SemaphoreType.REGULAR((3,)),
    ] + packs
    result = pl.pallas_call(
        functools.partial(kernel, count_x, count_y, wx, wy),
        out_shape=pltpu.VMEM((3, columns * faces, depth), f32),
        in_specs=[anywhere] * len(operands),
        out_specs=pl.BlockSpec(memory_space=pltpu.VMEM),
        scratch_shapes=scratch,
        compiler_params=pltpu.CompilerParams(collective_id=0, has_side_effects=True),
        name="apply",
    )(*operands)
    result = pl.pallas_call(
        functools.partial(deliver, faces, columns),
        out_shape=jax.ShapeDtypeStruct((3, faces, columns, depth), bf16),
        in_specs=[pl.BlockSpec(memory_space=pltpu.VMEM)],
        out_specs=anywhere,
        scratch_shapes=[pltpu.VMEM((3, faces, columns, depth), bf16), pltpu.SemaphoreType.DMA((3,))],
        compiler_params=pltpu.CompilerParams(vmem_limit_bytes=16 * 2**20),
        name="deliver",
    )(result)
    return result.reshape(3, faces, wx, wy, depth)


def solution(mesh):
    count_x, count_y = mesh.shape["gx"], mesh.shape["gy"]
    in_specs = (
        P(None, None, "gx", "gy", None),
        P(None, "gx", "gy", None),
        P("gx", "gy", None),
        P(),
        P("gx", "gy", None),
        P(),
        P(),
    )
    out_specs = P(None, None, "gx", "gy", None)
    return jax.shard_map(
        functools.partial(local, count_x, count_y), mesh=mesh, in_specs=in_specs, out_specs=out_specs, check_vma=False
    )
```

```python
import functools
import itertools
import math

import jax
import jax.numpy as jnp
import ml_dtypes
import numpy as np
from jax import lax
from jax.experimental import pallas as pl
from jax.experimental.pallas import tpu as pltpu
from jax.sharding import PartitionSpec as P

MESH = pl.DeviceIdType.MESH
penalty = 0.5
ORDER = (0, 2, 4, 5, 1, 3)
CORNER = 4


def corner_table():
    points = [-1.0, -math.sqrt(0.2), math.sqrt(0.2), 1.0]
    table = np.zeros((16, 4), np.float64)
    for a, b, p, q in itertools.product(range(4), range(4), range(2), range(2)):
        table[4 * a + b, 2 * p + q] = (1 + (2 * p - 1) * points[a]) * (1 + (2 * q - 1) * points[b]) / 4
    return table.astype(np.float32)


def in_two(table):
    high = table.astype(ml_dtypes.bfloat16)
    low = (table - high.astype(np.float32)).astype(ml_dtypes.bfloat16)
    return high, low


def gather_table():
    weights = corner_table()
    table = np.zeros((32, 6, 3, 16), np.float32)
    for dx, dy, dz, m in itertools.product(range(2), range(2), range(2), range(3)):
        row = 16 * dx + 8 * dy + CORNER * dz + m
        table[row, dx, m] = weights[:, 2 * dy + dz]
        table[row, 2 + dy, m] = weights[:, 2 * dx + dz]
        table[row, 4 + dz, m] = weights[:, 2 * dx + dy]
    return np.concatenate(in_two(table.reshape(32, 288)), axis=0)


def spread_table():
    weights = corner_table()
    table = np.zeros((3, 3, 16, 32), np.float32)
    for dx, dy, dz, m in itertools.product(range(2), range(2), range(2), range(3)):
        column = 16 * dx + 8 * dy + CORNER * dz + m
        if dx == 0:
            table[0, m, :, column] = weights[:, 2 * dy + dz]
        if dy == 0:
            table[1, m, :, column] = weights[:, 2 * dx + dz]
        if dz == 0:
            table[2, m, :, column] = weights[:, 2 * dx + dy]
    high, low = in_two(table.reshape(144, 32))
    return np.concatenate([high, high, low], axis=1)


def kernel(
    count_x, count_y, wx, wy,
    traces_hbm, dirichlet_hbm, class_hbm, viscosity_hbm, diag_hbm, solve_hbm, flux_hbm, gather_hbm, spread_hbm,
    out,
    traces, dirichlet, classes, viscosity, diag, solve_t, flux_map, gather, spread,
    staged, product, lifted, keep, scale, visc, halo_x, halo_y, first_y, flag_x, flag_y, keep_x, keep_y,
    residual, high, base, send_x, send_y, recv_x, recv_y, visc_x, visc_y, prev_x, prev_y, last_x, last_y, corner_x, corner_y,
    edge_x, edge_y, edge_c, rim_x, rim_y, rim_c,
    load_sem, send_sem, recv_sem, ready,
):
    columns, depth = wx * wy, traces.shape[3]
    faces = traces.shape[1]
    me_x, me_y = lax.axis_index("gx"), lax.axis_index("gy")
    there = {-1: (me_x > 0, me_y > 0), 0: (None, None), 1: (me_x < count_x - 1, me_y < count_y - 1)}

    def present(dx, dy):
        a, b = there[dx][0], there[dy][1]
        if a is None:
            return b
        return a if b is None else jnp.logical_and(a, b)

    def device(dx, dy):
        return {"gx": me_x + dx, "gy": me_y + dy}

    around = [(-1, -1), (0, -1), (-1, 0), (1, -1), (1, 0), (-1, 1), (0, 1), (1, 1)]
    names = ("dirichlet", "y", "x", "z", "viscosity", "classes", "solve", "flux", "gather", "diag", "spread")
    pairs = [
        (dirichlet_hbm, dirichlet), (traces_hbm.at[1], traces.at[1]), (traces_hbm.at[0], traces.at[0]),
        (traces_hbm.at[2], traces.at[2]), (viscosity_hbm, viscosity), (class_hbm, classes), (solve_hbm, solve_t),
        (flux_hbm, flux_map), (gather_hbm, gather), (diag_hbm, diag), (spread_hbm, spread),
    ]
    loads = {name: pltpu.make_async_copy(a, b, load_sem.at[i]) for i, (name, (a, b)) in enumerate(zip(names, pairs))}
    for load in loads.values():
        load.start()

    barrier = pltpu.get_barrier_semaphore()
    total = 0
    below = [None, (0, -1), (-1, 0)]
    for dx, dy in below[1:]:
        total = total + present(dx, dy).astype(jnp.int32)

        @pl.when(present(-dx, -dy))
        def _():
            pl.semaphore_signal(barrier, inc=1, device_id=device(-dx, -dy), device_id_type=MESH)

    class Exchange:
        def __init__(self, slot, dx, dy, source, target):
            self.to, self.origin, self.target = present(dx, dy), present(-dx, -dy), target
            self.copy = pltpu.make_async_remote_copy(
                src_ref=source, dst_ref=target, send_sem=send_sem.at[slot], recv_sem=recv_sem.at[slot],
                device_id=device(dx, dy), device_id_type=MESH,
            )

        def clear(self):
            @pl.when(jnp.logical_not(self.origin))
            def _():
                self.target[...] = jnp.zeros(self.target.shape, self.target.dtype)

        def start(self):
            pl.when(self.to)(self.copy.start)

        def arrive(self):
            pl.when(self.origin)(self.copy.wait_recv)

        def drain(self):
            pl.when(self.to)(self.copy.wait_send)

    traces_x = Exchange(0, -1, 0, lifted.at[0, pl.ds(0, wy)], halo_x)
    flags_x = Exchange(1, -1, 0, flag_x, keep_x)
    traces_y = Exchange(2, 0, -1, first_y, halo_y)
    flags_y = Exchange(3, 0, -1, flag_y, keep_y)
    terms_x = Exchange(4, 1, 0, send_x, recv_x)
    terms_y = Exchange(5, 0, 1, send_y, recv_y)
    class_x = Exchange(6, 1, 0, visc_x, prev_x)
    class_y = Exchange(7, 0, 1, visc_y, prev_y)
    final_x = Exchange(8, 1, 0, last_x, corner_x)
    final_y = Exchange(9, 0, 1, last_y, corner_y)
    upward = [class_x, class_y, terms_x, terms_y]
    first = [flags_y, traces_y, flags_x, traces_x]
    rims = []
    for slot, (dx, dy) in enumerate(around):
        if dy == 0:
            source, target = edge_x.at[(dx + 1) // 2], rim_x.at[(dx + 1) // 2]
        elif dx == 0:
            source, target = edge_y.at[(dy + 1) // 2], rim_y.at[(dy + 1) // 2]
        else:
            source, target = edge_c.at[(dx + 1) // 2, (dy + 1) // 2], rim_c.at[(dx + 1) // 2, (dy + 1) // 2]
        rims.append(Exchange(10 + slot, dx, dy, source, target))

    lane = lax.broadcasted_iota(jnp.int32, (8, depth), 1)
    row = lax.broadcasted_iota(jnp.int32, (8, depth), 0)
    lane_faces = lax.broadcasted_iota(jnp.int32, (faces, depth), 1)

    def stage(d):
        for n in range(faces):
            staged[d, n * columns : (n + 1) * columns] = traces[d, n].astype(jnp.float32) * keep[d]

    def to_columns(d, chosen):
        for c in chosen:
            lifted[d, c] = staged[d, pl.ds(c, faces, stride=columns)].astype(jnp.bfloat16)

    loads["dirichlet"].wait()
    keep[...] = 1.0 - dirichlet[...].astype(jnp.float32)
    for x in range(wx):
        flag_y[x : x + 1] = keep[1, x * wy : x * wy + 1]
    flag_x[...] = keep[0, :wy]
    loads["y"].wait()
    stage(1)
    for x in range(wx):
        first_y[x] = staged[1, pl.ds(x * wy, faces, stride=columns)].astype(jnp.bfloat16)
    pl.when(total > 0)(lambda: pl.semaphore_wait(barrier, total))
    def tell(slot, dx, dy, if_present):
        @pl.when(if_present)
        def _():
            pl.semaphore_signal(ready.at[slot], inc=1, device_id=device(dx, dy), device_id_type=MESH)

    for slot in (1, 2):
        tell(slot, *below[slot], present(*below[slot]))
    flags_y.start()
    traces_y.start()
    flags_x.start()
    loads["x"].wait()
    stage(0)
    to_columns(0, range(wy))
    traces_x.start()

    def hear(slot, dx, dy):
        pl.when(present(dx, dy))(lambda: pl.semaphore_wait(ready.at[slot], 1))

    loads["z"].wait()
    stage(2)
    to_columns(0, range(wy, columns))
    to_columns(1, range(columns))
    to_columns(2, range(columns))
    for exchange in first + upward + [final_x, final_y] + rims:
        exchange.clear()
    for name in names[4:7]:
        loads[name].wait()
    level_sum = jnp.zeros(classes.shape, jnp.float32)
    for level in range(viscosity.shape[0]):
        level_sum = level_sum + jnp.where(classes[...] == level, viscosity[level], 0.0)
    visc[...] = level_sum
    visc_x[...] = level_sum[columns - wy :]
    for x in range(wx):
        c = x * wy + wy - 1
        visc_y[x : x + 1] = level_sum[c : c + 1]
    lanes_c = lax.broadcasted_iota(jnp.int32, (columns, depth), 1)
    for d in range(3):
        scale[2 * d] = level_sum * keep[d]
    scale[5] = level_sum * jnp.where(lanes_c == depth - 1, 0.0, pltpu.roll(keep[2], depth - 1, 1))
    scale[1, : columns - wy] = level_sum[: columns - wy] * keep[0, wy:]
    scale[3, : columns - 1] = level_sum[: columns - 1] * keep[1, 1:]
    for name in names[7:]:
        loads[name].wait()
    turned = jnp.concatenate([solve_t[f * faces : (f + 1) * faces] for f in ORDER], axis=0).T
    product[...] = jnp.dot(flux_map[...], turned, preferred_element_type=jnp.float32).astype(jnp.bfloat16)

    known = 4 * faces
    late = known // 128 * 128
    filler = jnp.zeros((known - late, depth), jnp.bfloat16)
    nothing = jnp.zeros((faces, depth), jnp.bfloat16)

    def rows_of(face_slot):
        return slice(face_slot * faces, (face_slot + 1) * faces)

    def lanes_of(index):
        return slice(index * depth, (index + 1) * depth)

    def z_above(c):
        low_z = lifted[2, c].astype(jnp.float32)
        return jnp.where(lane_faces == depth - 1, 0.0, pltpu.roll(low_z, depth - 1, 1)).astype(jnp.bfloat16)

    def low_part(c):
        return [lifted[0, c], lifted[1, c], lifted[2, c], z_above(c)]

    def high_x(c):
        return lifted[0, c + wy] if c + wy < columns else halo_x[c % wy]

    def high_y(c):
        return lifted[1, c + 1] if c % wy + 1 < wy else halo_y[c // wy]

    def side_by_side(blocks):
        return jnp.concatenate([jnp.concatenate(block, axis=0) for block in blocks], axis=1)

    def late_dot(left_rows, blocks):
        return jnp.dot(
            product[left_rows, late:],
            side_by_side([[filler, a, b] for a, b in blocks]),
            preferred_element_type=jnp.float32,
        )

    corners = {}

    def finish(chosen, flux, faces_in):
        rounded = []
        for index, c in enumerate(chosen):
            x, y = c // wy, c % wy
            parts = []
            for face_slot in range(6):
                term = flux(index, face_slot)
                trace = faces_in[index][face_slot]
                if trace is not None:
                    term = term + penalty * trace.astype(jnp.float32)
                parts.append(term * scale[face_slot, c : c + 1])
            residual[0, c] = parts[0]
            residual[1, c] = parts[2]
            residual[2, c] = parts[4] + pltpu.roll(parts[5], 1, 1)
            cut = jnp.concatenate(parts, axis=0).astype(jnp.bfloat16)
            if x + 1 < wx:
                high[0, c] = parts[1]
            elif y + 1 == wy:
                last_x[...] = cut[rows_of(1)]
            if y + 1 < wy:
                high[1, c] = parts[3]
            elif x + 1 == wx:
                last_y[...] = cut[rows_of(3)]
            rounded.append(cut)
        both = jnp.dot(gather[...], jnp.concatenate(rounded, axis=1), preferred_element_type=jnp.float32)
        sums = both[:32] + both[32:]
        for index, c in enumerate(chosen):
            x, y = c // wy, c % wy
            for dx, dy in itertools.product(range(2), range(2)):
                part = sums[16 * dx + 8 * dy : 16 * dx + 8 * dy + 8, lanes_of(index)]
                key = (x + dx, y + dy)
                corners[key] = part if key not in corners else corners[key] + part

    def process(chosen):
        slots = [low_part(c) + [high_x(c), high_y(c)] for c in chosen]
        flux = jnp.dot(product[...], side_by_side(slots), preferred_element_type=jnp.float32)
        by_slot = [[block[ORDER.index(f)] for f in range(6)] for block in slots]
        finish(chosen, lambda index, f: flux[rows_of(f), lanes_of(index)], by_slot)

    def prepare(which, chosen):
        slots = [low_part(c) for c in chosen]
        flux = jnp.dot(product[:, :known], side_by_side(slots), preferred_element_type=jnp.float32)
        for index in range(len(chosen)):
            for f in range(6):
                term = flux[rows_of(f), lanes_of(index)]
                if f in ORDER[:4]:
                    term = term + penalty * slots[index][ORDER.index(f)].astype(jnp.float32)
                base[which, rows_of(f), lanes_of(index)] = term

    def complete(which, chosen):
        pairs = [[high_x(c), high_y(c)] for c in chosen]
        flux = late_dot(slice(None), pairs)
        by_slot = [[None, a, None, b, None, None] for a, b in pairs]
        finish(
            chosen,
            lambda index, f: base[which, rows_of(f), lanes_of(index)] + flux[rows_of(f), lanes_of(index)],
            by_slot,
        )

    inner = [c for c in range(columns) if c + wy < columns and c % wy + 1 < wy]
    need_x = [c for c in range(columns) if c + wy >= columns and c % wy + 1 < wy]
    need_y = [c for c in range(columns) if c % wy + 1 == wy]
    early = len(inner) // 4 * 4
    rim_a, rim_b = need_x + inner[early:], need_y
    prepare(1, rim_b)
    prepare(0, rim_a)
    beside_y = late_dot(rows_of(3), [[high_x(c), nothing] for c in need_y[: wx - 1]])
    for x, c in enumerate(need_y[: wx - 1]):
        value = base[1, rows_of(3), lanes_of(x)] + beside_y[:, lanes_of(x)]
        send_y[x] = (value * visc[c : c + 1]).astype(jnp.bfloat16)
    beside_x = late_dot(rows_of(1), [[nothing, high_y(c)] for c in need_x])
    for y, c in enumerate(need_x):
        value = base[0, rows_of(1), lanes_of(y)] + beside_x[:, lanes_of(y)]
        send_x[y] = (value * visc[c : c + 1]).astype(jnp.bfloat16)
    for start in range(0, early, 4):
        process(inner[start : start + 4])
    hear(2, 1, 0)
    tell(3, 1, 0, present(1, -1))
    class_x.start()
    terms_x.start()
    hear(1, 0, 1)
    tell(0, -1, 0, present(-1, 1))
    class_y.start()
    terms_y.start()
    flags_x.arrive()
    traces_x.arrive()
    scale[1, columns - wy :] = visc[columns - wy :] * keep_x[...]
    complete(0, rim_a)
    flags_y.arrive()
    traces_y.arrive()
    for x in range(wx):
        c = x * wy + wy - 1
        scale[3, c : c + 1] = visc[c : c + 1] * keep_y[x : x + 1]
    complete(1, rim_b)

    vertices = list(itertools.product(range(wx + 1), range(wy + 1)))
    for x, y in vertices:
        value = corners[x, y]
        above = pltpu.roll(jnp.where(lane == depth - 1, 0.0, value), 1, 1)
        value = value + pltpu.roll(above, 4, 0)
        if x < wx and y < wy:
            corners[x, y] = jnp.where(row == CORNER - 1, diag[x * wy + y : x * wy + y + 1], value)
        else:
            corners[x, y] = jnp.where(row == CORNER - 1, 0.0, value)

    def pack(target, values):
        for i in range(0, len(values), 2):
            value = values[i]
            if i + 1 < len(values):
                value = jnp.where(row < CORNER, value, pltpu.roll(values[i + 1], 4, 0))
            target[i // 2] = value

    for side in range(2):
        for other in range(2):
            edge_c[side, other] = corners[side * wx, other * wy]
    for side in range(2):
        pack(edge_y.at[side], [corners[x, side * wy] for x in range(wx + 1)])
        pack(edge_x.at[side], [corners[side * wx, y] for y in range(wy + 1)])
    for exchange in rims[1:-1]:
        exchange.start()
    final_y.start()
    final_x.start()
    hear(3, -1, -1)
    rims[0].start()
    hear(0, 1, 1)
    rims[-1].start()

    for c in range(columns):
        if c >= wy:
            residual[0, c] += high[0, c - wy]
        if c % wy:
            residual[1, c] += high[1, c - 1]
    for exchange in upward:
        exchange.arrive()
    mine_x = late_dot(rows_of(1), [[lifted[0, y], nothing] for y in range(wy - 1)])
    for y in range(wy - 1):
        value = mine_x[:, lanes_of(y)] + penalty * lifted[0, y].astype(jnp.float32)
        value = value * prev_x[y : y + 1] + recv_x[y].astype(jnp.float32)
        residual[0, y] += value * keep[0, y : y + 1]
    mine_y = late_dot(rows_of(3), [[nothing, lifted[1, x * wy]] for x in range(wx - 1)])
    for x in range(wx - 1):
        c = x * wy
        value = mine_y[:, lanes_of(x)] + penalty * lifted[1, c].astype(jnp.float32)
        value = value * prev_y[x : x + 1] + recv_y[x].astype(jnp.float32)
        residual[1, c] += value * keep[1, c : c + 1]

    fixes = {}

    def correct(value, inside):
        under = jnp.broadcast_to(value[CORNER - 1 : CORNER], value.shape)
        if inside is not None:
            value = jnp.where(inside, value, 0.0)
            under = jnp.where(inside, under, 1.0)
        fix = value / under
        above = jnp.where(lane == depth - 1, 0.0, pltpu.roll(fix, depth - 1, 1))
        return jnp.where(row < CORNER, fix, pltpu.roll(above, 4, 0))

    def emit(chosen):
        stacks = []
        for c in chosen:
            x, y = c // wy, c % wy
            value = jnp.concatenate([fixes[x, y], fixes[x, y + 1], fixes[x + 1, y], fixes[x + 1, y + 1]], axis=0)
            upper = value.astype(jnp.bfloat16)
            lower = (value - upper.astype(jnp.float32)).astype(jnp.bfloat16)
            stacks.append(jnp.concatenate([upper, lower, upper], axis=0))
        lift = jnp.dot(spread[...], jnp.concatenate(stacks, axis=1), preferred_element_type=jnp.float32)
        for index, c in enumerate(chosen):
            x, y = c // wy, c % wy
            for d in range(3):
                value = residual[d, c]
                if d == 0 and x == 0 and y + 1 == wy:
                    value = value + corner_x[...].astype(jnp.float32)
                if d == 1 and y == 0 and x + 1 == wx:
                    value = value + corner_y[...].astype(jnp.float32)
                piece = lift[d * faces : (d + 1) * faces, lanes_of(index)]
                out[d, c * faces : (c + 1) * faces] = value + keep[d, c : c + 1] * piece

    for x, y in vertices:
        if 0 < x < wx and 0 < y < wy:
            fixes[x, y] = correct(corners[x, y], None)
    middle = [c for c in range(columns) if 0 < c // wy < wx - 1 and 0 < c % wy < wy - 1]
    outer = [c for c in range(columns) if c not in middle]
    emit(middle)
    for exchange in first + upward:
        exchange.drain()

    for exchange in rims:
        exchange.arrive()

    def unpack(source, index):
        value = source[index // 2]
        return pltpu.roll(value, 4, 0) if index % 2 else value

    for x, y in vertices:
        if (x, y) in fixes:
            continue
        value = corners[x, y]
        side_x = {0: 0, wx: 1}.get(x)
        side_y = {0: 0, wy: 1}.get(y)
        if side_x is not None:
            value = value + unpack(rim_x.at[1 - side_x], y)
        if side_y is not None:
            value = value + unpack(rim_y.at[1 - side_y], x)
        if side_x is not None and side_y is not None:
            value = value + rim_c[1 - side_x, 1 - side_y]
        fixes[x, y] = correct(value, present(int(x == wx), int(y == wy)))
    final_x.arrive()
    final_y.arrive()
    for start in range(0, len(outer), 4):
        emit(outer[start : start + 4])

    for exchange in rims + [final_x, final_y]:
        exchange.drain()

def deliver(faces, columns, values, out_hbm, rounded, store_sem):
    stores = []
    for d in range(3):
        for n in range(faces):
            rounded[d, n] = values[d, pl.ds(n, columns, stride=faces)].astype(jnp.bfloat16)
        stores.append(pltpu.make_async_copy(rounded.at[d], out_hbm.at[d], store_sem.at[d]))
        stores[-1].start()
    for store in stores:
        store.wait()


def local(count_x, count_y, traces, dirichlet, visc_class, viscosity, coarse_diag, solve_map, flux_map):
    faces, wx, wy, depth = traces.shape[1:]
    columns = wx * wy
    operands = (
        traces.reshape(3, faces, columns, depth),
        dirichlet.reshape(3, columns, depth),
        visc_class.reshape(columns, depth),
        viscosity,
        coarse_diag.reshape(columns, depth),
        solve_map.T,
        flux_map,
        jnp.asarray(gather_table()),
        jnp.asarray(spread_table()),
    )
    anywhere = pl.BlockSpec(memory_space=pl.ANY)
    exchanges = 18
    rims_x, rims_y = wy // 2 + 1, wx // 2 + 1
    f32, bf16 = jnp.float32, jnp.bfloat16
    scratch = [
        pltpu.SMEM(a.shape, a.dtype) if index == 3 else pltpu.VMEM(a.shape, a.dtype) for index, a in enumerate(operands)
    ] + [
        pltpu.VMEM((3, faces * columns, depth), f32),
        pltpu.VMEM((6 * faces, 6 * faces), bf16),
        pltpu.VMEM((3, columns, faces, depth), bf16),
        pltpu.VMEM((3, columns, depth), f32),
        pltpu.VMEM((6, columns, depth), f32),
        pltpu.VMEM((columns, depth), f32),
        pltpu.VMEM((wy, faces, depth), bf16),
        pltpu.VMEM((wx, faces, depth), bf16),
        pltpu.VMEM((wx, faces, depth), bf16),
        pltpu.VMEM((wy, depth), f32),
        pltpu.VMEM((wx, depth), f32),
        pltpu.VMEM((wy, depth), f32),
        pltpu.VMEM((wx, depth), f32),
        pltpu.VMEM((3, columns, faces, depth), f32),
        pltpu.VMEM((2, columns, faces, depth), f32),
        pltpu.VMEM((2, 6 * faces, 4 * depth), f32),
        pltpu.VMEM((wy - 1, faces, depth), bf16),
        pltpu.VMEM((wx - 1, faces, depth), bf16),
        pltpu.VMEM((wy - 1, faces, depth), bf16),
        pltpu.VMEM((wx - 1, faces, depth), bf16),
        pltpu.VMEM((wy, depth), f32),
        pltpu.VMEM((wx, depth), f32),
        pltpu.VMEM((wy, depth), f32),
        pltpu.VMEM((wx, depth), f32),
        pltpu.VMEM((faces, depth), bf16),
        pltpu.VMEM((faces, depth), bf16),
        pltpu.VMEM((faces, depth), bf16),
        pltpu.VMEM((faces, depth), bf16),
        pltpu.VMEM((2, rims_x, 8, depth), f32),
        pltpu.VMEM((2, rims_y, 8, depth), f32),
        pltpu.VMEM((2, 2, 8, depth), f32),
        pltpu.VMEM((2, rims_x, 8, depth), f32),
        pltpu.VMEM((2, rims_y, 8, depth), f32),
        pltpu.VMEM((2, 2, 8, depth), f32),
        pltpu.SemaphoreType.DMA((len(operands) + 2,)),
        pltpu.SemaphoreType.DMA((exchanges,)),
        pltpu.SemaphoreType.DMA((exchanges,)),
        pltpu.SemaphoreType.REGULAR((4,)),
    ]
    result = pl.pallas_call(
        functools.partial(kernel, count_x, count_y, wx, wy),
        out_shape=pltpu.VMEM((3, columns * faces, depth), f32),
        in_specs=[anywhere] * len(operands),
        out_specs=pl.BlockSpec(memory_space=pltpu.VMEM),
        scratch_shapes=scratch,
        compiler_params=pltpu.CompilerParams(collective_id=0, has_side_effects=True),
        name="apply",
    )(*operands)
    result = pl.pallas_call(
        functools.partial(deliver, faces, columns),
        out_shape=jax.ShapeDtypeStruct((3, faces, columns, depth), bf16),
        in_specs=[pl.BlockSpec(memory_space=pltpu.VMEM)],
        out_specs=anywhere,
        scratch_shapes=[pltpu.VMEM((3, faces, columns, depth), bf16), pltpu.SemaphoreType.DMA((3,))],
        compiler_params=pltpu.CompilerParams(vmem_limit_bytes=16 * 2**20),
        name="deliver",
    )(result)
    return result.reshape(3, faces, wx, wy, depth)


def solution(mesh):
    count_x, count_y = mesh.shape["gx"], mesh.shape["gy"]
    in_specs = (
        P(None, None, "gx", "gy", None),
        P(None, "gx", "gy", None),
        P("gx", "gy", None),
        P(),
        P("gx", "gy", None),
        P(),
        P(),
    )
    out_specs = P(None, None, "gx", "gy", None)
    return jax.shard_map(
        functools.partial(local, count_x, count_y), mesh=mesh, in_specs=in_specs, out_specs=out_specs, check_vma=False
    )
```

```python
import functools
import itertools
import math

import jax
import jax.numpy as jnp
import ml_dtypes
import numpy as np
from jax import lax
from jax.experimental import pallas as pl
from jax.experimental.pallas import tpu as pltpu
from jax.sharding import PartitionSpec as P

MESH = pl.DeviceIdType.MESH
penalty = 0.5
ORDER = (0, 2, 4, 5, 1, 3)
PITCH = 52
STAGE = 20
CORNER = 4


def corner_table():
    points = [-1.0, -math.sqrt(0.2), math.sqrt(0.2), 1.0]
    table = np.zeros((16, 4), np.float64)
    for a, b, p, q in itertools.product(range(4), range(4), range(2), range(2)):
        table[4 * a + b, 2 * p + q] = (1 + (2 * p - 1) * points[a]) * (1 + (2 * q - 1) * points[b]) / 4
    return table.astype(np.float32)


def in_two(table):
    high = table.astype(ml_dtypes.bfloat16)
    low = (table - high.astype(np.float32)).astype(ml_dtypes.bfloat16)
    return high, low


def gather_table():
    weights = corner_table()
    table = np.zeros((32, 6, 3, 16), np.float32)
    for dx, dy, dz, m in itertools.product(range(2), range(2), range(2), range(3)):
        row = 16 * dx + 8 * dy + CORNER * dz + m
        table[row, dx, m] = weights[:, 2 * dy + dz]
        table[row, 2 + dy, m] = weights[:, 2 * dx + dz]
        table[row, 4 + dz, m] = weights[:, 2 * dx + dy]
    return np.concatenate(in_two(table.reshape(32, 288)), axis=0)


def spread_table():
    weights = corner_table()
    table = np.zeros((3, 3, 16, 32), np.float32)
    for dx, dy, dz, m in itertools.product(range(2), range(2), range(2), range(3)):
        column = 16 * dx + 8 * dy + CORNER * dz + m
        if dx == 0:
            table[0, m, :, column] = weights[:, 2 * dy + dz]
        if dy == 0:
            table[1, m, :, column] = weights[:, 2 * dx + dz]
        if dz == 0:
            table[2, m, :, column] = weights[:, 2 * dx + dy]
    high, low = in_two(table.reshape(144, 32))
    return np.concatenate([high, high, low], axis=1)


def kernel(
    count_x, count_y, wx, wy,
    traces_hbm, dirichlet_hbm, class_hbm, viscosity_hbm, diag_hbm, solve_hbm, flux_hbm, gather_hbm, spread_hbm,
    out,
    traces, dirichlet, classes, viscosity, diag, solve_t, flux_map, gather, spread,
    staged, product, lifted, keep, scale, visc, halo_x, halo_y, first_y, flag_x, flag_y, keep_x, keep_y,
    residual, high, base, send_x, send_y, recv_x, recv_y, visc_x, visc_y, prev_x, prev_y, last_x, last_y, corner_x, corner_y,
    edge_x, edge_y, edge_c, rim_x, rim_y, rim_c,
    load_sem, send_sem, recv_sem, ready,
):
    columns, depth = wx * wy, traces.shape[3]
    faces = traces.shape[1]
    me_x, me_y = lax.axis_index("gx"), lax.axis_index("gy")
    there = {-1: (me_x > 0, me_y > 0), 0: (None, None), 1: (me_x < count_x - 1, me_y < count_y - 1)}

    def present(dx, dy):
        a, b = there[dx][0], there[dy][1]
        if a is None:
            return b
        return a if b is None else jnp.logical_and(a, b)

    def device(dx, dy):
        return {"gx": me_x + dx, "gy": me_y + dy}

    around = [(-1, -1), (0, -1), (-1, 0), (1, -1), (1, 0), (-1, 1), (0, 1), (1, 1)]
    names = ("dirichlet", "y", "x", "z", "viscosity", "classes", "solve", "flux", "gather", "diag", "spread")
    pairs = [
        (dirichlet_hbm, dirichlet), (traces_hbm.at[1], traces.at[1]), (traces_hbm.at[0], traces.at[0]),
        (traces_hbm.at[2], traces.at[2]), (viscosity_hbm, viscosity), (class_hbm, classes), (solve_hbm, solve_t),
        (flux_hbm, flux_map), (gather_hbm, gather), (diag_hbm, diag), (spread_hbm, spread),
    ]
    loads = {name: pltpu.make_async_copy(a, b, load_sem.at[i]) for i, (name, (a, b)) in enumerate(zip(names, pairs))}
    for load in loads.values():
        load.start()

    barrier = pltpu.get_barrier_semaphore()
    total = 0
    below = [None, (0, -1), (-1, 0)]
    for dx, dy in below[1:]:
        total = total + present(dx, dy).astype(jnp.int32)

        @pl.when(present(-dx, -dy))
        def _():
            pl.semaphore_signal(barrier, inc=1, device_id=device(-dx, -dy), device_id_type=MESH)

    class Exchange:
        def __init__(self, slot, dx, dy, source, target):
            self.to, self.origin, self.target = present(dx, dy), present(-dx, -dy), target
            self.copy = pltpu.make_async_remote_copy(
                src_ref=source, dst_ref=target, send_sem=send_sem.at[slot], recv_sem=recv_sem.at[slot],
                device_id=device(dx, dy), device_id_type=MESH,
            )

        def clear(self):
            @pl.when(jnp.logical_not(self.origin))
            def _():
                self.target[...] = jnp.zeros(self.target.shape, self.target.dtype)

        def start(self):
            pl.when(self.to)(self.copy.start)

        def arrive(self):
            pl.when(self.origin)(self.copy.wait_recv)

        def drain(self):
            pl.when(self.to)(self.copy.wait_send)

    traces_x = Exchange(0, -1, 0, lifted.at[0, pl.ds(0, wy)], halo_x)
    flags_x = Exchange(1, -1, 0, flag_x, keep_x)
    traces_y = Exchange(2, 0, -1, first_y, halo_y)
    flags_y = Exchange(3, 0, -1, flag_y, keep_y)
    terms_x = Exchange(4, 1, 0, send_x, recv_x)
    terms_y = Exchange(5, 0, 1, send_y, recv_y)
    class_x = Exchange(6, 1, 0, visc_x, prev_x)
    class_y = Exchange(7, 0, 1, visc_y, prev_y)
    final_x = Exchange(8, 1, 0, last_x, corner_x)
    final_y = Exchange(9, 0, 1, last_y, corner_y)
    upward = [class_x, class_y, terms_x, terms_y]
    first = [flags_y, traces_y, flags_x, traces_x]
    rims = []
    for slot, (dx, dy) in enumerate(around):
        if dy == 0:
            source, target = edge_x.at[(dx + 1) // 2], rim_x.at[(dx + 1) // 2]
        elif dx == 0:
            source, target = edge_y.at[(dy + 1) // 2], rim_y.at[(dy + 1) // 2]
        else:
            source, target = edge_c.at[(dx + 1) // 2, (dy + 1) // 2], rim_c.at[(dx + 1) // 2, (dy + 1) // 2]
        rims.append(Exchange(10 + slot, dx, dy, source, target))

    lane = lax.broadcasted_iota(jnp.int32, (8, depth), 1)
    row = lax.broadcasted_iota(jnp.int32, (8, depth), 0)
    lane_faces = lax.broadcasted_iota(jnp.int32, (faces, depth), 1)

    def stage(d):
        for n in range(faces):
            staged[d, n * STAGE : n * STAGE + columns] = traces[d, n].astype(jnp.float32) * keep[d]

    def to_columns(d, chosen):
        for c in chosen:
            lifted[d, c] = staged[d, pl.ds(c, faces, stride=STAGE)].astype(jnp.bfloat16)

    loads["dirichlet"].wait()
    keep[...] = 1.0 - dirichlet[...].astype(jnp.float32)
    for x in range(wx):
        flag_y[x : x + 1] = keep[1, x * wy : x * wy + 1]
    flag_x[...] = keep[0, :wy]
    loads["y"].wait()
    stage(1)
    for x in range(wx):
        first_y[x] = staged[1, pl.ds(x * wy, faces, stride=STAGE)].astype(jnp.bfloat16)
    pl.when(total > 0)(lambda: pl.semaphore_wait(barrier, total))
    def tell(slot, dx, dy, if_present):
        @pl.when(if_present)
        def _():
            pl.semaphore_signal(ready.at[slot], inc=1, device_id=device(dx, dy), device_id_type=MESH)

    for slot in (1, 2):
        tell(slot, *below[slot], present(*below[slot]))
    flags_y.start()
    traces_y.start()
    flags_x.start()
    loads["x"].wait()
    stage(0)
    to_columns(0, range(wy))
    traces_x.start()

    def hear(slot, dx, dy):
        pl.when(present(dx, dy))(lambda: pl.semaphore_wait(ready.at[slot], 1))

    loads["z"].wait()
    stage(2)
    to_columns(0, range(wy, columns))
    to_columns(1, range(columns))
    to_columns(2, range(columns))
    for exchange in first + upward + [final_x, final_y] + rims:
        exchange.clear()
    for name in names[4:7]:
        loads[name].wait()
    level_sum = jnp.zeros(classes.shape, jnp.float32)
    for level in range(viscosity.shape[0]):
        level_sum = level_sum + jnp.where(classes[...] == level, viscosity[level], 0.0)
    visc[...] = level_sum
    visc_x[...] = level_sum[columns - wy :]
    for x in range(wx):
        c = x * wy + wy - 1
        visc_y[x : x + 1] = level_sum[c : c + 1]
    lanes_c = lax.broadcasted_iota(jnp.int32, (columns, depth), 1)
    for d in range(3):
        scale[2 * d] = level_sum * keep[d]
    scale[5] = level_sum * jnp.where(lanes_c == depth - 1, 0.0, pltpu.roll(keep[2], depth - 1, 1))
    scale[1, : columns - wy] = level_sum[: columns - wy] * keep[0, wy:]
    scale[3, : columns - 1] = level_sum[: columns - 1] * keep[1, 1:]
    for name in names[7:]:
        loads[name].wait()
    turned = jnp.concatenate([solve_t[f * faces : (f + 1) * faces] for f in ORDER], axis=0).T
    product[...] = jnp.dot(flux_map[...], turned, preferred_element_type=jnp.float32).astype(jnp.bfloat16)

    known = 4 * faces
    late = known // 128 * 128
    filler = jnp.zeros((known - late, depth), jnp.bfloat16)
    nothing = jnp.zeros((faces, depth), jnp.bfloat16)

    def rows_of(face_slot):
        return slice(face_slot * faces, (face_slot + 1) * faces)

    def lanes_of(index):
        return slice(index * depth, (index + 1) * depth)

    def z_above(c):
        low_z = lifted[2, c].astype(jnp.float32)
        return jnp.where(lane_faces == depth - 1, 0.0, pltpu.roll(low_z, depth - 1, 1)).astype(jnp.bfloat16)

    def low_part(c):
        return [lifted[0, c], lifted[1, c], lifted[2, c], z_above(c)]

    def high_x(c):
        return lifted[0, c + wy] if c + wy < columns else halo_x[c % wy]

    def high_y(c):
        return lifted[1, c + 1] if c % wy + 1 < wy else halo_y[c // wy]

    def side_by_side(blocks):
        return jnp.concatenate([jnp.concatenate(block, axis=0) for block in blocks], axis=1)

    def late_dot(left_rows, blocks):
        return jnp.dot(
            product[left_rows, late:],
            side_by_side([[filler, a, b] for a, b in blocks]),
            preferred_element_type=jnp.float32,
        )

    corners = {}

    def finish(chosen, flux, faces_in):
        rounded = []
        for index, c in enumerate(chosen):
            x, y = c // wy, c % wy
            parts = []
            for face_slot in range(6):
                term = flux(index, face_slot)
                trace = faces_in[index][face_slot]
                if trace is not None:
                    term = term + penalty * trace.astype(jnp.float32)
                parts.append(term * scale[face_slot, c : c + 1])
            residual[0, c] = parts[0]
            residual[1, c] = parts[2]
            residual[2, c] = parts[4] + pltpu.roll(parts[5], 1, 1)
            cut = jnp.concatenate(parts, axis=0).astype(jnp.bfloat16)
            if x + 1 < wx:
                high[0, c] = parts[1]
            elif y + 1 == wy:
                last_x[...] = cut[rows_of(1)]
            if y + 1 < wy:
                high[1, c] = parts[3]
            elif x + 1 == wx:
                last_y[...] = cut[rows_of(3)]
            rounded.append(cut)
        both = jnp.dot(gather[...], jnp.concatenate(rounded, axis=1), preferred_element_type=jnp.float32)
        sums = both[:32] + both[32:]
        for index, c in enumerate(chosen):
            x, y = c // wy, c % wy
            for dx, dy in itertools.product(range(2), range(2)):
                part = sums[16 * dx + 8 * dy : 16 * dx + 8 * dy + 8, lanes_of(index)]
                key = (x + dx, y + dy)
                corners[key] = part if key not in corners else corners[key] + part

    def process(chosen):
        slots = [low_part(c) + [high_x(c), high_y(c)] for c in chosen]
        flux = jnp.dot(product[...], side_by_side(slots), preferred_element_type=jnp.float32)
        by_slot = [[block[ORDER.index(f)] for f in range(6)] for block in slots]
        finish(chosen, lambda index, f: flux[rows_of(f), lanes_of(index)], by_slot)

    def prepare(which, chosen):
        slots = [low_part(c) for c in chosen]
        flux = jnp.dot(product[:, :known], side_by_side(slots), preferred_element_type=jnp.float32)
        for index in range(len(chosen)):
            for f in range(6):
                term = flux[rows_of(f), lanes_of(index)]
                if f in ORDER[:4]:
                    term = term + penalty * slots[index][ORDER.index(f)].astype(jnp.float32)
                base[which, rows_of(f), lanes_of(index)] = term

    def complete(which, chosen):
        pairs = [[high_x(c), high_y(c)] for c in chosen]
        flux = late_dot(slice(None), pairs)
        by_slot = [[None, a, None, b, None, None] for a, b in pairs]
        finish(
            chosen,
            lambda index, f: base[which, rows_of(f), lanes_of(index)] + flux[rows_of(f), lanes_of(index)],
            by_slot,
        )

    inner = [c for c in range(columns) if c + wy < columns and c % wy + 1 < wy]
    need_x = [c for c in range(columns) if c + wy >= columns and c % wy + 1 < wy]
    need_y = [c for c in range(columns) if c % wy + 1 == wy]
    early = len(inner) // 4 * 4
    rim_a, rim_b = need_x + inner[early:], need_y
    prepare(1, rim_b)
    prepare(0, rim_a)
    beside_y = late_dot(rows_of(3), [[high_x(c), nothing] for c in need_y[: wx - 1]])
    for x, c in enumerate(need_y[: wx - 1]):
        value = base[1, rows_of(3), lanes_of(x)] + beside_y[:, lanes_of(x)]
        send_y[x] = (value * visc[c : c + 1]).astype(jnp.bfloat16)
    beside_x = late_dot(rows_of(1), [[nothing, high_y(c)] for c in need_x])
    for y, c in enumerate(need_x):
        value = base[0, rows_of(1), lanes_of(y)] + beside_x[:, lanes_of(y)]
        send_x[y] = (value * visc[c : c + 1]).astype(jnp.bfloat16)
    for start in range(0, early, 4):
        process(inner[start : start + 4])
    hear(2, 1, 0)
    tell(3, 1, 0, present(1, -1))
    class_x.start()
    terms_x.start()
    hear(1, 0, 1)
    tell(0, -1, 0, present(-1, 1))
    class_y.start()
    terms_y.start()
    flags_x.arrive()
    traces_x.arrive()
    scale[1, columns - wy :] = visc[columns - wy :] * keep_x[...]
    complete(0, rim_a)
    flags_y.arrive()
    traces_y.arrive()
    for x in range(wx):
        c = x * wy + wy - 1
        scale[3, c : c + 1] = visc[c : c + 1] * keep_y[x : x + 1]
    complete(1, rim_b)

    vertices = list(itertools.product(range(wx + 1), range(wy + 1)))
    for x, y in vertices:
        value = corners[x, y]
        above = pltpu.roll(jnp.where(lane == depth - 1, 0.0, value), 1, 1)
        value = value + pltpu.roll(above, 4, 0)
        if x < wx and y < wy:
            corners[x, y] = jnp.where(row == CORNER - 1, diag[x * wy + y : x * wy + y + 1], value)
        else:
            corners[x, y] = jnp.where(row == CORNER - 1, 0.0, value)

    def pack(target, values):
        for i in range(0, len(values), 2):
            value = values[i]
            if i + 1 < len(values):
                value = jnp.where(row < CORNER, value, pltpu.roll(values[i + 1], 4, 0))
            target[i // 2] = value

    for side in range(2):
        for other in range(2):
            edge_c[side, other] = corners[side * wx, other * wy]
    for side in range(2):
        pack(edge_y.at[side], [corners[x, side * wy] for x in range(wx + 1)])
        pack(edge_x.at[side], [corners[side * wx, y] for y in range(wy + 1)])
    for exchange in rims[1:-1]:
        exchange.start()
    final_y.start()
    final_x.start()
    hear(3, -1, -1)
    rims[0].start()
    hear(0, 1, 1)
    rims[-1].start()

    for c in range(columns):
        if c >= wy:
            residual[0, c] += high[0, c - wy]
        if c % wy:
            residual[1, c] += high[1, c - 1]
    for exchange in upward:
        exchange.arrive()
    mine_x = late_dot(rows_of(1), [[lifted[0, y], nothing] for y in range(wy - 1)])
    for y in range(wy - 1):
        value = mine_x[:, lanes_of(y)] + penalty * lifted[0, y].astype(jnp.float32)
        value = value * prev_x[y : y + 1] + recv_x[y].astype(jnp.float32)
        residual[0, y] += value * keep[0, y : y + 1]
    mine_y = late_dot(rows_of(3), [[nothing, lifted[1, x * wy]] for x in range(wx - 1)])
    for x in range(wx - 1):
        c = x * wy
        value = mine_y[:, lanes_of(x)] + penalty * lifted[1, c].astype(jnp.float32)
        value = value * prev_y[x : x + 1] + recv_y[x].astype(jnp.float32)
        residual[1, c] += value * keep[1, c : c + 1]

    fixes = {}

    def correct(value, inside):
        under = jnp.broadcast_to(value[CORNER - 1 : CORNER], value.shape)
        if inside is not None:
            value = jnp.where(inside, value, 0.0)
            under = jnp.where(inside, under, 1.0)
        fix = value / under
        above = jnp.where(lane == depth - 1, 0.0, pltpu.roll(fix, depth - 1, 1))
        return jnp.where(row < CORNER, fix, pltpu.roll(above, 4, 0))

    def emit(chosen):
        stacks = []
        for c in chosen:
            x, y = c // wy, c % wy
            value = jnp.concatenate([fixes[x, y], fixes[x, y + 1], fixes[x + 1, y], fixes[x + 1, y + 1]], axis=0)
            upper = value.astype(jnp.bfloat16)
            lower = (value - upper.astype(jnp.float32)).astype(jnp.bfloat16)
            stacks.append(jnp.concatenate([upper, lower, upper], axis=0))
        lift = jnp.dot(spread[...], jnp.concatenate(stacks, axis=1), preferred_element_type=jnp.float32)
        for index, c in enumerate(chosen):
            x, y = c // wy, c % wy
            for d in range(3):
                value = residual[d, c]
                if d == 0 and x == 0 and y + 1 == wy:
                    value = value + corner_x[...].astype(jnp.float32)
                if d == 1 and y == 0 and x + 1 == wx:
                    value = value + corner_y[...].astype(jnp.float32)
                piece = lift[d * faces : (d + 1) * faces, lanes_of(index)]
                out[d, c * PITCH : c * PITCH + faces] = value + keep[d, c : c + 1] * piece

    for x, y in vertices:
        if 0 < x < wx and 0 < y < wy:
            fixes[x, y] = correct(corners[x, y], None)
    middle = [c for c in range(columns) if 0 < c // wy < wx - 1 and 0 < c % wy < wy - 1]
    outer = [c for c in range(columns) if c not in middle]
    emit(middle)
    for exchange in first + upward + rims + [final_x, final_y]:
        exchange.drain()

    for exchange in rims:
        exchange.arrive()

    def unpack(source, index):
        value = source[index // 2]
        return pltpu.roll(value, 4, 0) if index % 2 else value

    for x, y in vertices:
        if (x, y) in fixes:
            continue
        value = corners[x, y]
        side_x = {0: 0, wx: 1}.get(x)
        side_y = {0: 0, wy: 1}.get(y)
        if side_x is not None:
            value = value + unpack(rim_x.at[1 - side_x], y)
        if side_y is not None:
            value = value + unpack(rim_y.at[1 - side_y], x)
        if side_x is not None and side_y is not None:
            value = value + rim_c[1 - side_x, 1 - side_y]
        fixes[x, y] = correct(value, present(int(x == wx), int(y == wy)))
    final_x.arrive()
    final_y.arrive()
    for start in range(0, len(outer), 4):
        emit(outer[start : start + 4])


def deliver(faces, columns, values, out_hbm, rounded, store_sem):
    stores = []
    for d in range(3):
        for n in range(faces):
            rounded[d, n] = values[d, pl.ds(n, columns, stride=PITCH)].astype(jnp.bfloat16)
        stores.append(pltpu.make_async_copy(rounded.at[d], out_hbm.at[d], store_sem.at[d]))
        stores[-1].start()
    for store in stores:
        store.wait()


def local(count_x, count_y, traces, dirichlet, visc_class, viscosity, coarse_diag, solve_map, flux_map):
    faces, wx, wy, depth = traces.shape[1:]
    columns = wx * wy
    operands = (
        traces.reshape(3, faces, columns, depth),
        dirichlet.reshape(3, columns, depth),
        visc_class.reshape(columns, depth),
        viscosity,
        coarse_diag.reshape(columns, depth),
        solve_map.T,
        flux_map,
        jnp.asarray(gather_table()),
        jnp.asarray(spread_table()),
    )
    anywhere = pl.BlockSpec(memory_space=pl.ANY)
    exchanges = 18
    rims_x, rims_y = wy // 2 + 1, wx // 2 + 1
    f32, bf16 = jnp.float32, jnp.bfloat16
    scratch = [
        pltpu.SMEM(a.shape, a.dtype) if index == 3 else pltpu.VMEM(a.shape, a.dtype) for index, a in enumerate(operands)
    ] + [
        pltpu.VMEM((3, (faces + 1) * STAGE, depth), f32),
        pltpu.VMEM((6 * faces, 6 * faces), bf16),
        pltpu.VMEM((3, columns, faces, depth), bf16),
        pltpu.VMEM((3, columns, depth), f32),
        pltpu.VMEM((6, columns, depth), f32),
        pltpu.VMEM((columns, depth), f32),
        pltpu.VMEM((wy, faces, depth), bf16),
        pltpu.VMEM((wx, faces, depth), bf16),
        pltpu.VMEM((wx, faces, depth), bf16),
        pltpu.VMEM((wy, depth), f32),
        pltpu.VMEM((wx, depth), f32),
        pltpu.VMEM((wy, depth), f32),
        pltpu.VMEM((wx, depth), f32),
        pltpu.VMEM((3, columns, faces, depth), f32),
        pltpu.VMEM((2, columns, faces, depth), f32),
        pltpu.VMEM((2, 6 * faces, 4 * depth), f32),
        pltpu.VMEM((wy - 1, faces, depth), bf16),
        pltpu.VMEM((wx - 1, faces, depth), bf16),
        pltpu.VMEM((wy - 1, faces, depth), bf16),
        pltpu.VMEM((wx - 1, faces, depth), bf16),
        pltpu.VMEM((wy, depth), f32),
        pltpu.VMEM((wx, depth), f32),
        pltpu.VMEM((wy, depth), f32),
        pltpu.VMEM((wx, depth), f32),
        pltpu.VMEM((faces, depth), bf16),
        pltpu.VMEM((faces, depth), bf16),
        pltpu.VMEM((faces, depth), bf16),
        pltpu.VMEM((faces, depth), bf16),
        pltpu.VMEM((2, rims_x, 8, depth), f32),
        pltpu.VMEM((2, rims_y, 8, depth), f32),
        pltpu.VMEM((2, 2, 8, depth), f32),
        pltpu.VMEM((2, rims_x, 8, depth), f32),
        pltpu.VMEM((2, rims_y, 8, depth), f32),
        pltpu.VMEM((2, 2, 8, depth), f32),
        pltpu.SemaphoreType.DMA((len(operands) + 2,)),
        pltpu.SemaphoreType.DMA((exchanges,)),
        pltpu.SemaphoreType.DMA((exchanges,)),
        pltpu.SemaphoreType.REGULAR((4,)),
    ]
    result = pl.pallas_call(
        functools.partial(kernel, count_x, count_y, wx, wy),
        out_shape=pltpu.VMEM((3, (columns + 1) * PITCH, depth), f32),
        in_specs=[anywhere] * len(operands),
        out_specs=pl.BlockSpec(memory_space=pltpu.VMEM),
        scratch_shapes=scratch,
        compiler_params=pltpu.CompilerParams(collective_id=0, has_side_effects=True),
        name="apply",
    )(*operands)
    result = pl.pallas_call(
        functools.partial(deliver, faces, columns),
        out_shape=jax.ShapeDtypeStruct((3, faces, columns, depth), bf16),
        in_specs=[pl.BlockSpec(memory_space=pltpu.VMEM)],
        out_specs=anywhere,
        scratch_shapes=[pltpu.VMEM((3, faces, columns, depth), bf16), pltpu.SemaphoreType.DMA((3,))],
        compiler_params=pltpu.CompilerParams(vmem_limit_bytes=16 * 2**20),
        name="deliver",
    )(result)
    return result.reshape(3, faces, wx, wy, depth)


def solution(mesh):
    count_x, count_y = mesh.shape["gx"], mesh.shape["gy"]
    in_specs = (
        P(None, None, "gx", "gy", None),
        P(None, "gx", "gy", None),
        P("gx", "gy", None),
        P(),
        P("gx", "gy", None),
        P(),
        P(),
    )
    out_specs = P(None, None, "gx", "gy", None)
    return jax.shard_map(
        functools.partial(local, count_x, count_y), mesh=mesh, in_specs=in_specs, out_specs=out_specs, check_vma=False
    )
```

```python
import functools
import itertools
import math

import jax
import jax.numpy as jnp
import ml_dtypes
import numpy as np
from jax import lax
from jax.experimental import pallas as pl
from jax.experimental.pallas import tpu as pltpu
from jax.sharding import PartitionSpec as P

MESH = pl.DeviceIdType.MESH
penalty = 0.5
ORDER = (0, 2, 4, 5, 1, 3)
PITCH = 52
STAGE = 20
CORNER = 4


def corner_table():
    points = [-1.0, -math.sqrt(0.2), math.sqrt(0.2), 1.0]
    table = np.zeros((16, 4), np.float64)
    for a, b, p, q in itertools.product(range(4), range(4), range(2), range(2)):
        table[4 * a + b, 2 * p + q] = (1 + (2 * p - 1) * points[a]) * (1 + (2 * q - 1) * points[b]) / 4
    return table.astype(np.float32)


def in_two(table):
    high = table.astype(ml_dtypes.bfloat16)
    low = (table - high.astype(np.float32)).astype(ml_dtypes.bfloat16)
    return high, low


def gather_table():
    weights = corner_table()
    table = np.zeros((32, 6, 3, 16), np.float32)
    for dx, dy, dz, m in itertools.product(range(2), range(2), range(2), range(3)):
        row = 16 * dx + 8 * dy + CORNER * dz + m
        table[row, dx, m] = weights[:, 2 * dy + dz]
        table[row, 2 + dy, m] = weights[:, 2 * dx + dz]
        table[row, 4 + dz, m] = weights[:, 2 * dx + dy]
    return np.concatenate(in_two(table.reshape(32, 288)), axis=0)


def spread_table():
    weights = corner_table()
    table = np.zeros((3, 3, 16, 32), np.float32)
    for dx, dy, dz, m in itertools.product(range(2), range(2), range(2), range(3)):
        column = 16 * dx + 8 * dy + CORNER * dz + m
        if dx == 0:
            table[0, m, :, column] = weights[:, 2 * dy + dz]
        if dy == 0:
            table[1, m, :, column] = weights[:, 2 * dx + dz]
        if dz == 0:
            table[2, m, :, column] = weights[:, 2 * dx + dy]
    high, low = in_two(table.reshape(144, 32))
    return np.concatenate([high, high, low], axis=1)


def kernel(
    count_x, count_y, wx, wy,
    traces_hbm, dirichlet_hbm, class_hbm, viscosity_hbm, diag_hbm, solve_hbm, flux_hbm, gather_hbm, spread_hbm,
    out,
    traces, dirichlet, classes, viscosity, diag, solve_t, flux_map, gather, spread,
    staged, product, lifted, keep, scale, visc, halo_x, halo_y, first_y, flag_x, flag_y, keep_x, keep_y,
    residual, high, base, send_x, send_y, recv_x, recv_y, visc_x, visc_y, prev_x, prev_y, last_x, last_y, corner_x, corner_y,
    edge_x, edge_y, edge_c, rim_x, rim_y, rim_c,
    load_sem, send_sem, recv_sem, ready,
):
    columns, depth = wx * wy, traces.shape[3]
    faces = traces.shape[1]
    me_x, me_y = lax.axis_index("gx"), lax.axis_index("gy")
    there = {-1: (me_x > 0, me_y > 0), 0: (None, None), 1: (me_x < count_x - 1, me_y < count_y - 1)}

    def present(dx, dy):
        a, b = there[dx][0], there[dy][1]
        if a is None:
            return b
        return a if b is None else jnp.logical_and(a, b)

    def device(dx, dy):
        return {"gx": me_x + dx, "gy": me_y + dy}

    around = [(-1, -1), (0, -1), (-1, 0), (1, -1), (1, 0), (-1, 1), (0, 1), (1, 1)]
    names = ("dirichlet", "y", "x", "z", "viscosity", "classes", "solve", "flux", "gather", "diag", "spread")
    pairs = [
        (dirichlet_hbm, dirichlet), (traces_hbm.at[1], traces.at[1]), (traces_hbm.at[0], traces.at[0]),
        (traces_hbm.at[2], traces.at[2]), (viscosity_hbm, viscosity), (class_hbm, classes), (solve_hbm, solve_t),
        (flux_hbm, flux_map), (gather_hbm, gather), (diag_hbm, diag), (spread_hbm, spread),
    ]
    loads = {name: pltpu.make_async_copy(a, b, load_sem.at[i]) for i, (name, (a, b)) in enumerate(zip(names, pairs))}
    for load in loads.values():
        load.start()

    barrier = pltpu.get_barrier_semaphore()
    total = 0
    below = [None, (0, -1), (-1, 0)]
    for dx, dy in below[1:]:
        total = total + present(dx, dy).astype(jnp.int32)

        @pl.when(present(-dx, -dy))
        def _():
            pl.semaphore_signal(barrier, inc=1, device_id=device(-dx, -dy), device_id_type=MESH)

    class Exchange:
        def __init__(self, slot, dx, dy, source, target):
            self.to, self.origin, self.target = present(dx, dy), present(-dx, -dy), target
            self.copy = pltpu.make_async_remote_copy(
                src_ref=source, dst_ref=target, send_sem=send_sem.at[slot], recv_sem=recv_sem.at[slot],
                device_id=device(dx, dy), device_id_type=MESH,
            )

        def clear(self):
            @pl.when(jnp.logical_not(self.origin))
            def _():
                self.target[...] = jnp.zeros(self.target.shape, self.target.dtype)

        def start(self):
            pl.when(self.to)(self.copy.start)

        def arrive(self):
            pl.when(self.origin)(self.copy.wait_recv)

        def drain(self):
            pl.when(self.to)(self.copy.wait_send)

    traces_x = Exchange(0, -1, 0, lifted.at[0, pl.ds(0, wy)], halo_x)
    flags_x = Exchange(1, -1, 0, flag_x, keep_x)
    traces_y = Exchange(2, 0, -1, first_y, halo_y)
    flags_y = Exchange(3, 0, -1, flag_y, keep_y)
    terms_x = Exchange(4, 1, 0, send_x, recv_x)
    terms_y = Exchange(5, 0, 1, send_y, recv_y)
    class_x = Exchange(6, 1, 0, visc_x, prev_x)
    class_y = Exchange(7, 0, 1, visc_y, prev_y)
    final_x = Exchange(8, 1, 0, last_x, corner_x)
    final_y = Exchange(9, 0, 1, last_y, corner_y)
    upward = [class_x, class_y, terms_x, terms_y]
    first = [flags_y, traces_y, flags_x, traces_x]
    rims = []
    for slot, (dx, dy) in enumerate(around):
        if dy == 0:
            source, target = edge_x.at[(dx + 1) // 2], rim_x.at[(dx + 1) // 2]
        elif dx == 0:
            source, target = edge_y.at[(dy + 1) // 2], rim_y.at[(dy + 1) // 2]
        else:
            source, target = edge_c.at[(dx + 1) // 2, (dy + 1) // 2], rim_c.at[(dx + 1) // 2, (dy + 1) // 2]
        rims.append(Exchange(10 + slot, dx, dy, source, target))

    lane = lax.broadcasted_iota(jnp.int32, (8, depth), 1)
    row = lax.broadcasted_iota(jnp.int32, (8, depth), 0)
    lane_faces = lax.broadcasted_iota(jnp.int32, (faces, depth), 1)

    def stage(d):
        for n in range(faces):
            staged[d, n * STAGE : n * STAGE + columns] = traces[d, n].astype(jnp.float32) * keep[d]

    def to_columns(d, chosen):
        for c in chosen:
            lifted[d, c] = staged[d, pl.ds(c, faces, stride=STAGE)].astype(jnp.bfloat16)

    loads["dirichlet"].wait()
    keep[...] = 1.0 - dirichlet[...].astype(jnp.float32)
    for x in range(wx):
        flag_y[x : x + 1] = keep[1, x * wy : x * wy + 1]
    flag_x[...] = keep[0, :wy]
    loads["y"].wait()
    stage(1)
    for x in range(wx):
        first_y[x] = staged[1, pl.ds(x * wy, faces, stride=STAGE)].astype(jnp.bfloat16)
    pl.when(total > 0)(lambda: pl.semaphore_wait(barrier, total))
    def tell(slot, dx, dy, if_present):
        @pl.when(if_present)
        def _():
            pl.semaphore_signal(ready.at[slot], inc=1, device_id=device(dx, dy), device_id_type=MESH)

    for slot in (1, 2):
        tell(slot, *below[slot], present(*below[slot]))
    flags_y.start()
    traces_y.start()
    flags_x.start()
    loads["x"].wait()
    stage(0)
    to_columns(0, range(wy))
    traces_x.start()

    def hear(slot, dx, dy):
        pl.when(present(dx, dy))(lambda: pl.semaphore_wait(ready.at[slot], 1))

    loads["z"].wait()
    stage(2)
    to_columns(0, range(wy, columns))
    to_columns(1, range(columns))
    to_columns(2, range(columns))
    for exchange in first + upward + [final_x, final_y] + rims:
        exchange.clear()
    for name in names[4:7]:
        loads[name].wait()
    level_sum = jnp.zeros(classes.shape, jnp.float32)
    for level in range(viscosity.shape[0]):
        level_sum = level_sum + jnp.where(classes[...] == level, viscosity[level], 0.0)
    visc[...] = level_sum
    visc_x[...] = level_sum[columns - wy :]
    for x in range(wx):
        c = x * wy + wy - 1
        visc_y[x : x + 1] = level_sum[c : c + 1]
    lanes_c = lax.broadcasted_iota(jnp.int32, (columns, depth), 1)
    for d in range(3):
        scale[2 * d] = level_sum * keep[d]
    scale[5] = level_sum * jnp.where(lanes_c == depth - 1, 0.0, pltpu.roll(keep[2], depth - 1, 1))
    scale[1, : columns - wy] = level_sum[: columns - wy] * keep[0, wy:]
    scale[3, : columns - 1] = level_sum[: columns - 1] * keep[1, 1:]
    for name in names[7:]:
        loads[name].wait()
    turned = jnp.concatenate([solve_t[f * faces : (f + 1) * faces] for f in ORDER], axis=0).T
    product[...] = jnp.dot(flux_map[...], turned, preferred_element_type=jnp.float32).astype(jnp.bfloat16)

    known = 4 * faces
    late = known // 128 * 128
    filler = jnp.zeros((known - late, depth), jnp.bfloat16)
    nothing = jnp.zeros((faces, depth), jnp.bfloat16)

    def rows_of(face_slot):
        return slice(face_slot * faces, (face_slot + 1) * faces)

    def lanes_of(index):
        return slice(index * depth, (index + 1) * depth)

    def z_above(c):
        low_z = lifted[2, c].astype(jnp.float32)
        return jnp.where(lane_faces == depth - 1, 0.0, pltpu.roll(low_z, depth - 1, 1)).astype(jnp.bfloat16)

    def low_part(c):
        return [lifted[0, c], lifted[1, c], lifted[2, c], z_above(c)]

    def high_x(c):
        return lifted[0, c + wy] if c + wy < columns else halo_x[c % wy]

    def high_y(c):
        return lifted[1, c + 1] if c % wy + 1 < wy else halo_y[c // wy]

    def side_by_side(blocks):
        return jnp.concatenate([jnp.concatenate(block, axis=0) for block in blocks], axis=1)

    def late_dot(left_rows, blocks):
        return jnp.dot(
            product[left_rows, late:],
            side_by_side([[filler, a, b] for a, b in blocks]),
            preferred_element_type=jnp.float32,
        )

    corners = {}

    def finish(chosen, flux, faces_in):
        rounded = []
        for index, c in enumerate(chosen):
            x, y = c // wy, c % wy
            parts = []
            for face_slot in range(6):
                term = flux(index, face_slot)
                trace = faces_in[index][face_slot]
                if trace is not None:
                    term = term + penalty * trace.astype(jnp.float32)
                parts.append(term * scale[face_slot, c : c + 1])
            residual[0, c] = parts[0]
            residual[1, c] = parts[2]
            residual[2, c] = parts[4] + pltpu.roll(parts[5], 1, 1)
            cut = jnp.concatenate(parts, axis=0).astype(jnp.bfloat16)
            if x + 1 < wx:
                high[0, c] = parts[1]
            elif y + 1 == wy:
                last_x[...] = cut[rows_of(1)]
            if y + 1 < wy:
                high[1, c] = parts[3]
            elif x + 1 == wx:
                last_y[...] = cut[rows_of(3)]
            rounded.append(cut)
        both = jnp.dot(gather[...], jnp.concatenate(rounded, axis=1), preferred_element_type=jnp.float32)
        sums = both[:32] + both[32:]
        for index, c in enumerate(chosen):
            x, y = c // wy, c % wy
            for dx, dy in itertools.product(range(2), range(2)):
                part = sums[16 * dx + 8 * dy : 16 * dx + 8 * dy + 8, lanes_of(index)]
                key = (x + dx, y + dy)
                corners[key] = part if key not in corners else corners[key] + part

    def process(chosen):
        slots = [low_part(c) + [high_x(c), high_y(c)] for c in chosen]
        flux = jnp.dot(product[...], side_by_side(slots), preferred_element_type=jnp.float32)
        by_slot = [[block[ORDER.index(f)] for f in range(6)] for block in slots]
        finish(chosen, lambda index, f: flux[rows_of(f), lanes_of(index)], by_slot)

    def prepare(which, chosen):
        slots = [low_part(c) for c in chosen]
        flux = jnp.dot(product[:, :known], side_by_side(slots), preferred_element_type=jnp.float32)
        for index in range(len(chosen)):
            for f in range(6):
                term = flux[rows_of(f), lanes_of(index)]
                if f in ORDER[:4]:
                    term = term + penalty * slots[index][ORDER.index(f)].astype(jnp.float32)
                base[which, rows_of(f), lanes_of(index)] = term

    def complete(which, chosen):
        pairs = [[high_x(c), high_y(c)] for c in chosen]
        flux = late_dot(slice(None), pairs)
        by_slot = [[None, a, None, b, None, None] for a, b in pairs]
        finish(
            chosen,
            lambda index, f: base[which, rows_of(f), lanes_of(index)] + flux[rows_of(f), lanes_of(index)],
            by_slot,
        )

    inner = [c for c in range(columns) if c + wy < columns and c % wy + 1 < wy]
    need_x = [c for c in range(columns) if c + wy >= columns and c % wy + 1 < wy]
    need_y = [c for c in range(columns) if c % wy + 1 == wy]
    early = len(inner) // 4 * 4
    rim_a, rim_b = need_x + inner[early:], need_y
    prepare(1, rim_b)
    prepare(0, rim_a)
    beside_y = late_dot(rows_of(3), [[high_x(c), nothing] for c in need_y[: wx - 1]])
    for x, c in enumerate(need_y[: wx - 1]):
        value = base[1, rows_of(3), lanes_of(x)] + beside_y[:, lanes_of(x)]
        send_y[x] = (value * visc[c : c + 1]).astype(jnp.bfloat16)
    beside_x = late_dot(rows_of(1), [[nothing, high_y(c)] for c in need_x])
    for y, c in enumerate(need_x):
        value = base[0, rows_of(1), lanes_of(y)] + beside_x[:, lanes_of(y)]
        send_x[y] = (value * visc[c : c + 1]).astype(jnp.bfloat16)
    for start in range(0, early, 4):
        process(inner[start : start + 4])
    hear(2, 1, 0)
    tell(3, 1, 0, present(1, -1))
    class_x.start()
    terms_x.start()
    hear(1, 0, 1)
    tell(0, -1, 0, present(-1, 1))
    class_y.start()
    terms_y.start()
    flags_x.arrive()
    traces_x.arrive()
    scale[1, columns - wy :] = visc[columns - wy :] * keep_x[...]
    complete(0, rim_a)
    vertices = list(itertools.product(range(wx + 1), range(wy + 1)))

    def settle(chosen):
        for x, y in chosen:
            value = corners[x, y]
            above = pltpu.roll(jnp.where(lane == depth - 1, 0.0, value), 1, 1)
            value = value + pltpu.roll(above, 4, 0)
            if x < wx and y < wy:
                corners[x, y] = jnp.where(row == CORNER - 1, diag[x * wy + y : x * wy + y + 1], value)
            else:
                corners[x, y] = jnp.where(row == CORNER - 1, 0.0, value)

    def pack(target, values):
        for i in range(0, len(values), 2):
            value = values[i]
            if i + 1 < len(values):
                value = jnp.where(row < CORNER, value, pltpu.roll(values[i + 1], 4, 0))
            target[i // 2] = value

    def pack_y(side):
        pack(edge_y.at[side], [corners[x, side * wy] for x in range(wx + 1)])
        for other in range(2):
            edge_c[other, side] = corners[other * wx, side * wy]

    rim = dict(zip(around, rims))
    settle([place for place in vertices if place[1] < wy - 1])
    pack_y(0)
    rim[0, -1].start()
    rim[1, -1].start()
    hear(3, -1, -1)
    rim[-1, -1].start()
    flags_y.arrive()
    traces_y.arrive()
    for x in range(wx):
        c = x * wy + wy - 1
        scale[3, c : c + 1] = visc[c : c + 1] * keep_y[x : x + 1]
    complete(1, rim_b)
    settle([place for place in vertices if place[1] >= wy - 1])
    pack_y(1)
    rim[0, 1].start()
    rim[-1, 1].start()
    for side in range(2):
        pack(edge_x.at[side], [corners[side * wx, y] for y in range(wy + 1)])
    rim[-1, 0].start()
    rim[1, 0].start()
    final_y.start()
    final_x.start()
    hear(0, 1, 1)
    rim[1, 1].start()

    for c in range(columns):
        if c >= wy:
            residual[0, c] += high[0, c - wy]
        if c % wy:
            residual[1, c] += high[1, c - 1]
    for exchange in upward:
        exchange.arrive()
    mine_x = late_dot(rows_of(1), [[lifted[0, y], nothing] for y in range(wy - 1)])
    for y in range(wy - 1):
        value = mine_x[:, lanes_of(y)] + penalty * lifted[0, y].astype(jnp.float32)
        value = value * prev_x[y : y + 1] + recv_x[y].astype(jnp.float32)
        residual[0, y] += value * keep[0, y : y + 1]
    mine_y = late_dot(rows_of(3), [[nothing, lifted[1, x * wy]] for x in range(wx - 1)])
    for x in range(wx - 1):
        c = x * wy
        value = mine_y[:, lanes_of(x)] + penalty * lifted[1, c].astype(jnp.float32)
        value = value * prev_y[x : x + 1] + recv_y[x].astype(jnp.float32)
        residual[1, c] += value * keep[1, c : c + 1]

    fixes = {}

    def correct(value, inside):
        under = jnp.broadcast_to(value[CORNER - 1 : CORNER], value.shape)
        if inside is not None:
            value = jnp.where(inside, value, 0.0)
            under = jnp.where(inside, under, 1.0)
        fix = value / under
        above = jnp.where(lane == depth - 1, 0.0, pltpu.roll(fix, depth - 1, 1))
        return jnp.where(row < CORNER, fix, pltpu.roll(above, 4, 0))

    def emit(chosen):
        stacks = []
        for c in chosen:
            x, y = c // wy, c % wy
            value = jnp.concatenate([fixes[x, y], fixes[x, y + 1], fixes[x + 1, y], fixes[x + 1, y + 1]], axis=0)
            upper = value.astype(jnp.bfloat16)
            lower = (value - upper.astype(jnp.float32)).astype(jnp.bfloat16)
            stacks.append(jnp.concatenate([upper, lower, upper], axis=0))
        lift = jnp.dot(spread[...], jnp.concatenate(stacks, axis=1), preferred_element_type=jnp.float32)
        for index, c in enumerate(chosen):
            x, y = c // wy, c % wy
            for d in range(3):
                value = residual[d, c]
                if d == 0 and x == 0 and y + 1 == wy:
                    value = value + corner_x[...].astype(jnp.float32)
                if d == 1 and y == 0 and x + 1 == wx:
                    value = value + corner_y[...].astype(jnp.float32)
                piece = lift[d * faces : (d + 1) * faces, lanes_of(index)]
                out[d, c * PITCH : c * PITCH + faces] = value + keep[d, c : c + 1] * piece

    for x, y in vertices:
        if 0 < x < wx and 0 < y < wy:
            fixes[x, y] = correct(corners[x, y], None)
    middle = [c for c in range(columns) if 0 < c // wy < wx - 1 and 0 < c % wy < wy - 1]
    outer = [c for c in range(columns) if c not in middle]
    emit(middle)
    for exchange in first + upward + rims + [final_x, final_y]:
        exchange.drain()

    for exchange in rims:
        exchange.arrive()

    def unpack(source, index):
        value = source[index // 2]
        return pltpu.roll(value, 4, 0) if index % 2 else value

    for x, y in vertices:
        if (x, y) in fixes:
            continue
        value = corners[x, y]
        side_x = {0: 0, wx: 1}.get(x)
        side_y = {0: 0, wy: 1}.get(y)
        if side_x is not None:
            value = value + unpack(rim_x.at[1 - side_x], y)
        if side_y is not None:
            value = value + unpack(rim_y.at[1 - side_y], x)
        if side_x is not None and side_y is not None:
            value = value + rim_c[1 - side_x, 1 - side_y]
        fixes[x, y] = correct(value, present(int(x == wx), int(y == wy)))
    final_x.arrive()
    final_y.arrive()
    for start in range(0, len(outer), 4):
        emit(outer[start : start + 4])


def deliver(faces, columns, values, out_hbm, rounded, store_sem):
    stores = []
    for d in range(3):
        for n in range(faces):
            rounded[d, n] = values[d, pl.ds(n, columns, stride=PITCH)].astype(jnp.bfloat16)
        stores.append(pltpu.make_async_copy(rounded.at[d], out_hbm.at[d], store_sem.at[d]))
        stores[-1].start()
    for store in stores:
        store.wait()


def local(count_x, count_y, traces, dirichlet, visc_class, viscosity, coarse_diag, solve_map, flux_map):
    faces, wx, wy, depth = traces.shape[1:]
    columns = wx * wy
    operands = (
        traces.reshape(3, faces, columns, depth),
        dirichlet.reshape(3, columns, depth),
        visc_class.reshape(columns, depth),
        viscosity,
        coarse_diag.reshape(columns, depth),
        solve_map.T,
        flux_map,
        jnp.asarray(gather_table()),
        jnp.asarray(spread_table()),
    )
    anywhere = pl.BlockSpec(memory_space=pl.ANY)
    exchanges = 18
    rims_x, rims_y = wy // 2 + 1, wx // 2 + 1
    f32, bf16 = jnp.float32, jnp.bfloat16
    scratch = [
        pltpu.SMEM(a.shape, a.dtype) if index == 3 else pltpu.VMEM(a.shape, a.dtype) for index, a in enumerate(operands)
    ] + [
        pltpu.VMEM((3, (faces + 1) * STAGE, depth), f32),
        pltpu.VMEM((6 * faces, 6 * faces), bf16),
        pltpu.VMEM((3, columns, faces, depth), bf16),
        pltpu.VMEM((3, columns, depth), f32),
        pltpu.VMEM((6, columns, depth), f32),
        pltpu.VMEM((columns, depth), f32),
        pltpu.VMEM((wy, faces, depth), bf16),
        pltpu.VMEM((wx, faces, depth), bf16),
        pltpu.VMEM((wx, faces, depth), bf16),
        pltpu.VMEM((wy, depth), f32),
        pltpu.VMEM((wx, depth), f32),
        pltpu.VMEM((wy, depth), f32),
        pltpu.VMEM((wx, depth), f32),
        pltpu.VMEM((3, columns, faces, depth), f32),
        pltpu.VMEM((2, columns, faces, depth), f32),
        pltpu.VMEM((2, 6 * faces, 4 * depth), f32),
        pltpu.VMEM((wy - 1, faces, depth), bf16),
        pltpu.VMEM((wx - 1, faces, depth), bf16),
        pltpu.VMEM((wy - 1, faces, depth), bf16),
        pltpu.VMEM((wx - 1, faces, depth), bf16),
        pltpu.VMEM((wy, depth), f32),
        pltpu.VMEM((wx, depth), f32),
        pltpu.VMEM((wy, depth), f32),
        pltpu.VMEM((wx, depth), f32),
        pltpu.VMEM((faces, depth), bf16),
        pltpu.VMEM((faces, depth), bf16),
        pltpu.VMEM((faces, depth), bf16),
        pltpu.VMEM((faces, depth), bf16),
        pltpu.VMEM((2, rims_x, 8, depth), f32),
        pltpu.VMEM((2, rims_y, 8, depth), f32),
        pltpu.VMEM((2, 2, 8, depth), f32),
        pltpu.VMEM((2, rims_x, 8, depth), f32),
        pltpu.VMEM((2, rims_y, 8, depth), f32),
        pltpu.VMEM((2, 2, 8, depth), f32),
        pltpu.SemaphoreType.DMA((len(operands) + 2,)),
        pltpu.SemaphoreType.DMA((exchanges,)),
        pltpu.SemaphoreType.DMA((exchanges,)),
        pltpu.SemaphoreType.REGULAR((4,)),
    ]
    result = pl.pallas_call(
        functools.partial(kernel, count_x, count_y, wx, wy),
        out_shape=pltpu.VMEM((3, (columns + 1) * PITCH, depth), f32),
        in_specs=[anywhere] * len(operands),
        out_specs=pl.BlockSpec(memory_space=pltpu.VMEM),
        scratch_shapes=scratch,
        compiler_params=pltpu.CompilerParams(collective_id=0, has_side_effects=True),
        name="apply",
    )(*operands)
    result = pl.pallas_call(
        functools.partial(deliver, faces, columns),
        out_shape=jax.ShapeDtypeStruct((3, faces, columns, depth), bf16),
        in_specs=[pl.BlockSpec(memory_space=pltpu.VMEM)],
        out_specs=anywhere,
        scratch_shapes=[pltpu.VMEM((3, faces, columns, depth), bf16), pltpu.SemaphoreType.DMA((3,))],
        compiler_params=pltpu.CompilerParams(vmem_limit_bytes=16 * 2**20),
        name="deliver",
    )(result)
    return result.reshape(3, faces, wx, wy, depth)


def solution(mesh):
    count_x, count_y = mesh.shape["gx"], mesh.shape["gy"]
    in_specs = (
        P(None, None, "gx", "gy", None),
        P(None, "gx", "gy", None),
        P("gx", "gy", None),
        P(),
        P("gx", "gy", None),
        P(),
        P(),
    )
    out_specs = P(None, None, "gx", "gy", None)
    return jax.shard_map(
        functools.partial(local, count_x, count_y), mesh=mesh, in_specs=in_specs, out_specs=out_specs, check_vma=False
    )
```

```python
import functools
import itertools
import math

import jax
import jax.numpy as jnp
import ml_dtypes
import numpy as np
from jax import lax
from jax.experimental import pallas as pl
from jax.experimental.pallas import tpu as pltpu
from jax.sharding import PartitionSpec as P

MESH = pl.DeviceIdType.MESH
penalty = 0.5
ORDER = (0, 2, 4, 5, 1, 3)
PITCH = 52
STAGE = 20
CORNER = 4


def corner_table():
    points = [-1.0, -math.sqrt(0.2), math.sqrt(0.2), 1.0]
    table = np.zeros((16, 4), np.float64)
    for a, b, p, q in itertools.product(range(4), range(4), range(2), range(2)):
        table[4 * a + b, 2 * p + q] = (1 + (2 * p - 1) * points[a]) * (1 + (2 * q - 1) * points[b]) / 4
    return table.astype(np.float32)


def in_two(table):
    high = table.astype(ml_dtypes.bfloat16)
    low = (table - high.astype(np.float32)).astype(ml_dtypes.bfloat16)
    return high, low


def gather_table():
    weights = corner_table()
    table = np.zeros((32, 6, 3, 16), np.float32)
    for dx, dy, dz, m in itertools.product(range(2), range(2), range(2), range(3)):
        row = 16 * dx + 8 * dy + CORNER * dz + m
        table[row, dx, m] = weights[:, 2 * dy + dz]
        table[row, 2 + dy, m] = weights[:, 2 * dx + dz]
        table[row, 4 + dz, m] = weights[:, 2 * dx + dy]
    return np.concatenate(in_two(table.reshape(32, 288)), axis=0)


def spread_table():
    weights = corner_table()
    table = np.zeros((3, 3, 16, 32), np.float32)
    for dx, dy, dz, m in itertools.product(range(2), range(2), range(2), range(3)):
        column = 16 * dx + 8 * dy + CORNER * dz + m
        if dx == 0:
            table[0, m, :, column] = weights[:, 2 * dy + dz]
        if dy == 0:
            table[1, m, :, column] = weights[:, 2 * dx + dz]
        if dz == 0:
            table[2, m, :, column] = weights[:, 2 * dx + dy]
    high, low = in_two(table.reshape(144, 32))
    return np.concatenate([high, high, low], axis=1)


def kernel(
    count_x, count_y, wx, wy,
    traces_hbm, dirichlet_hbm, class_hbm, viscosity_hbm, diag_hbm, solve_hbm, flux_hbm, gather_hbm, spread_hbm,
    out,
    traces, dirichlet, classes, viscosity, diag, solve_t, flux_map, gather, spread,
    staged, product, lifted, keep, scale, visc, halo_x, halo_y, first_y, flag_x, flag_y, keep_x, keep_y,
    residual, high, base, send_x, send_y, recv_x, recv_y, visc_x, visc_y, prev_x, prev_y, last_x, last_y, corner_x, corner_y,
    edge_x, edge_y, edge_c, rim_x, rim_y, rim_c,
    load_sem, send_sem, recv_sem, ready,
):
    columns, depth = wx * wy, traces.shape[3]
    faces = traces.shape[1]
    me_x, me_y = lax.axis_index("gx"), lax.axis_index("gy")
    there = {-1: (me_x > 0, me_y > 0), 0: (None, None), 1: (me_x < count_x - 1, me_y < count_y - 1)}

    def present(dx, dy):
        a, b = there[dx][0], there[dy][1]
        if a is None:
            return b
        return a if b is None else jnp.logical_and(a, b)

    def device(dx, dy):
        return {"gx": me_x + dx, "gy": me_y + dy}

    around = [(-1, -1), (0, -1), (-1, 0), (1, -1), (1, 0), (-1, 1), (0, 1), (1, 1)]
    names = ("dirichlet", "y", "x", "z", "viscosity", "classes", "solve", "flux", "gather", "diag", "spread")
    pairs = [
        (dirichlet_hbm, dirichlet), (traces_hbm.at[1], traces.at[1]), (traces_hbm.at[0], traces.at[0]),
        (traces_hbm.at[2], traces.at[2]), (viscosity_hbm, viscosity), (class_hbm, classes), (solve_hbm, solve_t),
        (flux_hbm, flux_map), (gather_hbm, gather), (diag_hbm, diag), (spread_hbm, spread),
    ]
    loads = {name: pltpu.make_async_copy(a, b, load_sem.at[i]) for i, (name, (a, b)) in enumerate(zip(names, pairs))}
    for load in loads.values():
        load.start()

    barrier = pltpu.get_barrier_semaphore()
    total = 0
    below = [None, (0, -1), (-1, 0)]
    for dx, dy in below[1:]:
        total = total + present(dx, dy).astype(jnp.int32)

        @pl.when(present(-dx, -dy))
        def _():
            pl.semaphore_signal(barrier, inc=1, device_id=device(-dx, -dy), device_id_type=MESH)

    class Exchange:
        def __init__(self, slot, dx, dy, source, target):
            self.to, self.origin, self.target = present(dx, dy), present(-dx, -dy), target
            self.copy = pltpu.make_async_remote_copy(
                src_ref=source, dst_ref=target, send_sem=send_sem.at[slot], recv_sem=recv_sem.at[slot],
                device_id=device(dx, dy), device_id_type=MESH,
            )

        def clear(self):
            @pl.when(jnp.logical_not(self.origin))
            def _():
                self.target[...] = jnp.zeros(self.target.shape, self.target.dtype)

        def start(self):
            pl.when(self.to)(self.copy.start)

        def arrive(self):
            pl.when(self.origin)(self.copy.wait_recv)

        def drain(self):
            pl.when(self.to)(self.copy.wait_send)

    traces_x = Exchange(0, -1, 0, lifted.at[0, pl.ds(0, wy)], halo_x)
    flags_x = Exchange(1, -1, 0, flag_x, keep_x)
    traces_y = Exchange(2, 0, -1, first_y, halo_y)
    flags_y = Exchange(3, 0, -1, flag_y, keep_y)
    terms_x = Exchange(4, 1, 0, send_x, recv_x)
    terms_y = Exchange(5, 0, 1, send_y, recv_y)
    class_x = Exchange(6, 1, 0, visc_x, prev_x)
    class_y = Exchange(7, 0, 1, visc_y, prev_y)
    final_x = Exchange(8, 1, 0, last_x, corner_x)
    final_y = Exchange(9, 0, 1, last_y, corner_y)
    upward = [class_x, class_y, terms_x, terms_y]
    first = [flags_y, traces_y, flags_x, traces_x]
    rims = []
    for slot, (dx, dy) in enumerate(around):
        if dy == 0:
            source, target = edge_x.at[(dx + 1) // 2], rim_x.at[(dx + 1) // 2]
        elif dx == 0:
            source, target = edge_y.at[(dy + 1) // 2], rim_y.at[(dy + 1) // 2]
        else:
            source, target = edge_c.at[(dx + 1) // 2, (dy + 1) // 2], rim_c.at[(dx + 1) // 2, (dy + 1) // 2]
        rims.append(Exchange(10 + slot, dx, dy, source, target))

    lane = lax.broadcasted_iota(jnp.int32, (8, depth), 1)
    row = lax.broadcasted_iota(jnp.int32, (8, depth), 0)
    lane_faces = lax.broadcasted_iota(jnp.int32, (faces, depth), 1)

    def stage(d):
        for n in range(faces):
            staged[d, n * STAGE : n * STAGE + columns] = traces[d, n].astype(jnp.float32) * keep[d]

    def to_columns(d, chosen):
        for c in chosen:
            lifted[d, c] = staged[d, pl.ds(c, faces, stride=STAGE)].astype(jnp.bfloat16)

    loads["dirichlet"].wait()
    keep[...] = 1.0 - dirichlet[...].astype(jnp.float32)
    for x in range(wx):
        flag_y[x : x + 1] = keep[1, x * wy : x * wy + 1]
    flag_x[...] = keep[0, :wy]
    loads["y"].wait()
    stage(1)
    for x in range(wx):
        first_y[x] = staged[1, pl.ds(x * wy, faces, stride=STAGE)].astype(jnp.bfloat16)
    pl.when(total > 0)(lambda: pl.semaphore_wait(barrier, total))
    def tell(slot, dx, dy, if_present):
        @pl.when(if_present)
        def _():
            pl.semaphore_signal(ready.at[slot], inc=1, device_id=device(dx, dy), device_id_type=MESH)

    for slot in (1, 2):
        tell(slot, *below[slot], present(*below[slot]))
    flags_y.start()
    traces_y.start()
    flags_x.start()
    loads["x"].wait()
    stage(0)
    to_columns(0, range(wy))
    traces_x.start()

    def hear(slot, dx, dy):
        pl.when(present(dx, dy))(lambda: pl.semaphore_wait(ready.at[slot], 1))

    loads["z"].wait()
    stage(2)
    to_columns(0, range(wy, columns))
    to_columns(1, range(columns))
    to_columns(2, range(columns))
    for exchange in first + upward + [final_x, final_y] + rims:
        exchange.clear()
    for name in names[4:7]:
        loads[name].wait()
    level_sum = jnp.zeros(classes.shape, jnp.float32)
    for level in range(viscosity.shape[0]):
        level_sum = level_sum + jnp.where(classes[...] == level, viscosity[level], 0.0)
    visc[...] = level_sum
    visc_x[...] = level_sum[columns - wy :]
    for x in range(wx):
        c = x * wy + wy - 1
        visc_y[x : x + 1] = level_sum[c : c + 1]
    lanes_c = lax.broadcasted_iota(jnp.int32, (columns, depth), 1)
    for d in range(3):
        scale[2 * d] = level_sum * keep[d]
    scale[5] = level_sum * jnp.where(lanes_c == depth - 1, 0.0, pltpu.roll(keep[2], depth - 1, 1))
    scale[1, : columns - wy] = level_sum[: columns - wy] * keep[0, wy:]
    scale[3, : columns - 1] = level_sum[: columns - 1] * keep[1, 1:]
    for name in names[7:]:
        loads[name].wait()
    turned = jnp.concatenate([solve_t[f * faces : (f + 1) * faces] for f in ORDER], axis=0).T
    product[...] = jnp.dot(flux_map[...], turned, preferred_element_type=jnp.float32).astype(jnp.bfloat16)

    known = 4 * faces
    late = known // 128 * 128
    filler = jnp.zeros((known - late, depth), jnp.bfloat16)
    nothing = jnp.zeros((faces, depth), jnp.bfloat16)

    def rows_of(face_slot):
        return slice(face_slot * faces, (face_slot + 1) * faces)

    def lanes_of(index):
        return slice(index * depth, (index + 1) * depth)

    def z_above(c):
        low_z = lifted[2, c].astype(jnp.float32)
        return jnp.where(lane_faces == depth - 1, 0.0, pltpu.roll(low_z, depth - 1, 1)).astype(jnp.bfloat16)

    def low_part(c):
        return [lifted[0, c], lifted[1, c], lifted[2, c], z_above(c)]

    def high_x(c):
        return lifted[0, c + wy] if c + wy < columns else halo_x[c % wy]

    def high_y(c):
        return lifted[1, c + 1] if c % wy + 1 < wy else halo_y[c // wy]

    def side_by_side(blocks):
        return jnp.concatenate([jnp.concatenate(block, axis=0) for block in blocks], axis=1)

    def late_dot(left_rows, blocks):
        return jnp.dot(
            product[left_rows, late:],
            side_by_side([[filler, a, b] for a, b in blocks]),
            preferred_element_type=jnp.float32,
        )

    corners = {}

    def finish(chosen, flux, faces_in):
        rounded = []
        for index, c in enumerate(chosen):
            x, y = c // wy, c % wy
            parts = []
            for face_slot in range(6):
                term = flux(index, face_slot)
                trace = faces_in[index][face_slot]
                if trace is not None:
                    term = term + penalty * trace.astype(jnp.float32)
                parts.append(term * scale[face_slot, c : c + 1])
            residual[0, c] = parts[0]
            residual[1, c] = parts[2]
            residual[2, c] = parts[4] + pltpu.roll(parts[5], 1, 1)
            cut = jnp.concatenate(parts, axis=0).astype(jnp.bfloat16)
            if x + 1 < wx:
                high[0, c] = parts[1]
            elif y + 1 == wy:
                last_x[...] = cut[rows_of(1)]
            if y + 1 < wy:
                high[1, c] = parts[3]
            elif x + 1 == wx:
                last_y[...] = cut[rows_of(3)]
            rounded.append(cut)
        both = jnp.dot(gather[...], jnp.concatenate(rounded, axis=1), preferred_element_type=jnp.float32)
        sums = both[:32] + both[32:]
        for index, c in enumerate(chosen):
            x, y = c // wy, c % wy
            for dx, dy in itertools.product(range(2), range(2)):
                part = sums[16 * dx + 8 * dy : 16 * dx + 8 * dy + 8, lanes_of(index)]
                key = (x + dx, y + dy)
                corners[key] = part if key not in corners else corners[key] + part

    def process(chosen):
        slots = [low_part(c) + [high_x(c), high_y(c)] for c in chosen]
        flux = jnp.dot(product[...], side_by_side(slots), preferred_element_type=jnp.float32)
        by_slot = [[block[ORDER.index(f)] for f in range(6)] for block in slots]
        finish(chosen, lambda index, f: flux[rows_of(f), lanes_of(index)], by_slot)

    def prepare(which, chosen):
        slots = [low_part(c) for c in chosen]
        flux = jnp.dot(product[:, :known], side_by_side(slots), preferred_element_type=jnp.float32)
        for index in range(len(chosen)):
            for f in range(6):
                term = flux[rows_of(f), lanes_of(index)]
                if f in ORDER[:4]:
                    term = term + penalty * slots[index][ORDER.index(f)].astype(jnp.float32)
                base[which, rows_of(f), lanes_of(index)] = term

    def complete(which, chosen):
        pairs = [[high_x(c), high_y(c)] for c in chosen]
        flux = late_dot(slice(None), pairs)
        by_slot = [[None, a, None, b, None, None] for a, b in pairs]
        finish(
            chosen,
            lambda index, f: base[which, rows_of(f), lanes_of(index)] + flux[rows_of(f), lanes_of(index)],
            by_slot,
        )

    inner = [c for c in range(columns) if c + wy < columns and c % wy + 1 < wy]
    need_x = [c for c in range(columns) if c + wy >= columns and c % wy + 1 < wy]
    need_y = [c for c in range(columns) if c % wy + 1 == wy]
    early = len(inner) // 4 * 4
    rim_a, rim_b = need_x + inner[early:], need_y
    prepare(1, rim_b)
    prepare(0, rim_a)
    beside_y = late_dot(rows_of(3), [[high_x(c), nothing] for c in need_y[: wx - 1]])
    for x, c in enumerate(need_y[: wx - 1]):
        value = base[1, rows_of(3), lanes_of(x)] + beside_y[:, lanes_of(x)]
        send_y[x] = (value * visc[c : c + 1]).astype(jnp.bfloat16)
    beside_x = late_dot(rows_of(1), [[nothing, high_y(c)] for c in need_x])
    for y, c in enumerate(need_x):
        value = base[0, rows_of(1), lanes_of(y)] + beside_x[:, lanes_of(y)]
        send_x[y] = (value * visc[c : c + 1]).astype(jnp.bfloat16)
    for start in range(0, early, 4):
        process(inner[start : start + 4])
    hear(2, 1, 0)
    tell(3, 1, 0, present(1, -1))
    class_x.start()
    terms_x.start()
    hear(1, 0, 1)
    tell(0, -1, 0, present(-1, 1))
    class_y.start()
    terms_y.start()
    flags_x.arrive()
    traces_x.arrive()
    scale[1, columns - wy :] = visc[columns - wy :] * keep_x[...]
    complete(0, rim_a)
    vertices = list(itertools.product(range(wx + 1), range(wy + 1)))

    def settle(chosen):
        for x, y in chosen:
            value = corners[x, y]
            above = pltpu.roll(jnp.where(lane == depth - 1, 0.0, value), 1, 1)
            value = value + pltpu.roll(above, 4, 0)
            if x < wx and y < wy:
                corners[x, y] = jnp.where(row == CORNER - 1, diag[x * wy + y : x * wy + y + 1], value)
            else:
                corners[x, y] = jnp.where(row == CORNER - 1, 0.0, value)

    def pack(target, values):
        for i in range(0, len(values), 2):
            value = values[i]
            if i + 1 < len(values):
                value = jnp.where(row < CORNER, value, pltpu.roll(values[i + 1], 4, 0))
            target[i // 2] = value

    def pack_y(side):
        pack(edge_y.at[side], [corners[x, side * wy] for x in range(wx + 1)])
        for other in range(2):
            edge_c[other, side] = corners[other * wx, side * wy]

    rim = dict(zip(around, rims))
    settle([place for place in vertices if place[1] < wy - 1])
    pack_y(0)
    rim[0, -1].start()
    rim[1, -1].start()
    hear(3, -1, -1)
    rim[-1, -1].start()
    flags_y.arrive()
    traces_y.arrive()
    for x in range(wx):
        c = x * wy + wy - 1
        scale[3, c : c + 1] = visc[c : c + 1] * keep_y[x : x + 1]
    complete(1, rim_b)
    settle([place for place in vertices if place[1] >= wy - 1])
    pack_y(1)
    rim[-1, 1].start()
    hear(0, 1, 1)
    rim[1, 1].start()
    rim[0, 1].start()
    for side in range(2):
        pack(edge_x.at[side], [corners[side * wx, y] for y in range(wy + 1)])
    rim[-1, 0].start()
    rim[1, 0].start()
    final_y.start()
    final_x.start()

    for c in range(columns):
        if c >= wy:
            residual[0, c] += high[0, c - wy]
        if c % wy:
            residual[1, c] += high[1, c - 1]
    for exchange in upward:
        exchange.arrive()
    mine_x = late_dot(rows_of(1), [[lifted[0, y], nothing] for y in range(wy - 1)])
    for y in range(wy - 1):
        value = mine_x[:, lanes_of(y)] + penalty * lifted[0, y].astype(jnp.float32)
        value = value * prev_x[y : y + 1] + recv_x[y].astype(jnp.float32)
        residual[0, y] += value * keep[0, y : y + 1]
    mine_y = late_dot(rows_of(3), [[nothing, lifted[1, x * wy]] for x in range(wx - 1)])
    for x in range(wx - 1):
        c = x * wy
        value = mine_y[:, lanes_of(x)] + penalty * lifted[1, c].astype(jnp.float32)
        value = value * prev_y[x : x + 1] + recv_y[x].astype(jnp.float32)
        residual[1, c] += value * keep[1, c : c + 1]

    fixes = {}

    def correct(value, inside):
        under = jnp.broadcast_to(value[CORNER - 1 : CORNER], value.shape)
        if inside is not None:
            value = jnp.where(inside, value, 0.0)
            under = jnp.where(inside, under, 1.0)
        fix = value / under
        above = jnp.where(lane == depth - 1, 0.0, pltpu.roll(fix, depth - 1, 1))
        return jnp.where(row < CORNER, fix, pltpu.roll(above, 4, 0))

    def emit(chosen):
        stacks = []
        for c in chosen:
            x, y = c // wy, c % wy
            value = jnp.concatenate([fixes[x, y], fixes[x, y + 1], fixes[x + 1, y], fixes[x + 1, y + 1]], axis=0)
            upper = value.astype(jnp.bfloat16)
            lower = (value - upper.astype(jnp.float32)).astype(jnp.bfloat16)
            stacks.append(jnp.concatenate([upper, lower, upper], axis=0))
        lift = jnp.dot(spread[...], jnp.concatenate(stacks, axis=1), preferred_element_type=jnp.float32)
        for index, c in enumerate(chosen):
            x, y = c // wy, c % wy
            for d in range(3):
                value = residual[d, c]
                if d == 0 and x == 0 and y + 1 == wy:
                    value = value + corner_x[...].astype(jnp.float32)
                if d == 1 and y == 0 and x + 1 == wx:
                    value = value + corner_y[...].astype(jnp.float32)
                piece = lift[d * faces : (d + 1) * faces, lanes_of(index)]
                out[d, c * PITCH : c * PITCH + faces] = value + keep[d, c : c + 1] * piece

    for x, y in vertices:
        if 0 < x < wx and 0 < y < wy:
            fixes[x, y] = correct(corners[x, y], None)
    middle = [c for c in range(columns) if 0 < c // wy < wx - 1 and 0 < c % wy < wy - 1]
    outer = [c for c in range(columns) if c not in middle]
    emit(middle)
    for exchange in first + upward + rims + [final_x, final_y]:
        exchange.drain()

    for exchange in rims:
        exchange.arrive()

    def unpack(source, index):
        value = source[index // 2]
        return pltpu.roll(value, 4, 0) if index % 2 else value

    for x, y in vertices:
        if (x, y) in fixes:
            continue
        value = corners[x, y]
        side_x = {0: 0, wx: 1}.get(x)
        side_y = {0: 0, wy: 1}.get(y)
        if side_x is not None:
            value = value + unpack(rim_x.at[1 - side_x], y)
        if side_y is not None:
            value = value + unpack(rim_y.at[1 - side_y], x)
        if side_x is not None and side_y is not None:
            value = value + rim_c[1 - side_x, 1 - side_y]
        fixes[x, y] = correct(value, present(int(x == wx), int(y == wy)))
    outer.sort(key=lambda c: c in (wy - 1, (wx - 1) * wy))
    for start in range(0, len(outer), 4):
        if start + 4 >= len(outer):
            final_x.arrive()
            final_y.arrive()
        emit(outer[start : start + 4])


def deliver(faces, columns, values, out_hbm, rounded, store_sem):
    stores = []
    for d in range(3):
        for n in range(faces):
            rounded[d, n] = values[d, pl.ds(n, columns, stride=PITCH)].astype(jnp.bfloat16)
        stores.append(pltpu.make_async_copy(rounded.at[d], out_hbm.at[d], store_sem.at[d]))
        stores[-1].start()
    for store in stores:
        store.wait()


def local(count_x, count_y, traces, dirichlet, visc_class, viscosity, coarse_diag, solve_map, flux_map):
    faces, wx, wy, depth = traces.shape[1:]
    columns = wx * wy
    operands = (
        traces.reshape(3, faces, columns, depth),
        dirichlet.reshape(3, columns, depth),
        visc_class.reshape(columns, depth),
        viscosity,
        coarse_diag.reshape(columns, depth),
        solve_map.T,
        flux_map,
        jnp.asarray(gather_table()),
        jnp.asarray(spread_table()),
    )
    anywhere = pl.BlockSpec(memory_space=pl.ANY)
    exchanges = 18
    rims_x, rims_y = wy // 2 + 1, wx // 2 + 1
    f32, bf16 = jnp.float32, jnp.bfloat16
    scratch = [
        pltpu.SMEM(a.shape, a.dtype) if index == 3 else pltpu.VMEM(a.shape, a.dtype) for index, a in enumerate(operands)
    ] + [
        pltpu.VMEM((3, (faces + 1) * STAGE, depth), f32),
        pltpu.VMEM((6 * faces, 6 * faces), bf16),
        pltpu.VMEM((3, columns, faces, depth), bf16),
        pltpu.VMEM((3, columns, depth), f32),
        pltpu.VMEM((6, columns, depth), f32),
        pltpu.VMEM((columns, depth), f32),
        pltpu.VMEM((wy, faces, depth), bf16),
        pltpu.VMEM((wx, faces, depth), bf16),
        pltpu.VMEM((wx, faces, depth), bf16),
        pltpu.VMEM((wy, depth), f32),
        pltpu.VMEM((wx, depth), f32),
        pltpu.VMEM((wy, depth), f32),
        pltpu.VMEM((wx, depth), f32),
        pltpu.VMEM((3, columns, faces, depth), f32),
        pltpu.VMEM((2, columns, faces, depth), f32),
        pltpu.VMEM((2, 6 * faces, 4 * depth), f32),
        pltpu.VMEM((wy - 1, faces, depth), bf16),
        pltpu.VMEM((wx - 1, faces, depth), bf16),
        pltpu.VMEM((wy - 1, faces, depth), bf16),
        pltpu.VMEM((wx - 1, faces, depth), bf16),
        pltpu.VMEM((wy, depth), f32),
        pltpu.VMEM((wx, depth), f32),
        pltpu.VMEM((wy, depth), f32),
        pltpu.VMEM((wx, depth), f32),
        pltpu.VMEM((faces, depth), bf16),
        pltpu.VMEM((faces, depth), bf16),
        pltpu.VMEM((faces, depth), bf16),
        pltpu.VMEM((faces, depth), bf16),
        pltpu.VMEM((2, rims_x, 8, depth), f32),
        pltpu.VMEM((2, rims_y, 8, depth), f32),
        pltpu.VMEM((2, 2, 8, depth), f32),
        pltpu.VMEM((2, rims_x, 8, depth), f32),
        pltpu.VMEM((2, rims_y, 8, depth), f32),
        pltpu.VMEM((2, 2, 8, depth), f32),
        pltpu.SemaphoreType.DMA((len(operands) + 2,)),
        pltpu.SemaphoreType.DMA((exchanges,)),
        pltpu.SemaphoreType.DMA((exchanges,)),
        pltpu.SemaphoreType.REGULAR((4,)),
    ]
    result = pl.pallas_call(
        functools.partial(kernel, count_x, count_y, wx, wy),
        out_shape=pltpu.VMEM((3, (columns + 1) * PITCH, depth), f32),
        in_specs=[anywhere] * len(operands),
        out_specs=pl.BlockSpec(memory_space=pltpu.VMEM),
        scratch_shapes=scratch,
        compiler_params=pltpu.CompilerParams(collective_id=0, has_side_effects=True),
        name="apply",
    )(*operands)
    result = pl.pallas_call(
        functools.partial(deliver, faces, columns),
        out_shape=jax.ShapeDtypeStruct((3, faces, columns, depth), bf16),
        in_specs=[pl.BlockSpec(memory_space=pltpu.VMEM)],
        out_specs=anywhere,
        scratch_shapes=[pltpu.VMEM((3, faces, columns, depth), bf16), pltpu.SemaphoreType.DMA((3,))],
        compiler_params=pltpu.CompilerParams(vmem_limit_bytes=16 * 2**20),
        name="deliver",
    )(result)
    return result.reshape(3, faces, wx, wy, depth)


def solution(mesh):
    count_x, count_y = mesh.shape["gx"], mesh.shape["gy"]
    in_specs = (
        P(None, None, "gx", "gy", None),
        P(None, "gx", "gy", None),
        P("gx", "gy", None),
        P(),
        P("gx", "gy", None),
        P(),
        P(),
    )
    out_specs = P(None, None, "gx", "gy", None)
    return jax.shard_map(
        functools.partial(local, count_x, count_y), mesh=mesh, in_specs=in_specs, out_specs=out_specs, check_vma=False
    )
```
